32 devices in a mesh: ctx: 8 (over y, x, core), mp: 4 (over z).
Axes of the slice: x: 2, y: 2, z: 4, core: 2. Of those that a mesh axis runs over, the one named last changes fastest.
Arguments:
- tokens: bfloat16 [1, 4096, 4096], P(None, 'ctx', 'mp'), may hold values from -40 to 40
- w_branch: bfloat16 [4096, 2048], P(None, 'mp'), may hold values from -0.09375 to 0.09375
- w_input: bfloat16 [4096, 2048], P(None, 'mp'), may hold values from -0.09375 to 0.09375
- conv_kernel: float32 [4, 2048], P(None, 'mp'), may hold values from -3 to 3
- w_rate: bfloat16 [8, 256, 256], P('mp'), may hold values from -0.375 to 0.375
- w_admit: bfloat16 [8, 256, 256], P('mp'), may hold values from -0.375 to 0.375
- lam: float32 [2048], P('mp'), may hold values from 3 to 16
- w_out: bfloat16 [2048, 4096], P('mp'), may hold values from -0.375 to 0.375
- w_query: bfloat16 [4096, 2048], P(None, 'mp'), may hold values from -0.0625 to 0.0625
- w_key: bfloat16 [4096, 256], P(None, 'mp'), may hold values from -4.0625 to 4.0625
- w_value: bfloat16 [4096, 256], P(None, 'mp'), may hold values from -0.09375 to 0.09375
- w_attn_out: bfloat16 [2048, 4096], P('mp'), may hold values from -0.25 to 0.25
Outputs:
- layer_output: bfloat16 [1, 4096, 4096], P(None, 'ctx', 'mp')
The draws below stay inside these ranges and needn't reach their ends.
All inputs are finite; a program needn't handle non-finite values.
Results may differ from the reference program's by a relative error of at most 0.0065.
Values may be sent and summed in bfloat16 or wider, within the bound.
A program may use at most 128 MiB of HBM per device.

```python
import math
import jax
import jax.numpy as jnp
from jax import lax

D = 4096
LRU = 2048
BW = 256
NB = 8
HEADS = 8
HD = 256
CONV = 4
S_DEV = 512
WINDOW = 2048
B = 1
SEQ = 4096


def draw_tokens(key, part):
    base = jax.random.normal(jax.random.fold_in(key, 1), (B, SEQ, D), jnp.float32)
    base = jnp.clip(base, -4.0, 4.0)
    low = math.log(0.3)
    high = math.log(3.0)
    row_scale = jnp.exp(jax.random.uniform(jax.random.fold_in(key, 2), (B, SEQ, 1), jnp.float32, low, high))
    col_scale = jnp.exp(jax.random.uniform(jax.random.fold_in(key, 3), (1, 1, D), jnp.float32, low, high))
    return (base * row_scale * col_scale).astype(jnp.bfloat16)


def draw_lam(key, part):
    share = 0.5
    pick = jax.random.uniform(jax.random.fold_in(key, 21), (LRU,), jnp.float32)
    quick = 1.0 / jax.random.uniform(jax.random.fold_in(key, 22), (LRU,), jnp.float32, 30.0, 50.0)
    slow = jnp.exp(jax.random.uniform(jax.random.fold_in(key, 23), (LRU,), jnp.float32, math.log(0.2), math.log(2.0))) / SEQ
    rate = jnp.where(pick < share, quick, slow)
    return -jnp.log(jnp.expm1(rate / 4.0))


def query_matrix(key):
    drawn = jnp.clip(jax.random.normal(jax.random.fold_in(key, 31), (D, HEADS * HD), jnp.float32), -4.0, 4.0)
    return drawn / math.sqrt(D)


def draw_w_query(key, part):
    return query_matrix(key).astype(jnp.bfloat16)


def draw_w_key(key, part):
    own = jnp.clip(jax.random.normal(jax.random.fold_in(key, 32), (D, HD), jnp.float32), -4.0, 4.0) / math.sqrt(D)
    return own.astype(jnp.bfloat16)


def block_scale(own_key, dims, cuts, smallest, largest):
    factor_of = 1.0
    for dim, shards_of in cuts:
        heights = jax.random.uniform(jax.random.fold_in(jax.random.fold_in(own_key, 6), dim), (shards_of,), jnp.float32, smallest / len(cuts), largest / len(cuts))
        factor_of = factor_of * jnp.repeat(jnp.exp(heights), dims[dim] // shards_of).reshape((-1,) + (1,) * (len(dims) - 1 - dim))
    return factor_of


def scatter_about(rng, dims, scale, most, split=(), kind=jnp.bfloat16):
    values = scale * jax.random.normal(rng, dims, jnp.float32)
    if split:
        values = values * block_scale(rng, dims, split, -0.22, 0.18)
    return jnp.clip(values, -most, most).astype(kind)


def setup_inputs(seed: int = 0) -> dict:
    arg_keys = jax.random.split(jax.random.key(seed), 13)
    return {
        "tokens": draw_tokens(jax.random.fold_in(arg_keys[12], 71), 0),
        "w_branch": scatter_about(arg_keys[1], (D, LRU), D ** -0.5, 0.09375, ((1, 4),)),
        "w_input": scatter_about(arg_keys[2], (D, LRU), D ** -0.5, 0.09375, ((1, 4),)),
        "conv_kernel": scatter_about(arg_keys[3], (CONV, LRU), CONV ** -0.5, 3.0, ((1, 4),), jnp.float32),
        "w_rate": scatter_about(arg_keys[4], (NB, BW, BW), BW ** -0.5, 0.375, ((0, 4),)),
        "w_admit": scatter_about(arg_keys[5], (NB, BW, BW), BW ** -0.5, 0.375, ((0, 4),)),
        "lam": draw_lam(jax.random.fold_in(arg_keys[12], 71), 0),
        "w_out": scatter_about(arg_keys[7], (LRU, D), (LRU // 8) ** -0.5, 0.375, ((0, 4),)),
        "w_query": draw_w_query(jax.random.fold_in(arg_keys[12], 71), 0),
        "w_key": draw_w_key(jax.random.fold_in(arg_keys[12], 71), 0),
        "w_value": scatter_about(arg_keys[10], (D, HD), D ** -0.5, 0.09375, ((1, 4),)),
        "w_attn_out": scatter_about(arg_keys[11], (HEADS * HD, D), (HEADS * HD // 4) ** -0.5, 0.25, ((0, 4),)),
    }


def normalize(values):
    wide = values.astype(jnp.float32)
    return wide * lax.rsqrt(lax.optimization_barrier(jnp.mean(wide * wide, axis=-1, keepdims=True)) + 1e-06)

def rounded(values):
    return lax.optimization_barrier(values.astype(jnp.bfloat16)).astype(jnp.float32)

def rotate(values, positions):
    width = values.shape[-1]
    turned = width // 2
    half = turned // 2
    freqs = 10000.0 ** (-jnp.arange(half, dtype=jnp.float32) * 2.0 / turned)
    angles = positions.astype(jnp.float32)[:, None] * freqs[None, :]
    cosine = jnp.cos(angles)[:, None, :]
    sine = jnp.sin(angles)[:, None, :]
    first = values[..., :half]
    second = values[..., half:turned]
    return jnp.concatenate([first * cosine - second * sine, second * cosine + first * sine, values[..., turned:]], axis=-1)

def reference(tokens, w_branch, w_input, conv_kernel, w_rate, w_admit, lam, w_out, w_query, w_key, w_value, w_attn_out):
    count = B * SEQ
    normed = normalize(tokens).astype(jnp.bfloat16).reshape(count, D)
    branch = jax.nn.gelu(jnp.dot(normed, w_branch, preferred_element_type=jnp.float32))
    inner = jnp.dot(normed, w_input, preferred_element_type=jnp.float32).reshape(B, SEQ, LRU)
    padded = jnp.pad(inner, ((0, 0), (CONV - 1, 0), (0, 0)))
    convolved = jnp.zeros((B, SEQ, LRU), jnp.float32)
    for tap in range(CONV):
        convolved = convolved + conv_kernel[tap] * padded[:, CONV - 1 - tap:CONV - 1 - tap + SEQ, :]
    grouped = rounded(convolved).reshape(B, SEQ, NB, BW)
    rate_gate = jax.nn.sigmoid(jnp.einsum('bsnc,ncd->bsnd', grouped, w_rate.astype(jnp.float32))).reshape(B, SEQ, LRU)
    admit_gate = jax.nn.sigmoid(jnp.einsum('bsnc,ncd->bsnd', grouped, w_admit.astype(jnp.float32))).reshape(B, SEQ, LRU)
    log_decay = -8.0 * rate_gate * jax.nn.softplus(-lam)
    decay = jnp.exp(log_decay)
    scaled = admit_gate * convolved * jnp.sqrt(-jnp.expm1(2.0 * log_decay))

    def advance(carried, inputs):
        step_decay, step_input = inputs
        fresh = step_decay * carried + step_input
        return (fresh, fresh)
    _, states = lax.scan(advance, jnp.zeros((B, LRU), jnp.float32), (decay.transpose(1, 0, 2), scaled.transpose(1, 0, 2)))
    state = states.transpose(1, 0, 2)
    gated = (state.reshape(count, LRU) * branch).astype(jnp.bfloat16)
    resid = (tokens.reshape(count, D).astype(jnp.float32) + jnp.dot(gated, w_out, preferred_element_type=jnp.float32)).astype(jnp.bfloat16)
    normed_two = normalize(resid).astype(jnp.bfloat16)
    positions = jnp.arange(SEQ, dtype=jnp.int32)
    query = jnp.dot(normed_two, w_query, preferred_element_type=jnp.float32).reshape(B, SEQ, HEADS, HD)
    query = (rotate(query, positions) * HD ** (-0.5)).astype(jnp.bfloat16)
    key_raw = jnp.dot(normed_two, w_key, preferred_element_type=jnp.float32).astype(jnp.bfloat16)
    keys = rotate(key_raw.astype(jnp.float32).reshape(B, SEQ, 1, HD), positions).astype(jnp.bfloat16).reshape(B, SEQ, HD)
    values = jnp.dot(normed_two, w_value, preferred_element_type=jnp.float32).astype(jnp.bfloat16).reshape(B, SEQ, HD)
    key_pad = jnp.pad(keys, ((0, 0), (WINDOW, 0), (0, 0)))
    value_pad = jnp.pad(values, ((0, 0), (WINDOW, 0), (0, 0)))
    span = WINDOW + S_DEV

    def one_block(index):
        start = (index * S_DEV).astype(jnp.int32)
        query_block = lax.dynamic_slice_in_dim(query, start, S_DEV, 1).astype(jnp.float32)
        key_block = lax.dynamic_slice_in_dim(key_pad, start, span, 1).astype(jnp.float32)
        value_block = lax.dynamic_slice_in_dim(value_pad, start, span, 1).astype(jnp.float32)
        scores = jnp.einsum('bshc,bkc->bhsk', query_block, key_block)
        rows = jnp.arange(S_DEV, dtype=jnp.int32)[:, None]
        cols = jnp.arange(span, dtype=jnp.int32)[None, :]
        distance = rows + WINDOW - cols
        valid = (distance >= 0) & (distance < WINDOW) & (cols >= WINDOW - start)
        masked = jnp.where(valid, scores, -1e+30)
        top = lax.optimization_barrier(jnp.max(masked, axis=-1, keepdims=True))
        weights = jnp.where(valid, jnp.exp(masked - top), 0.0)
        probs = rounded(weights / lax.optimization_barrier(jnp.sum(weights, axis=-1, keepdims=True)))
        return jnp.einsum('bhsk,bkc->bshc', probs, value_block).astype(jnp.bfloat16)
    blocks = lax.map(one_block, jnp.arange(SEQ // S_DEV, dtype=jnp.int32))
    attended = blocks.transpose(1, 0, 2, 3, 4).reshape(count, HEADS * HD)
    result = resid.astype(jnp.float32) + jnp.dot(attended, w_attn_out, preferred_element_type=jnp.float32)
    return result.astype(jnp.bfloat16).reshape(B, SEQ, D)
```

```python
import functools

import jax
import jax.numpy as jnp
from jax import lax
from jax.experimental import pallas as pl
from jax.experimental.pallas import tpu as pltpu
from jax.sharding import PartitionSpec as P

HD = 256
WINDOW = 2048


EPSILON = 1e-06


def from_behind(x, axis, by):
    count = lax.axis_size(axis)
    pairs = [(i, i + by) for i in range(count) if 0 <= i + by < count]
    return lax.ppermute(x, axis, pairs)


def normalize(values):
    wide = values.astype(jnp.float32)
    return wide * lax.rsqrt(jnp.mean(wide * wide, axis=-1, keepdims=True) + EPSILON)


def recurrence_kernel(
    count, decay_ref, scaled_ref, branch_ref, out_ref, local, cumulative, edge, got, send, recv
):
    me = lax.axis_index("ctx")
    barrier = pltpu.get_barrier_semaphore()
    for step in range(1, count):
        pl.semaphore_signal(barrier, inc=1, device_id={"ctx": lax.rem(me + step, count)})
    rows, width = decay_ref.shape
    tile = 8
    place = lax.broadcasted_iota(jnp.int32, (tile, width), 0)

    def advance(index, carried):
        state, product = carried
        at = pl.ds(pl.multiple_of(index * tile, tile), tile)
        a = decay_ref[at, :]
        b = scaled_ref[at, :]
        for shift in (1, 2, 4):
            inside = place >= shift
            a_back = jnp.where(inside, pltpu.roll(a, shift, 0), 1.0)
            b_back = jnp.where(inside, pltpu.roll(b, shift, 0), 0.0)
            b = a * b_back + b
            a = a * a_back
        b = b + a * state
        a = a * product
        local[at, :] = b
        cumulative[at, :] = a
        return b[tile - 1 :, :], a[tile - 1 :, :]

    start = (jnp.zeros((1, width), jnp.float32), jnp.ones((1, width), jnp.float32))
    state, product = lax.fori_loop(0, rows // tile, advance, start, unroll=4)
    edge[0:1, :] = state
    edge[1:2, :] = product
    pl.semaphore_wait(barrier, count - 1)
    copies = []
    for step in range(1, count):
        copy = pltpu.make_async_remote_copy(
            src_ref=edge,
            dst_ref=got.at[step],
            send_sem=send.at[step],
            recv_sem=recv.at[step],
            device_id={"ctx": lax.rem(me + step, count)},
        )
        copy.start()
        copies.append(copy)
    for copy in copies:
        copy.wait()
    carry = jnp.zeros((1, width), jnp.float32)
    for step in range(count - 1, 0, -1):
        fresh = got[step, 0:1, :] + got[step, 1:2, :] * carry
        carry = jnp.where(me >= step, fresh, 0.0)

    def finish(index, _):
        at = pl.ds(pl.multiple_of(index * 16, 16), 16)
        whole = local[at, :] + cumulative[at, :] * carry
        out_ref[at, :] = (whole * branch_ref[at, :]).astype(out_ref.dtype)
        return 0

    lax.fori_loop(0, rows // 16, finish, 0, unroll=4)


def recurrence(decay, scaled, branch):
    rows, width = decay.shape
    count = lax.axis_size("ctx")
    vmem = pl.BlockSpec(memory_space=pltpu.VMEM)
    return pl.pallas_call(
        functools.partial(recurrence_kernel, count),
        out_shape=jax.ShapeDtypeStruct((rows, width), jnp.bfloat16),
        in_specs=[vmem] * 3,
        out_specs=vmem,
        scratch_shapes=[
            pltpu.VMEM((rows, width), jnp.float32),
            pltpu.VMEM((rows, width), jnp.float32),
            pltpu.VMEM((2, width), jnp.float32),
            pltpu.VMEM((count, 2, width), jnp.float32),
            pltpu.SemaphoreType.DMA((count,)),
            pltpu.SemaphoreType.DMA((count,)),
        ],
        compiler_params=pltpu.CompilerParams(collective_id=0, has_side_effects=True),
    )(decay, scaled, branch)


CHUNKS = 4
CHUNKS_MIDDLE = 8
CHUNKS_LAST = 8


def greet(me, count):
    barrier = pltpu.get_barrier_semaphore()
    for step in range(1, count):
        pl.semaphore_signal(barrier, inc=1, device_id={"mp": lax.rem(me + step, count)})
    pl.semaphore_wait(barrier, count - 1)


def each(chunks, body):
    def turn(chunk, _):
        body(chunk)
        return 0

    lax.fori_loop(0, chunks, turn, 0)


def span_of(chunk, rows):
    return pl.ds(pl.multiple_of(chunk * rows, rows), rows)


class Line:
    def __init__(self, me, count):
        self.me, self.count = me, count

    def steps(self, way):
        return self.me + 1 if way == 0 else self.me - 1

    def has_next(self, way):
        return self.me < self.count - 1 if way == 0 else self.me > 0

    def has_last(self, way):
        return self.me > 0 if way == 0 else self.me < self.count - 1

    def copy(self, way, src, dst, send, recv):
        return pltpu.make_async_remote_copy(
            src_ref=src,
            dst_ref=dst,
            send_sem=send,
            recv_sem=recv,
            device_id={"mp": self.steps(way)},
        )


def gather_part(line, own, out_ref, send, recv, cols, rows, chunks):
    me, count = line.me, line.count

    def region(owner, chunk):
        return out_ref.at[
            span_of(chunk, rows), pl.ds(pl.multiple_of(owner * cols, cols), cols)
        ]

    def source(way, step):
        return me - step if way == 0 else me + step

    def moved(way, step, chunk):
        owner = source(way, step)
        place = region(owner, chunk)
        return line.copy(
            way,
            own.at[span_of(chunk, rows), :] if step == 0 else place,
            place,
            send.at[way, step, chunk],
            recv.at[way, step, chunk],
        )

    def there(way, step):
        return source(way, step) >= 0 if way == 0 else source(way, step) < count

    def begin(chunk):
        for way in (0, 1):

            @pl.when(line.has_next(way))
            def _():
                moved(way, 0, chunk).start()

    def relay():
        for step in range(1, count):

            def turn(chunk, step=step):
                for way in (0, 1):

                    @pl.when(there(way, step))
                    def _():
                        place = region(source(way, step), chunk)
                        line.copy(
                            1 - way,
                            place,
                            place,
                            send.at[way, step - 1, chunk],
                            recv.at[way, step - 1, chunk],
                        ).wait_recv()

                    @pl.when(jnp.logical_and(there(way, step), line.has_next(way)))
                    def _():
                        moved(way, step, chunk).start()

            each(chunks, turn)

        for step in range(count):

            def turn(chunk, step=step):
                for way in (0, 1):

                    @pl.when(jnp.logical_and(there(way, step), line.has_next(way)))
                    def _():
                        moved(way, step, chunk).wait_send()

            each(chunks, turn)

    return region, begin, relay


def gather_kernel(count, chunks, own_ref, out_ref, send, recv, local):
    me = lax.axis_index("mp")
    rows, cols = own_ref.shape[0] // chunks, own_ref.shape[1]
    greet(me, count)
    line = Line(me, count)
    region, begin, relay = gather_part(line, own_ref, out_ref, send, recv, cols, rows, chunks)

    def turn(chunk):
        begin(chunk)

    each(chunks, turn)
    mine = out_ref.at[:, pl.ds(pl.multiple_of(me * cols, cols), cols)]
    kept = pltpu.make_async_copy(own_ref, mine, local.at[0])
    kept.start()
    relay()
    kept.wait()


def gather(own, mark, chunks=CHUNKS):
    count = lax.axis_size("mp")
    rows, cols = own.shape
    return pl.pallas_call(
        functools.partial(gather_kernel, count, chunks),
        out_shape=jax.ShapeDtypeStruct((rows, cols * count), own.dtype),
        in_specs=[pl.BlockSpec(memory_space=pltpu.VMEM)],
        out_specs=pl.BlockSpec(memory_space=pl.ANY),
        scratch_shapes=[
            pltpu.SemaphoreType.DMA((2, count, chunks)),
            pltpu.SemaphoreType.DMA((2, count, chunks)),
            pltpu.SemaphoreType.DMA((1,)),
        ],
        compiler_params=pltpu.CompilerParams(collective_id=mark, has_side_effects=True),
    )(own)


VMEM_LIMIT = 56 * 1024 * 1024


def meet(n, m):
    at, me = lax.axis_index("ctx"), lax.axis_index("mp")
    barrier = pltpu.get_barrier_semaphore()
    for step in range(1, n):
        pl.semaphore_signal(barrier, inc=1, device_id={"ctx": lax.rem(at + step, n)})
    for step in range(1, m):
        pl.semaphore_signal(barrier, inc=1, device_id={"mp": lax.rem(me + step, m)})
    pl.semaphore_wait(barrier, n + m - 2)


def meet_line(m):
    me = lax.axis_index("mp")
    barrier = pltpu.get_barrier_semaphore()
    for step in range(1, m):
        pl.semaphore_signal(barrier, inc=1, device_id={"mp": lax.rem(me + step, m)})
    pl.semaphore_wait(barrier, m - 1)


def within(chunk, chunks):
    return jnp.logical_and(chunk >= 0, chunk < chunks)


class Scatter:
    def __init__(self, line, part, held, send, recv, cols, rows, chunks):
        self.line, self.part, self.held = line, part, held
        self.send, self.recv = send, recv
        self.cols, self.rows, self.chunks = cols, rows, chunks

    def goal(self, way, step):
        return self.line.count - 1 - step if way == 0 else step

    def beyond(self, way, step):
        goal = self.goal(way, step)
        return goal > self.line.me if way == 0 else goal < self.line.me

    def hop(self, way):
        return self.line.me if way == 0 else self.line.count - 1 - self.line.me

    def late(self):
        return jnp.maximum(self.hop(0), self.hop(1))

    def moved(self, way, step, chunk, towards):
        place = self.held.at[way, step, span_of(chunk, self.rows), :]
        return self.line.copy(
            towards, place, place, self.send.at[way, step, chunk], self.recv.at[way, step, chunk]
        )

    def term(self, owner, chunk):
        at = pl.ds(pl.multiple_of(owner * self.cols, self.cols), self.cols)
        return self.part[span_of(chunk, self.rows), at]

    def pass_on(self, tick):
        line, held = self.line, self.held
        for way in (0, 1):
            chunk = tick - self.hop(way)
            at = span_of(chunk, self.rows)
            for step in range(line.count - 1):

                @pl.when(jnp.logical_and(within(chunk, self.chunks), self.beyond(way, step)))
                def _(way=way, step=step, chunk=chunk, at=at):
                    own = self.term(self.goal(way, step), chunk)

                    @pl.when(line.has_last(way))
                    def _():
                        self.moved(way, step, chunk, 1 - way).wait_recv()
                        total = held[way, step, at, :].astype(jnp.float32) + own
                        held[way, step, at, :] = total.astype(held.dtype)

                    @pl.when(jnp.logical_not(line.has_last(way)))
                    def _():
                        held[way, step, at, :] = own.astype(held.dtype)

                    self.moved(way, step, chunk, way).start()

    def arrive(self, chunk, base, total):
        line = self.line
        total[...] = base.astype(jnp.float32) + self.term(line.me, chunk)
        for way in (0, 1):
            step = line.count - 1 - line.me if way == 0 else line.me

            @pl.when(line.has_last(way))
            def _(way=way, step=step):
                self.moved(way, step, chunk, 1 - way).wait_recv()
                total[...] += self.held[way, step, span_of(chunk, self.rows), :].astype(
                    jnp.float32
                )

    def settle(self):
        for step in range(self.line.count - 1):

            def turn(chunk, step=step):
                for way in (0, 1):

                    @pl.when(self.beyond(way, step))
                    def _(way=way):
                        self.moved(way, step, chunk, way).wait_send()

            each(self.chunks, turn)


class Gather:
    def __init__(self, line, full, send, recv, cols, rows, chunks):
        self.line, self.full = line, full
        self.send, self.recv = send, recv
        self.cols, self.rows, self.chunks = cols, rows, chunks

    def place(self, owner, chunk):
        at = pl.ds(pl.multiple_of(owner * self.cols, self.cols), self.cols)
        return self.full.at[span_of(chunk, self.rows), at]

    def source(self, way, step):
        return self.line.me - step if way == 0 else self.line.me + step

    def there(self, way, step):
        source = self.source(way, step)
        return source >= 0 if way == 0 else source < self.line.count

    def moved(self, way, step, source, chunk, towards):
        place = self.place(source, chunk)
        return self.line.copy(
            towards, place, place, self.send.at[way, step, chunk], self.recv.at[way, step, chunk]
        )

    def begin(self, chunk):
        for way in (0, 1):

            @pl.when(self.line.has_next(way))
            def _(way=way):
                self.moved(way, 0, self.line.me, chunk, way).start()

    def relay(self, tick, late):
        for step in range(1, self.line.count):
            for way in (0, 1):
                source = self.source(way, step)
                chunk = tick - late(source) - step

                @pl.when(jnp.logical_and(within(chunk, self.chunks), self.there(way, step)))
                def _(way=way, step=step, source=source, chunk=chunk):
                    self.moved(way, step - 1, source, chunk, 1 - way).wait_recv()

                    @pl.when(self.line.has_next(way))
                    def _():
                        self.moved(way, step, source, chunk, way).start()

    def settle(self):
        for step in range(self.line.count):

            def turn(chunk, step=step):
                for way in (0, 1):

                    @pl.when(jnp.logical_and(self.there(way, step), self.line.has_next(way)))
                    def _(way=way):
                        self.moved(way, step, self.source(way, step), chunk, way).wait_send()

            each(self.chunks, turn)


def loop(count, body):
    def turn(index, _):
        body(index)
        return 0

    lax.fori_loop(0, count, turn, 0)


def turn_pairs(values, cosine, sine):
    turned = cosine.shape[-1]
    head = values[:, :turned]
    head = head * cosine + pltpu.roll(head, turned // 2, 1) * sine
    return jnp.concatenate([head, values[:, turned:]], axis=-1)


def middle_kernel(
    n, m, chunks,
    gated_ref, base_ref, w_out_ref, w_query_ref, w_kv_ref, cos_ref, sin_ref,
    own_ref, query_ref, window_ref,
    w_out, w_query, w_kv, part, total, held, full, kv, zeros,
    loads, s_send, s_recv, g_send, g_recv, k_send, k_recv, k_local, z_local,
):
    at, me = lax.axis_index("ctx"), lax.axis_index("mp")
    count, cols = base_ref.shape
    rows = count // chunks
    back = window_ref.shape[0] // count - 1
    fetches = [
        pltpu.make_async_copy(w_out_ref, w_out, loads.at[0]),
        pltpu.make_async_copy(w_query_ref, w_query, loads.at[1]),
        pltpu.make_async_copy(w_kv_ref, w_kv, loads.at[2]),
    ]
    for fetch in fetches:
        fetch.start()
    meet(n, m)
    line = Line(me, m)
    scatter = Scatter(line, part, held, s_send, s_recv, cols, rows, chunks)
    gather = Gather(line, full, g_send, g_recv, cols, rows, chunks)

    def product(chunk):
        taken = gated_ref[span_of(chunk, rows), :]
        for owner in range(m):
            there = slice(owner * cols, (owner + 1) * cols)
            part[span_of(chunk, rows), there] = jnp.dot(
                taken, w_out[:, there], preferred_element_type=jnp.float32
            )

    def ahead(distance, chunk):
        return pltpu.make_async_remote_copy(
            src_ref=kv.at[span_of(chunk, rows), :],
            dst_ref=window_ref.at[span_of((back - distance) * chunks + chunk, rows), :],
            send_sem=k_send.at[distance - 1, chunk],
            recv_sem=k_recv.at[distance - 1, chunk],
            device_id={"ctx": lax.rem(at + distance, n)},
        )

    def kept(chunk):
        return pltpu.make_async_copy(
            kv.at[span_of(chunk, rows), :],
            window_ref.at[span_of(back * chunks + chunk, rows), :],
            k_local.at[chunk],
        )

    def blank(distance):
        return pltpu.make_async_copy(
            zeros, window_ref.at[span_of(back - distance, count), :], z_local.at[distance - 1]
        )

    def late(source):
        return jnp.maximum(source, m - 1 - source)

    def latest():
        most = late(me)
        for source in range(m):
            most = jnp.maximum(most, max(source, m - 1 - source) + jnp.abs(me - source))
        return most

    def project(chunk):
        span = span_of(chunk, rows)
        wide = full[span, :].astype(jnp.float32)
        scale = lax.rsqrt(jnp.mean(wide * wide, axis=-1, keepdims=True) + EPSILON)
        normed = (wide * scale).astype(jnp.bfloat16)
        cosine, sine = cos_ref[span, :], sin_ref[span, :]
        both = jnp.dot(normed, w_kv[...], preferred_element_type=jnp.float32)
        key = both[:, :HD].astype(jnp.bfloat16).astype(jnp.float32)
        kv[span, :HD] = turn_pairs(key, cosine, sine).astype(kv.dtype)
        kv[span, HD:] = both[:, HD:].astype(kv.dtype)
        kept(chunk).start()
        for distance in range(1, back + 1):

            @pl.when(at + distance < n)
            def _(distance=distance):
                ahead(distance, chunk).start()

        query = jnp.dot(normed, w_query[...], preferred_element_type=jnp.float32)
        for head in range(query.shape[1] // HD):
            there = slice(head * HD, (head + 1) * HD)
            turned = turn_pairs(query[:, there], cosine, sine) * HD ** (-0.5)
            query_ref[span, there] = turned.astype(query_ref.dtype)

    zeros[...] = jnp.zeros_like(zeros)
    for distance in range(1, back + 1):

        @pl.when(at < distance)
        def _(distance=distance):
            blank(distance).start()

    fetches[0].wait()
    product(0)

    def tick(t):
        scatter.pass_on(t)
        done = t - scatter.late()

        @pl.when(within(done, chunks))
        def _():
            span = span_of(done, rows)
            scatter.arrive(done, base_ref[span, :], total)
            mine = total[...].astype(own_ref.dtype)
            own_ref[span, :] = mine
            full[span, pl.ds(pl.multiple_of(me * cols, cols), cols)] = mine
            gather.begin(done)

        gather.relay(t, late)

        @pl.when(t + 1 < chunks)
        def _():
            product(t + 1)

        whole = t - latest()

        @pl.when(whole == 0)
        def _():
            fetches[1].wait()
            fetches[2].wait()

        @pl.when(within(whole, chunks))
        def _():
            project(whole)

    loop(chunks + 2 * (m - 1), tick)
    scatter.settle()
    gather.settle()
    for distance in range(1, back + 1):

        @pl.when(at < distance)
        def _(distance=distance):
            blank(distance).wait()

        def turn(chunk, distance=distance):
            @pl.when(at + distance < n)
            def _():
                ahead(distance, chunk).wait_send()

            @pl.when(at >= distance)
            def _():
                ahead(distance, chunk).wait_recv()

        each(chunks, turn)
    each(chunks, lambda chunk: kept(chunk).wait())


def middle(gated, base, w_out, w_query, w_kv, cosine, sine, mark, chunks):
    n, m = lax.axis_size("ctx"), lax.axis_size("mp")
    count, cols = base.shape
    channels, width = w_out.shape
    queries = w_query.shape[1]
    wide = w_kv.shape[1]
    rows = count // chunks
    back = WINDOW // count
    vmem = pl.BlockSpec(memory_space=pltpu.VMEM)
    hbm = pl.BlockSpec(memory_space=pl.ANY)
    low = jnp.bfloat16
    dma = pltpu.SemaphoreType.DMA
    return pl.pallas_call(
        functools.partial(middle_kernel, n, m, chunks),
        out_shape=(
            jax.ShapeDtypeStruct((count, cols), low),
            jax.ShapeDtypeStruct((count, queries), low),
            jax.ShapeDtypeStruct(((back + 1) * count, wide), low),
        ),
        in_specs=[vmem, vmem, hbm, hbm, hbm, vmem, vmem],
        out_specs=(vmem, vmem, hbm),
        scratch_shapes=[
            pltpu.VMEM((channels, width), low),
            pltpu.VMEM((width, queries), low),
            pltpu.VMEM((width, wide), low),
            pltpu.VMEM((count, width), jnp.float32),
            pltpu.VMEM((rows, cols), jnp.float32),
            pltpu.VMEM((2, m - 1, count, cols), low),
            pltpu.VMEM((count, width), low),
            pltpu.VMEM((count, wide), low),
            pltpu.VMEM((count, wide), low),
            dma((3,)),
            dma((2, m - 1, chunks)),
            dma((2, m - 1, chunks)),
            dma((2, m, chunks)),
            dma((2, m, chunks)),
            dma((back, chunks)),
            dma((back, chunks)),
            dma((chunks,)),
            dma((back,)),
        ],
        compiler_params=pltpu.CompilerParams(
            collective_id=mark, has_side_effects=True, vmem_limit_bytes=VMEM_LIMIT
        ),
    )(gated, base, w_out, w_query, w_kv, cosine, sine)


def last_kernel(
    m, chunks,
    query_ref, window_ref, base_ref, w_out_ref,
    own_ref,
    w_out, part, total, held, loads, s_send, s_recv,
):
    at, me = lax.axis_index("ctx"), lax.axis_index("mp")
    count, cols = base_ref.shape
    rows = count // chunks
    heads = query_ref.shape[1] // HD
    fetch = pltpu.make_async_copy(w_out_ref, w_out, loads.at[0])
    fetch.start()
    meet_line(m)
    line = Line(me, m)
    scatter = Scatter(line, part, held, s_send, s_recv, cols, rows, chunks)
    step = max(rows, 128)
    reach = WINDOW + step

    def attend(chunk):
        span = span_of(chunk, rows)
        first = pl.multiple_of(chunk * rows // step * step, step)
        keys = window_ref[pl.ds(first, reach), :HD]
        values = window_ref[pl.ds(first, reach), HD:]
        row = chunk * rows + lax.broadcasted_iota(jnp.int32, (rows, reach), 0)
        col = first + lax.broadcasted_iota(jnp.int32, (rows, reach), 1)
        distance = row + WINDOW - col
        valid = (distance >= 0) & (distance < WINDOW) & (col >= WINDOW - at * count)
        attended = []
        for head in range(heads):
            scores = lax.dot_general(
                query_ref[span, head * HD : (head + 1) * HD],
                keys,
                (((1,), (1,)), ((), ())),
                preferred_element_type=jnp.float32,
            )
            masked = jnp.where(valid, scores, -1e30)
            top = jnp.max(masked, axis=-1, keepdims=True)
            weights = jnp.exp(masked - top)
            share = 1.0 / jnp.sum(weights, axis=-1, keepdims=True)
            probs = (weights * share).astype(jnp.bfloat16)
            attended.append(
                jnp.dot(probs, values, preferred_element_type=jnp.float32).astype(jnp.bfloat16)
            )
        taken = jnp.concatenate(attended, axis=-1)
        for owner in range(m):
            there = slice(owner * cols, (owner + 1) * cols)
            part[span, there] = jnp.dot(
                taken, w_out[:, there], preferred_element_type=jnp.float32
            )

    fetch.wait()
    attend(0)

    def tick(t):
        scatter.pass_on(t)
        done = t - scatter.late()

        @pl.when(within(done, chunks))
        def _():
            span = span_of(done, rows)
            scatter.arrive(done, base_ref[span, :], total)
            own_ref[span, :] = total[...].astype(own_ref.dtype)

        @pl.when(t + 1 < chunks)
        def _():
            attend(t + 1)

    loop(chunks + m - 1, tick)
    scatter.settle()


def last(query, window, base, w_out, mark, chunks):
    m = lax.axis_size("mp")
    count, cols = base.shape
    channels, width = w_out.shape
    rows = count // chunks
    vmem = pl.BlockSpec(memory_space=pltpu.VMEM)
    hbm = pl.BlockSpec(memory_space=pl.ANY)
    low = jnp.bfloat16
    dma = pltpu.SemaphoreType.DMA
    return pl.pallas_call(
        functools.partial(last_kernel, m, chunks),
        out_shape=jax.ShapeDtypeStruct((count, cols), low),
        in_specs=[vmem, vmem, vmem, hbm],
        out_specs=vmem,
        scratch_shapes=[
            pltpu.VMEM((channels, width), low),
            pltpu.VMEM((count, width), jnp.float32),
            pltpu.VMEM((rows, cols), jnp.float32),
            pltpu.VMEM((2, m - 1, count, cols), low),
            dma((1,)),
            dma((2, m - 1, chunks)),
            dma((2, m - 1, chunks)),
        ],
        compiler_params=pltpu.CompilerParams(
            collective_id=mark, has_side_effects=True, vmem_limit_bytes=VMEM_LIMIT
        ),
    )(query, window, base, w_out)


def whole_kv(w_key, w_value):
    n, m = lax.axis_size("ctx"), lax.axis_size("mp")
    width, part = w_key.shape
    rows = width // n
    mine = lax.axis_index("ctx") * rows
    both = jnp.concatenate(
        [
            lax.dynamic_slice_in_dim(w_key, mine, rows, 0),
            lax.dynamic_slice_in_dim(w_value, mine, rows, 0),
        ],
        axis=1,
    )
    every = lax.all_gather(both, ("ctx", "mp"))
    every = every.reshape(n, m, rows, 2, part).transpose(0, 2, 3, 1, 4)
    return every.reshape(width, 2 * m * part)


def turns(positions):
    turned = HD // 2
    half = turned // 2
    freqs = 10000.0 ** (-jnp.arange(half, dtype=jnp.float32) * 2.0 / turned)
    angles = positions.astype(jnp.float32)[:, None] * freqs[None, :]
    cosine, sine = jnp.cos(angles), jnp.sin(angles)
    return (
        jnp.concatenate([cosine, cosine], axis=-1),
        jnp.concatenate([-sine, sine], axis=-1),
    )


def on_device(
    tokens,
    w_branch,
    w_input,
    conv_kernel,
    w_rate,
    w_admit,
    lam,
    w_out,
    w_query,
    w_key,
    w_value,
    w_attn_out,
):
    batch, rows_dev, cols_dev = tokens.shape
    count = batch * rows_dev
    width = w_branch.shape[0]
    tokens_flat = tokens.reshape(count, cols_dev)
    w_kv = whole_kv(w_key, w_value)
    full = gather(tokens_flat, 1)
    normed = normalize(full).astype(jnp.bfloat16).reshape(count, width)
    branch = jax.nn.gelu(jnp.dot(normed, w_branch, preferred_element_type=jnp.float32))
    inner = jnp.dot(normed, w_input, preferred_element_type=jnp.float32).reshape(
        batch, rows_dev, -1
    )
    taps = conv_kernel.shape[0]
    rim = from_behind(inner[:, rows_dev - taps + 1 :, :], "ctx", 1)
    extended = jnp.concatenate([rim, inner], axis=1)
    convolved = jnp.zeros_like(inner)
    for tap in range(taps):
        convolved = (
            convolved
            + conv_kernel[tap] * extended[:, taps - 1 - tap : taps - 1 - tap + rows_dev, :]
        )
    blocks = w_rate.shape[0]
    block_width = w_rate.shape[1]
    low = convolved.astype(jnp.bfloat16).reshape(count, -1)

    def gate(weights):
        products = [
            jnp.dot(
                low[:, block * block_width : (block + 1) * block_width],
                weights[block],
                preferred_element_type=jnp.float32,
            )
            for block in range(blocks)
        ]
        return jax.nn.sigmoid(jnp.concatenate(products, axis=-1)).reshape(batch, rows_dev, -1)

    rate_gate = gate(w_rate)
    admit_gate = gate(w_admit)
    log_decay = -8.0 * rate_gate * jax.nn.softplus(-lam)
    decay = jnp.exp(log_decay)
    scaled = admit_gate * convolved * jnp.sqrt(-jnp.expm1(2.0 * log_decay))
    channels = decay.shape[-1]
    gated = recurrence(
        decay.reshape(count, channels), scaled.reshape(count, channels), branch
    )
    base = lax.axis_index("ctx") * rows_dev
    positions = base + jnp.arange(rows_dev, dtype=jnp.int32)
    cosine, sine = turns(positions)
    resid, query, window = middle(
        gated, tokens_flat, w_out, w_query, w_kv, cosine, sine, 2, CHUNKS_MIDDLE
    )
    result = last(query, window, resid, w_attn_out, 3, CHUNKS_LAST)
    return result.reshape(batch, rows_dev, cols_dev)


def solution(mesh):
    in_specs = (
        P(None, "ctx", "mp"),
        P(None, "mp"),
        P(None, "mp"),
        P(None, "mp"),
        P("mp", None, None),
        P("mp", None, None),
        P("mp"),
        P("mp", None),
        P(None, "mp"),
        P(None, "mp"),
        P(None, "mp"),
        P("mp", None),
    )
    out_specs = P(None, "ctx", "mp")
    return jax.shard_map(
        on_device, mesh=mesh, in_specs=in_specs, out_specs=out_specs, check_vma=False
    )
```

```python
import functools

import jax
import jax.numpy as jnp
from jax import lax
from jax.experimental import pallas as pl
from jax.experimental.pallas import tpu as pltpu
from jax.sharding import PartitionSpec as P

HD = 256
WINDOW = 2048


EPSILON = 1e-06


def from_behind(x, axis, by):
    count = lax.axis_size(axis)
    pairs = [(i, i + by) for i in range(count) if 0 <= i + by < count]
    return lax.ppermute(x, axis, pairs)


def normalize(values):
    wide = values.astype(jnp.float32)
    return wide * lax.rsqrt(jnp.mean(wide * wide, axis=-1, keepdims=True) + EPSILON)


def recurrence_kernel(
    count, decay_ref, scaled_ref, branch_ref, out_ref, local, cumulative, edge, got, send, recv
):
    me = lax.axis_index("ctx")
    barrier = pltpu.get_barrier_semaphore()
    for step in range(1, count):
        pl.semaphore_signal(barrier, inc=1, device_id={"ctx": lax.rem(me + step, count)})
    rows, width = decay_ref.shape
    tile = 8
    place = lax.broadcasted_iota(jnp.int32, (tile, width), 0)

    def advance(index, carried):
        state, product = carried
        at = pl.ds(pl.multiple_of(index * tile, tile), tile)
        a = decay_ref[at, :]
        b = scaled_ref[at, :]
        for shift in (1, 2, 4):
            inside = place >= shift
            a_back = jnp.where(inside, pltpu.roll(a, shift, 0), 1.0)
            b_back = jnp.where(inside, pltpu.roll(b, shift, 0), 0.0)
            b = a * b_back + b
            a = a * a_back
        b = b + a * state
        a = a * product
        local[at, :] = b
        cumulative[at, :] = a
        return b[tile - 1 :, :], a[tile - 1 :, :]

    start = (jnp.zeros((1, width), jnp.float32), jnp.ones((1, width), jnp.float32))
    state, product = lax.fori_loop(0, rows // tile, advance, start, unroll=4)
    edge[0:1, :] = state
    edge[1:2, :] = product
    pl.semaphore_wait(barrier, count - 1)
    copies = []
    for step in range(1, count):
        copy = pltpu.make_async_remote_copy(
            src_ref=edge,
            dst_ref=got.at[step],
            send_sem=send.at[step],
            recv_sem=recv.at[step],
            device_id={"ctx": lax.rem(me + step, count)},
        )
        copy.start()
        copies.append(copy)
    for copy in copies:
        copy.wait()
    carry = jnp.zeros((1, width), jnp.float32)
    for step in range(count - 1, 0, -1):
        fresh = got[step, 0:1, :] + got[step, 1:2, :] * carry
        carry = jnp.where(me >= step, fresh, 0.0)

    def finish(index, _):
        at = pl.ds(pl.multiple_of(index * 16, 16), 16)
        whole = local[at, :] + cumulative[at, :] * carry
        out_ref[at, :] = (whole * branch_ref[at, :]).astype(out_ref.dtype)
        return 0

    lax.fori_loop(0, rows // 16, finish, 0, unroll=4)


def recurrence(decay, scaled, branch):
    rows, width = decay.shape
    count = lax.axis_size("ctx")
    vmem = pl.BlockSpec(memory_space=pltpu.VMEM)
    return pl.pallas_call(
        functools.partial(recurrence_kernel, count),
        out_shape=jax.ShapeDtypeStruct((rows, width), jnp.bfloat16),
        in_specs=[vmem] * 3,
        out_specs=vmem,
        scratch_shapes=[
            pltpu.VMEM((rows, width), jnp.float32),
            pltpu.VMEM((rows, width), jnp.float32),
            pltpu.VMEM((2, width), jnp.float32),
            pltpu.VMEM((count, 2, width), jnp.float32),
            pltpu.SemaphoreType.DMA((count,)),
            pltpu.SemaphoreType.DMA((count,)),
        ],
        compiler_params=pltpu.CompilerParams(collective_id=0, has_side_effects=True),
    )(decay, scaled, branch)


CHUNKS = 4
CHUNKS_MIDDLE = 16
CHUNKS_LAST = 8


def greet(me, count):
    barrier = pltpu.get_barrier_semaphore()
    for step in range(1, count):
        pl.semaphore_signal(barrier, inc=1, device_id={"mp": lax.rem(me + step, count)})
    pl.semaphore_wait(barrier, count - 1)


def each(chunks, body):
    def turn(chunk, _):
        body(chunk)
        return 0

    lax.fori_loop(0, chunks, turn, 0)


def span_of(chunk, rows):
    return pl.ds(pl.multiple_of(chunk * rows, rows), rows)


class Line:
    def __init__(self, me, count):
        self.me, self.count = me, count

    def steps(self, way):
        return self.me + 1 if way == 0 else self.me - 1

    def has_next(self, way):
        return self.me < self.count - 1 if way == 0 else self.me > 0

    def has_last(self, way):
        return self.me > 0 if way == 0 else self.me < self.count - 1

    def copy(self, way, src, dst, send, recv):
        return pltpu.make_async_remote_copy(
            src_ref=src,
            dst_ref=dst,
            send_sem=send,
            recv_sem=recv,
            device_id={"mp": self.steps(way)},
        )


def gather_part(line, own, out_ref, send, recv, cols, rows, chunks):
    me, count = line.me, line.count

    def region(owner, chunk):
        return out_ref.at[
            span_of(chunk, rows), pl.ds(pl.multiple_of(owner * cols, cols), cols)
        ]

    def source(way, step):
        return me - step if way == 0 else me + step

    def moved(way, step, chunk):
        owner = source(way, step)
        place = region(owner, chunk)
        return line.copy(
            way,
            own.at[span_of(chunk, rows), :] if step == 0 else place,
            place,
            send.at[way, step, chunk],
            recv.at[way, step, chunk],
        )

    def there(way, step):
        return source(way, step) >= 0 if way == 0 else source(way, step) < count

    def begin(chunk):
        for way in (0, 1):

            @pl.when(line.has_next(way))
            def _():
                moved(way, 0, chunk).start()

    def relay():
        for step in range(1, count):

            def turn(chunk, step=step):
                for way in (0, 1):

                    @pl.when(there(way, step))
                    def _():
                        place = region(source(way, step), chunk)
                        line.copy(
                            1 - way,
                            place,
                            place,
                            send.at[way, step - 1, chunk],
                            recv.at[way, step - 1, chunk],
                        ).wait_recv()

                    @pl.when(jnp.logical_and(there(way, step), line.has_next(way)))
                    def _():
                        moved(way, step, chunk).start()

            each(chunks, turn)

        for step in range(count):

            def turn(chunk, step=step):
                for way in (0, 1):

                    @pl.when(jnp.logical_and(there(way, step), line.has_next(way)))
                    def _():
                        moved(way, step, chunk).wait_send()

            each(chunks, turn)

    return region, begin, relay


def gather_kernel(count, chunks, own_ref, out_ref, send, recv, local):
    me = lax.axis_index("mp")
    rows, cols = own_ref.shape[0] // chunks, own_ref.shape[1]
    greet(me, count)
    line = Line(me, count)
    region, begin, relay = gather_part(line, own_ref, out_ref, send, recv, cols, rows, chunks)

    def turn(chunk):
        begin(chunk)

    each(chunks, turn)
    mine = out_ref.at[:, pl.ds(pl.multiple_of(me * cols, cols), cols)]
    kept = pltpu.make_async_copy(own_ref, mine, local.at[0])
    kept.start()
    relay()
    kept.wait()


def gather(own, mark, chunks=CHUNKS):
    count = lax.axis_size("mp")
    rows, cols = own.shape
    return pl.pallas_call(
        functools.partial(gather_kernel, count, chunks),
        out_shape=jax.ShapeDtypeStruct((rows, cols * count), own.dtype),
        in_specs=[pl.BlockSpec(memory_space=pltpu.VMEM)],
        out_specs=pl.BlockSpec(memory_space=pl.ANY),
        scratch_shapes=[
            pltpu.SemaphoreType.DMA((2, count, chunks)),
            pltpu.SemaphoreType.DMA((2, count, chunks)),
            pltpu.SemaphoreType.DMA((1,)),
        ],
        compiler_params=pltpu.CompilerParams(collective_id=mark, has_side_effects=True),
    )(own)


VMEM_LIMIT = 56 * 1024 * 1024


def meet(n, m):
    at, me = lax.axis_index("ctx"), lax.axis_index("mp")
    barrier = pltpu.get_barrier_semaphore()
    for step in range(1, n):
        pl.semaphore_signal(barrier, inc=1, device_id={"ctx": lax.rem(at + step, n)})
    for step in range(1, m):
        pl.semaphore_signal(barrier, inc=1, device_id={"mp": lax.rem(me + step, m)})
    pl.semaphore_wait(barrier, n + m - 2)


def meet_line(m):
    me = lax.axis_index("mp")
    barrier = pltpu.get_barrier_semaphore()
    for step in range(1, m):
        pl.semaphore_signal(barrier, inc=1, device_id={"mp": lax.rem(me + step, m)})
    pl.semaphore_wait(barrier, m - 1)


def within(chunk, chunks):
    return jnp.logical_and(chunk >= 0, chunk < chunks)


class Scatter:
    def __init__(self, line, part, held, send, recv, cols, rows, chunks):
        self.line, self.part, self.held = line, part, held
        self.send, self.recv = send, recv
        self.cols, self.rows, self.chunks = cols, rows, chunks

    def goal(self, way, step):
        return self.line.count - 1 - step if way == 0 else step

    def beyond(self, way, step):
        goal = self.goal(way, step)
        return goal > self.line.me if way == 0 else goal < self.line.me

    def hop(self, way):
        return self.line.me if way == 0 else self.line.count - 1 - self.line.me

    def late(self):
        return jnp.maximum(self.hop(0), self.hop(1))

    def moved(self, way, step, chunk, towards):
        place = self.held.at[way, step, span_of(chunk, self.rows), :]
        return self.line.copy(
            towards, place, place, self.send.at[way, step, chunk], self.recv.at[way, step, chunk]
        )

    def term(self, owner, chunk):
        at = pl.ds(pl.multiple_of(owner * self.cols, self.cols), self.cols)
        return self.part[span_of(chunk, self.rows), at]

    def pass_on(self, tick):
        line, held = self.line, self.held
        for way in (0, 1):
            chunk = tick - self.hop(way)
            at = span_of(chunk, self.rows)
            for step in range(line.count - 1):

                @pl.when(jnp.logical_and(within(chunk, self.chunks), self.beyond(way, step)))
                def _(way=way, step=step, chunk=chunk, at=at):
                    own = self.term(self.goal(way, step), chunk)

                    @pl.when(line.has_last(way))
                    def _():
                        self.moved(way, step, chunk, 1 - way).wait_recv()
                        total = held[way, step, at, :].astype(jnp.float32) + own
                        held[way, step, at, :] = total.astype(held.dtype)

                    @pl.when(jnp.logical_not(line.has_last(way)))
                    def _():
                        held[way, step, at, :] = own.astype(held.dtype)

                    self.moved(way, step, chunk, way).start()

    def arrive(self, chunk, base, total):
        line = self.line
        total[...] = base.astype(jnp.float32) + self.term(line.me, chunk)
        for way in (0, 1):
            step = line.count - 1 - line.me if way == 0 else line.me

            @pl.when(line.has_last(way))
            def _(way=way, step=step):
                self.moved(way, step, chunk, 1 - way).wait_recv()
                total[...] += self.held[way, step, span_of(chunk, self.rows), :].astype(
                    jnp.float32
                )

    def settle(self):
        for step in range(self.line.count - 1):

            def turn(chunk, step=step):
                for way in (0, 1):

                    @pl.when(self.beyond(way, step))
                    def _(way=way):
                        self.moved(way, step, chunk, way).wait_send()

            each(self.chunks, turn)


class Gather:
    def __init__(self, line, full, send, recv, cols, rows, chunks):
        self.line, self.full = line, full
        self.send, self.recv = send, recv
        self.cols, self.rows, self.chunks = cols, rows, chunks

    def place(self, owner, chunk):
        at = pl.ds(pl.multiple_of(owner * self.cols, self.cols), self.cols)
        return self.full.at[span_of(chunk, self.rows), at]

    def source(self, way, step):
        return self.line.me - step if way == 0 else self.line.me + step

    def there(self, way, step):
        source = self.source(way, step)
        return source >= 0 if way == 0 else source < self.line.count

    def moved(self, way, step, source, chunk, towards):
        place = self.place(source, chunk)
        return self.line.copy(
            towards, place, place, self.send.at[way, step, chunk], self.recv.at[way, step, chunk]
        )

    def begin(self, chunk):
        for way in (0, 1):

            @pl.when(self.line.has_next(way))
            def _(way=way):
                self.moved(way, 0, self.line.me, chunk, way).start()

    def relay(self, tick, late):
        for step in range(1, self.line.count):
            for way in (0, 1):
                source = self.source(way, step)
                chunk = tick - late(source) - step

                @pl.when(jnp.logical_and(within(chunk, self.chunks), self.there(way, step)))
                def _(way=way, step=step, source=source, chunk=chunk):
                    self.moved(way, step - 1, source, chunk, 1 - way).wait_recv()

                    @pl.when(self.line.has_next(way))
                    def _():
                        self.moved(way, step, source, chunk, way).start()

    def settle(self):
        for step in range(self.line.count):

            def turn(chunk, step=step):
                for way in (0, 1):

                    @pl.when(jnp.logical_and(self.there(way, step), self.line.has_next(way)))
                    def _(way=way):
                        self.moved(way, step, self.source(way, step), chunk, way).wait_send()

            each(self.chunks, turn)


def loop(count, body):
    def turn(index, _):
        body(index)
        return 0

    lax.fori_loop(0, count, turn, 0)


def turn_pairs(values, cosine, sine):
    turned = cosine.shape[-1]
    head = values[:, :turned]
    head = head * cosine + pltpu.roll(head, turned // 2, 1) * sine
    return jnp.concatenate([head, values[:, turned:]], axis=-1)


def middle_kernel(
    n, m, chunks,
    gated_ref, base_ref, w_out_ref, w_query_ref, w_key_ref, w_value_ref, cos_ref, sin_ref,
    own_ref, query_ref, window_ref,
    w_out, w_query, w_key, w_value, part, total, held, full, raw, kv, zeros,
    loads, s_send, s_recv, g_send, g_recv, r_send, r_recv, k_send, k_recv, k_local, z_local,
):
    at, me = lax.axis_index("ctx"), lax.axis_index("mp")
    count, cols = base_ref.shape
    rows = count // chunks
    back = window_ref.shape[0] // count - 1
    fetches = [
        pltpu.make_async_copy(w_out_ref, w_out, loads.at[0]),
        pltpu.make_async_copy(w_query_ref, w_query, loads.at[1]),
        pltpu.make_async_copy(w_key_ref, w_key, loads.at[2]),
        pltpu.make_async_copy(w_value_ref, w_value, loads.at[3]),
    ]
    for fetch in fetches:
        fetch.start()
    meet(n, m)
    line = Line(me, m)
    scatter = Scatter(line, part, held, s_send, s_recv, cols, rows, chunks)
    gather = Gather(line, full, g_send, g_recv, cols, rows, chunks)

    def product(chunk):
        taken = gated_ref[span_of(chunk, rows), :]
        for owner in range(m):
            there = slice(owner * cols, (owner + 1) * cols)
            part[span_of(chunk, rows), there] = jnp.dot(
                taken, w_out[:, there], preferred_element_type=jnp.float32
            )

    def ahead(distance, chunk):
        return pltpu.make_async_remote_copy(
            src_ref=kv.at[span_of(chunk, rows), :],
            dst_ref=window_ref.at[span_of((back - distance) * chunks + chunk, rows), :],
            send_sem=k_send.at[distance - 1, chunk],
            recv_sem=k_recv.at[distance - 1, chunk],
            device_id={"ctx": lax.rem(at + distance, n)},
        )

    def kept(chunk):
        return pltpu.make_async_copy(
            kv.at[span_of(chunk, rows), :],
            window_ref.at[span_of(back * chunks + chunk, rows), :],
            k_local.at[chunk],
        )

    def blank(distance):
        return pltpu.make_async_copy(
            zeros, window_ref.at[span_of(back - distance, count), :], z_local.at[distance - 1]
        )

    def late(source):
        return jnp.maximum(source, m - 1 - source)

    def latest(mine):
        most = late(mine)
        for source in range(m):
            most = jnp.maximum(most, max(source, m - 1 - source) + jnp.abs(mine - source))
        return most

    def shared(turn, chunk):
        place = raw.at[me, span_of(chunk, rows), :]
        return pltpu.make_async_remote_copy(
            src_ref=place,
            dst_ref=place,
            send_sem=r_send.at[turn - 1, chunk],
            recv_sem=r_recv.at[turn - 1, chunk],
            device_id={"mp": lax.rem(me + turn, m)},
        )

    def taken(turn, chunk):
        place = raw.at[lax.rem(me - turn + m, m), span_of(chunk, rows), :]
        return pltpu.make_async_remote_copy(
            src_ref=place,
            dst_ref=place,
            send_sem=r_send.at[turn - 1, chunk],
            recv_sem=r_recv.at[turn - 1, chunk],
            device_id={"mp": lax.rem(me + turn, m)},
        )

    def project(chunk):
        span = span_of(chunk, rows)
        wide = full[span, :].astype(jnp.float32)
        scale = lax.rsqrt(jnp.mean(wide * wide, axis=-1, keepdims=True) + EPSILON)
        normed = (wide * scale).astype(jnp.bfloat16)
        part_width = w_key.shape[1]
        key = jnp.dot(normed, w_key[...], preferred_element_type=jnp.float32)
        value = jnp.dot(normed, w_value[...], preferred_element_type=jnp.float32)
        raw[me, span, :part_width] = key.astype(raw.dtype)
        raw[me, span, part_width:] = value.astype(raw.dtype)
        for turn in range(1, m):
            shared(turn, chunk).start()
        cosine, sine = cos_ref[span, :], sin_ref[span, :]
        query = jnp.dot(normed, w_query[...], preferred_element_type=jnp.float32)
        for head in range(query.shape[1] // HD):
            there = slice(head * HD, (head + 1) * HD)
            turned = turn_pairs(query[:, there], cosine, sine) * HD ** (-0.5)
            query_ref[span, there] = turned.astype(query_ref.dtype)

    def spread(chunk):
        for turn in range(1, m):
            taken(turn, chunk).wait_recv()
        span = span_of(chunk, rows)
        part_width = w_key.shape[1]
        pieces = [raw[owner, span, :].astype(jnp.float32) for owner in range(m)]
        key = jnp.concatenate([piece[:, :part_width] for piece in pieces], axis=-1)
        value = jnp.concatenate([piece[:, part_width:] for piece in pieces], axis=-1)
        kv[span, :HD] = turn_pairs(key, cos_ref[span, :], sin_ref[span, :]).astype(kv.dtype)
        kv[span, HD:] = value.astype(kv.dtype)
        kept(chunk).start()
        for distance in range(1, back + 1):

            @pl.when(at + distance < n)
            def _(distance=distance):
                ahead(distance, chunk).start()

    zeros[...] = jnp.zeros_like(zeros)
    for distance in range(1, back + 1):

        @pl.when(at < distance)
        def _(distance=distance):
            blank(distance).start()

    fetches[0].wait()
    product(0)
    everywhere = 2 * (m - 1) + 1

    def tick(t):
        scatter.pass_on(t)
        done = t - scatter.late()

        @pl.when(within(done, chunks))
        def _():
            span = span_of(done, rows)
            scatter.arrive(done, base_ref[span, :], total)
            mine = total[...].astype(own_ref.dtype)
            own_ref[span, :] = mine
            full[span, pl.ds(pl.multiple_of(me * cols, cols), cols)] = mine
            gather.begin(done)

        gather.relay(t, late)

        @pl.when(t + 1 < chunks)
        def _():
            product(t + 1)

        joined = t - everywhere

        @pl.when(within(joined, chunks))
        def _():
            spread(joined)

        whole = t - latest(me)

        @pl.when(whole == 0)
        def _():
            fetches[1].wait()
            fetches[2].wait()
            fetches[3].wait()

        @pl.when(within(whole, chunks))
        def _():
            project(whole)

    loop(chunks + everywhere, tick)
    scatter.settle()
    gather.settle()
    for distance in range(1, back + 1):

        @pl.when(at < distance)
        def _(distance=distance):
            blank(distance).wait()

        def turn(chunk, distance=distance):
            @pl.when(at + distance < n)
            def _():
                ahead(distance, chunk).wait_send()

            @pl.when(at >= distance)
            def _():
                ahead(distance, chunk).wait_recv()

        each(chunks, turn)
    each(chunks, lambda chunk: kept(chunk).wait())
    for turn in range(1, m):
        each(chunks, lambda chunk, turn=turn: shared(turn, chunk).wait_send())


def middle(gated, base, w_out, w_query, w_key, w_value, cosine, sine, mark, chunks):
    n, m = lax.axis_size("ctx"), lax.axis_size("mp")
    count, cols = base.shape
    channels, width = w_out.shape
    queries = w_query.shape[1]
    part = w_key.shape[1]
    wide = 2 * m * part
    rows = count // chunks
    back = WINDOW // count
    vmem = pl.BlockSpec(memory_space=pltpu.VMEM)
    hbm = pl.BlockSpec(memory_space=pl.ANY)
    low = jnp.bfloat16
    dma = pltpu.SemaphoreType.DMA
    return pl.pallas_call(
        functools.partial(middle_kernel, n, m, chunks),
        out_shape=(
            jax.ShapeDtypeStruct((count, cols), low),
            jax.ShapeDtypeStruct((count, queries), low),
            jax.ShapeDtypeStruct(((back + 1) * count, wide), low),
        ),
        in_specs=[vmem, vmem, hbm, hbm, hbm, hbm, vmem, vmem],
        out_specs=(vmem, vmem, hbm),
        scratch_shapes=[
            pltpu.VMEM((channels, width), low),
            pltpu.VMEM((width, queries), low),
            pltpu.VMEM((width, part), low),
            pltpu.VMEM((width, part), low),
            pltpu.VMEM((count, width), jnp.float32),
            pltpu.VMEM((rows, cols), jnp.float32),
            pltpu.VMEM((2, m - 1, count, cols), low),
            pltpu.VMEM((count, width), low),
            pltpu.VMEM((m, count, 2 * part), low),
            pltpu.VMEM((count, wide), low),
            pltpu.VMEM((count, wide), low),
            dma((4,)),
            dma((2, m - 1, chunks)),
            dma((2, m - 1, chunks)),
            dma((2, m, chunks)),
            dma((2, m, chunks)),
            dma((m - 1, chunks)),
            dma((m - 1, chunks)),
            dma((back, chunks)),
            dma((back, chunks)),
            dma((chunks,)),
            dma((back,)),
        ],
        compiler_params=pltpu.CompilerParams(
            collective_id=mark, has_side_effects=True, vmem_limit_bytes=VMEM_LIMIT
        ),
    )(gated, base, w_out, w_query, w_key, w_value, cosine, sine)


def last_kernel(
    m, chunks,
    query_ref, window_ref, base_ref, w_out_ref,
    own_ref,
    w_out, part, total, held, loads, s_send, s_recv,
):
    at, me = lax.axis_index("ctx"), lax.axis_index("mp")
    count, cols = base_ref.shape
    rows = count // chunks
    heads = query_ref.shape[1] // HD
    fetch = pltpu.make_async_copy(w_out_ref, w_out, loads.at[0])
    fetch.start()
    meet_line(m)
    line = Line(me, m)
    scatter = Scatter(line, part, held, s_send, s_recv, cols, rows, chunks)
    step = max(rows, 128)
    reach = WINDOW + step

    def attend(chunk):
        span = span_of(chunk, rows)
        first = pl.multiple_of(chunk * rows // step * step, step)
        keys = window_ref[pl.ds(first, reach), :HD]
        values = window_ref[pl.ds(first, reach), HD:]
        row = chunk * rows + lax.broadcasted_iota(jnp.int32, (rows, reach), 0)
        col = first + lax.broadcasted_iota(jnp.int32, (rows, reach), 1)
        distance = row + WINDOW - col
        valid = (distance >= 0) & (distance < WINDOW) & (col >= WINDOW - at * count)
        attended = []
        for head in range(heads):
            scores = lax.dot_general(
                query_ref[span, head * HD : (head + 1) * HD],
                keys,
                (((1,), (1,)), ((), ())),
                preferred_element_type=jnp.float32,
            )
            masked = jnp.where(valid, scores, -1e30)
            top = jnp.max(masked, axis=-1, keepdims=True)
            weights = jnp.exp(masked - top)
            share = 1.0 / jnp.sum(weights, axis=-1, keepdims=True)
            probs = (weights * share).astype(jnp.bfloat16)
            attended.append(
                jnp.dot(probs, values, preferred_element_type=jnp.float32).astype(jnp.bfloat16)
            )
        taken = jnp.concatenate(attended, axis=-1)
        for owner in range(m):
            there = slice(owner * cols, (owner + 1) * cols)
            part[span, there] = jnp.dot(
                taken, w_out[:, there], preferred_element_type=jnp.float32
            )

    fetch.wait()
    attend(0)

    def tick(t):
        scatter.pass_on(t)
        done = t - scatter.late()

        @pl.when(within(done, chunks))
        def _():
            span = span_of(done, rows)
            scatter.arrive(done, base_ref[span, :], total)
            own_ref[span, :] = total[...].astype(own_ref.dtype)

        @pl.when(t + 1 < chunks)
        def _():
            attend(t + 1)

    loop(chunks + m - 1, tick)
    scatter.settle()


def last(query, window, base, w_out, mark, chunks):
    m = lax.axis_size("mp")
    count, cols = base.shape
    channels, width = w_out.shape
    rows = count // chunks
    vmem = pl.BlockSpec(memory_space=pltpu.VMEM)
    hbm = pl.BlockSpec(memory_space=pl.ANY)
    low = jnp.bfloat16
    dma = pltpu.SemaphoreType.DMA
    return pl.pallas_call(
        functools.partial(last_kernel, m, chunks),
        out_shape=jax.ShapeDtypeStruct((count, cols), low),
        in_specs=[vmem, vmem, vmem, hbm],
        out_specs=vmem,
        scratch_shapes=[
            pltpu.VMEM((channels, width), low),
            pltpu.VMEM((count, width), jnp.float32),
            pltpu.VMEM((rows, cols), jnp.float32),
            pltpu.VMEM((2, m - 1, count, cols), low),
            dma((1,)),
            dma((2, m - 1, chunks)),
            dma((2, m - 1, chunks)),
        ],
        compiler_params=pltpu.CompilerParams(
            collective_id=mark, has_side_effects=True, vmem_limit_bytes=VMEM_LIMIT
        ),
    )(query, window, base, w_out)


def turns(positions):
    turned = HD // 2
    half = turned // 2
    freqs = 10000.0 ** (-jnp.arange(half, dtype=jnp.float32) * 2.0 / turned)
    angles = positions.astype(jnp.float32)[:, None] * freqs[None, :]
    cosine, sine = jnp.cos(angles), jnp.sin(angles)
    return (
        jnp.concatenate([cosine, cosine], axis=-1),
        jnp.concatenate([-sine, sine], axis=-1),
    )


def on_device(
    tokens,
    w_branch,
    w_input,
    conv_kernel,
    w_rate,
    w_admit,
    lam,
    w_out,
    w_query,
    w_key,
    w_value,
    w_attn_out,
):
    batch, rows_dev, cols_dev = tokens.shape
    count = batch * rows_dev
    width = w_branch.shape[0]
    tokens_flat = tokens.reshape(count, cols_dev)
    full = gather(tokens_flat, 1)
    normed = normalize(full).astype(jnp.bfloat16).reshape(count, width)
    branch = jax.nn.gelu(jnp.dot(normed, w_branch, preferred_element_type=jnp.float32))
    inner = jnp.dot(normed, w_input, preferred_element_type=jnp.float32).reshape(
        batch, rows_dev, -1
    )
    taps = conv_kernel.shape[0]
    rim = from_behind(inner[:, rows_dev - taps + 1 :, :], "ctx", 1)
    extended = jnp.concatenate([rim, inner], axis=1)
    convolved = jnp.zeros_like(inner)
    for tap in range(taps):
        convolved = (
            convolved
            + conv_kernel[tap] * extended[:, taps - 1 - tap : taps - 1 - tap + rows_dev, :]
        )
    blocks = w_rate.shape[0]
    block_width = w_rate.shape[1]
    low = convolved.astype(jnp.bfloat16).reshape(count, -1)

    def gate(weights):
        products = [
            jnp.dot(
                low[:, block * block_width : (block + 1) * block_width],
                weights[block],
                preferred_element_type=jnp.float32,
            )
            for block in range(blocks)
        ]
        return jax.nn.sigmoid(jnp.concatenate(products, axis=-1)).reshape(batch, rows_dev, -1)

    rate_gate = gate(w_rate)
    admit_gate = gate(w_admit)
    log_decay = -8.0 * rate_gate * jax.nn.softplus(-lam)
    decay = jnp.exp(log_decay)
    scaled = admit_gate * convolved * jnp.sqrt(-jnp.expm1(2.0 * log_decay))
    channels = decay.shape[-1]
    gated = recurrence(
        decay.reshape(count, channels), scaled.reshape(count, channels), branch
    )
    base = lax.axis_index("ctx") * rows_dev
    positions = base + jnp.arange(rows_dev, dtype=jnp.int32)
    cosine, sine = turns(positions)
    resid, query, window = middle(
        gated, tokens_flat, w_out, w_query, w_key, w_value, cosine, sine, 2, CHUNKS_MIDDLE
    )
    result = last(query, window, resid, w_attn_out, 3, CHUNKS_LAST)
    return result.reshape(batch, rows_dev, cols_dev)


def solution(mesh):
    in_specs = (
        P(None, "ctx", "mp"),
        P(None, "mp"),
        P(None, "mp"),
        P(None, "mp"),
        P("mp", None, None),
        P("mp", None, None),
        P("mp"),
        P("mp", None),
        P(None, "mp"),
        P(None, "mp"),
        P(None, "mp"),
        P("mp", None),
    )
    out_specs = P(None, "ctx", "mp")
    return jax.shard_map(
        on_device, mesh=mesh, in_specs=in_specs, out_specs=out_specs, check_vma=False
    )
```

```python
import functools

import jax
import jax.numpy as jnp
from jax import lax
from jax.experimental import pallas as pl
from jax.experimental.pallas import tpu as pltpu
from jax.sharding import PartitionSpec as P

HD = 256
WINDOW = 2048


EPSILON = 1e-06


CHUNKS = 8
CHUNKS_MIDDLE = 8
CHUNKS_LAST = 8


def each(chunks, body):
    def turn(chunk, _):
        body(chunk)
        return 0

    lax.fori_loop(0, chunks, turn, 0)


def span_of(chunk, rows):
    return pl.ds(pl.multiple_of(chunk * rows, rows), rows)


class Line:
    def __init__(self, me, count, start=0):
        self.me, self.count, self.start = me, count, start

    def steps(self, way):
        return self.me + 1 if way == 0 else self.me - 1

    def has_next(self, way):
        return self.me < self.count - 1 if way == 0 else self.me > 0

    def has_last(self, way):
        return self.me > 0 if way == 0 else self.me < self.count - 1

    def copy(self, way, src, dst, send, recv):
        return pltpu.make_async_remote_copy(
            src_ref=src,
            dst_ref=dst,
            send_sem=send,
            recv_sem=recv,
            device_id={"mp": self.start + self.steps(way)},
        )


VMEM_LIMIT = 56 * 1024 * 1024


def meet(n, m):
    at, me = lax.axis_index("ctx"), lax.axis_index("mp")
    barrier = pltpu.get_barrier_semaphore()
    for step in range(1, n):
        pl.semaphore_signal(barrier, inc=1, device_id={"ctx": lax.rem(at + step, n)})
    for step in range(1, m):
        pl.semaphore_signal(barrier, inc=1, device_id={"mp": lax.rem(me + step, m)})
    pl.semaphore_wait(barrier, n + m - 2)


def meet_line(m):
    me = lax.axis_index("mp")
    barrier = pltpu.get_barrier_semaphore()
    for step in range(1, m):
        pl.semaphore_signal(barrier, inc=1, device_id={"mp": lax.rem(me + step, m)})
    pl.semaphore_wait(barrier, m - 1)


def within(chunk, chunks):
    return jnp.logical_and(chunk >= 0, chunk < chunks)


class Scatter:
    def __init__(self, line, part, held, send, recv, cols, rows, chunks):
        self.line, self.part, self.held = line, part, held
        self.send, self.recv = send, recv
        self.cols, self.rows, self.chunks = cols, rows, chunks

    def goal(self, way, step):
        return self.line.count - 1 - step if way == 0 else step

    def beyond(self, way, step):
        goal = self.goal(way, step)
        return goal > self.line.me if way == 0 else goal < self.line.me

    def hop(self, way):
        return self.line.me if way == 0 else self.line.count - 1 - self.line.me

    def late(self):
        return jnp.maximum(self.hop(0), self.hop(1))

    def moved(self, way, step, chunk, towards):
        place = self.held.at[way, step, span_of(chunk, self.rows), :]
        return self.line.copy(
            towards, place, place, self.send.at[way, step, chunk], self.recv.at[way, step, chunk]
        )

    def term(self, owner, chunk):
        at = pl.ds(pl.multiple_of(owner * self.cols, self.cols), self.cols)
        return self.part[span_of(chunk, self.rows), at]

    def pass_on(self, tick):
        line, held = self.line, self.held
        for way in (0, 1):
            chunk = tick - self.hop(way)
            at = span_of(chunk, self.rows)
            for step in range(line.count - 1):

                @pl.when(jnp.logical_and(within(chunk, self.chunks), self.beyond(way, step)))
                def _(way=way, step=step, chunk=chunk, at=at):
                    own = self.term(self.goal(way, step), chunk)

                    @pl.when(line.has_last(way))
                    def _():
                        self.moved(way, step, chunk, 1 - way).wait_recv()
                        total = held[way, step, at, :].astype(jnp.float32) + own
                        held[way, step, at, :] = total.astype(held.dtype)

                    @pl.when(jnp.logical_not(line.has_last(way)))
                    def _():
                        held[way, step, at, :] = own.astype(held.dtype)

                    self.moved(way, step, chunk, way).start()

    def arrive(self, chunk, base, total):
        line = self.line
        total[...] = base.astype(jnp.float32) + self.term(line.me, chunk)
        for way in (0, 1):
            step = line.count - 1 - line.me if way == 0 else line.me

            @pl.when(line.has_last(way))
            def _(way=way, step=step):
                self.moved(way, step, chunk, 1 - way).wait_recv()
                total[...] += self.held[way, step, span_of(chunk, self.rows), :].astype(
                    jnp.float32
                )

    def settle(self):
        for step in range(self.line.count - 1):

            def turn(chunk, step=step):
                for way in (0, 1):

                    @pl.when(self.beyond(way, step))
                    def _(way=way):
                        self.moved(way, step, chunk, way).wait_send()

            each(self.chunks, turn)


class Gather:
    def __init__(self, line, full, send, recv, cols, rows, chunks, own=None, shift=0):
        self.line, self.full, self.own, self.shift = line, full, own, shift
        self.send, self.recv = send, recv
        self.cols, self.rows, self.chunks = cols, rows, chunks

    def place(self, owner, chunk):
        at = pl.ds(pl.multiple_of(owner * self.cols, self.cols), self.cols)
        return self.full.at[self.span(chunk), at]

    def span(self, chunk):
        return span_of(lax.rem(chunk + self.shift, self.chunks), self.rows)

    def source(self, way, step):
        return self.line.me - step if way == 0 else self.line.me + step

    def there(self, way, step):
        source = self.source(way, step)
        return source >= 0 if way == 0 else source < self.line.count

    def moved(self, way, step, source, chunk, towards):
        place = self.place(source, chunk)
        return self.line.copy(
            towards, place, place, self.send.at[way, step, chunk], self.recv.at[way, step, chunk]
        )

    def begin(self, chunk):
        for way in (0, 1):

            @pl.when(self.line.has_next(way))
            def _(way=way):
                place = self.place(self.line.me, chunk)
                src = place if self.own is None else self.own.at[self.span(chunk), :]
                self.line.copy(
                    way, src, place, self.send.at[way, 0, chunk], self.recv.at[way, 0, chunk]
                ).start()

    def relay(self, tick, late):
        for step in range(1, self.line.count):
            for way in (0, 1):
                source = self.source(way, step)
                chunk = tick - late(source) - step

                @pl.when(jnp.logical_and(within(chunk, self.chunks), self.there(way, step)))
                def _(way=way, step=step, source=source, chunk=chunk):
                    self.moved(way, step - 1, source, chunk, 1 - way).wait_recv()

                    @pl.when(self.line.has_next(way))
                    def _():
                        self.moved(way, step, source, chunk, way).start()

    def settle(self):
        for step in range(self.line.count):

            def turn(chunk, step=step):
                for way in (0, 1):

                    @pl.when(jnp.logical_and(self.there(way, step), self.line.has_next(way)))
                    def _(way=way):
                        self.moved(way, step, self.source(way, step), chunk, way).wait_send()

            each(self.chunks, turn)


def loop(count, body):
    def turn(index, _):
        body(index)
        return 0

    lax.fori_loop(0, count, turn, 0)


def turn_pairs(values, cosine, sine):
    turned = cosine.shape[-1]
    head = values[:, :turned]
    head = head * cosine + pltpu.roll(head, turned // 2, 1) * sine
    return jnp.concatenate([head, values[:, turned:]], axis=-1)


class Lend:
    def __init__(self, own, far, axis, n, m, send, recv):
        self.own, self.far, self.axis, self.n = own, far, axis, n
        self.at, me = lax.axis_index("ctx"), lax.axis_index("mp")
        self.buddy = self.at + 1 - 2 * lax.rem(self.at, 2)
        self.other = lax.rem(me + m // 2, m)
        self.send, self.recv = send, recv

    def piece(self, ref, owner):
        size = ref.shape[self.axis] // self.n
        span = pl.ds(pl.multiple_of(owner * size, size), size)
        return ref.at[span, :] if self.axis == 0 else ref.at[:, span]

    def copy(self, src, dst, index, device):
        return pltpu.make_async_remote_copy(
            src_ref=src,
            dst_ref=dst,
            send_sem=self.send.at[index],
            recv_sem=self.recv.at[index],
            device_id=device,
        )

    def cross(self):
        return self.copy(
            self.piece(self.own, self.at), self.piece(self.far, self.at), 0, {"mp": self.other}
        )

    def plane(self, k, back):
        place = self.piece(self.far, lax.rem(self.at - 2 * k * back + self.n, self.n))
        return self.copy(place, place, k, {"ctx": lax.rem(self.at + 2 * k, self.n)})

    def core(self, k, back):
        mine = self.buddy if back else self.at
        place = self.piece(self.far, lax.rem(mine - 2 * k + self.n, self.n))
        return self.copy(place, place, self.n // 2 + k, {"ctx": self.buddy})

    def start(self):
        self.cross().start()

    def spread(self):
        self.cross().wait_recv()
        for k in range(1, self.n // 2):
            self.plane(k, 0).start()
        self.core(0, 0).start()

    def share(self):
        for k in range(1, self.n // 2):
            self.plane(k, 1).wait_recv()
            self.core(k, 0).start()

    def end(self):
        for k in range(self.n // 2):
            self.core(k, 1).wait_recv()
        self.cross().wait_send()
        for k in range(1, self.n // 2):
            self.plane(k, 0).wait_send()
        for k in range(self.n // 2):
            self.core(k, 0).wait_send()


def shortfall(x):
    series = jnp.ones_like(x)
    for term in range(12, 1, -1):
        series = 1.0 + series * x * (1.0 / term)
    return jnp.where(x > -1.0, -x * series, 1.0 - jnp.exp(x))


def first_kernel(
    n, m, chunks,
    own_ref, w_branch_ref, w_input_ref, taps_ref, w_rate_ref, w_admit_ref, soft_ref,
    w_out_ref, w_query_ref, w_kv_ref,
    gated_ref, share_ref, w_out_far_ref, w_query_far_ref, w_kv_far_ref,
    w_branch, w_input, full, inner, branch, decay, scaled, state, product, edge, got,
    loads, send, recv, local, l_send, l_recv, e_send, e_recv, b_send, b_recv,
):
    at, me = lax.axis_index("ctx"), lax.axis_index("mp")
    h = m // 2
    count, cols = own_ref.shape
    rows = count // chunks
    few = count // 2
    width = branch.shape[1]
    pad = 8
    fetches = [
        pltpu.make_async_copy(w_input_ref, w_input, loads.at[0]),
        pltpu.make_async_copy(w_branch_ref, w_branch, loads.at[1]),
    ]
    for fetch in fetches:
        fetch.start()
    meet(n, m)
    line = Line(me, m)
    gather = Gather(line, full, send, recv, cols, rows, chunks, own_ref, chunks - 1)
    outward, query, pair = [
        Lend(own, far, axis, n, m, l_send.at[index], l_recv.at[index])
        for index, (own, far, axis) in enumerate(
            [
                (w_out_ref, w_out_far_ref, 1),
                (w_query_ref, w_query_far_ref, 0),
                (w_kv_ref, w_kv_far_ref, 0),
            ]
        )
    ]
    outward.start()
    pair.start()
    query.start()
    each(chunks, gather.begin)
    mine = full.at[:, pl.ds(pl.multiple_of(me * cols, cols), cols)]
    kept = pltpu.make_async_copy(own_ref, mine, local.at[0])
    kept.start()

    def border():
        return pltpu.make_async_remote_copy(
            src_ref=inner.at[pl.ds(count, pad), :],
            dst_ref=inner.at[pl.ds(0, pad), :],
            send_sem=b_send.at[0],
            recv_sem=b_recv.at[0],
            device_id={"ctx": lax.rem(at + 1, n)},
        )

    def project(chunk):
        span = span_of(chunk, rows)
        wide = full[span, :].astype(jnp.float32)
        scale = lax.rsqrt(jnp.mean(wide * wide, axis=-1, keepdims=True) + EPSILON)
        normed = (wide * scale).astype(jnp.bfloat16)
        inner[pl.ds(pl.multiple_of(chunk * rows + pad, pad), rows), :] = jnp.dot(
            normed, w_input[...], preferred_element_type=jnp.float32
        )
        branch[span, :] = jax.nn.gelu(
            jnp.dot(normed, w_branch[...], preferred_element_type=jnp.float32)
        )

    tile = 8
    place = lax.broadcasted_iota(jnp.int32, (tile, width), 0)

    def mix(chunk):
        span = span_of(chunk, rows)
        seen = inner[pl.ds(pl.multiple_of(chunk * rows, rows), rows + pad), :]
        convolved = jnp.zeros((rows, width), jnp.float32)
        for tap in range(taps_ref.shape[0]):
            convolved = convolved + taps_ref[tap : tap + 1, :] * seen[pad - tap : pad - tap + rows]
        low = convolved.astype(jnp.bfloat16)
        each_block = w_rate_ref.shape[1]

        def gate(weights):
            return jax.nn.sigmoid(
                jnp.concatenate(
                    [
                        jnp.dot(
                            low[:, index * each_block : (index + 1) * each_block],
                            weights[index],
                            preferred_element_type=jnp.float32,
                        )
                        for index in range(weights.shape[0])
                    ],
                    axis=-1,
                )
            )

        log_decay = -8.0 * gate(w_rate_ref) * soft_ref[...]
        decay[...] = jnp.exp(log_decay)
        scaled[...] = gate(w_admit_ref) * convolved * jnp.sqrt(shortfall(2.0 * log_decay))

        def advance(index, carried):
            last_state, last_product = carried
            here = pl.ds(pl.multiple_of(index * tile, tile), tile)
            there = pl.ds(pl.multiple_of(chunk * rows + index * tile, tile), tile)
            a = decay[here, :]
            b = scaled[here, :]
            for shift in (1, 2, 4):
                inside = place >= shift
                a_back = jnp.where(inside, pltpu.roll(a, shift, 0), 1.0)
                b_back = jnp.where(inside, pltpu.roll(b, shift, 0), 0.0)
                b = a * b_back + b
                a = a * a_back
            b = b + a * last_state
            a = a * last_product
            state[there, :] = b
            product[there, :] = a
            return b[tile - 1 :, :], a[tile - 1 :, :]

        ends = lax.fori_loop(
            0, rows // tile, advance, (edge[0:1, :], edge[1:2, :]), unroll=True
        )
        edge[0:1, :] = ends[0]
        edge[1:2, :] = ends[1]

    edge[0:1, :] = jnp.zeros((1, width), jnp.float32)
    edge[1:2, :] = jnp.ones((1, width), jnp.float32)
    latest = jnp.maximum(me, m - 1 - me)

    def tick(t):
        gather.relay(t, lambda source: 0)

        @pl.when(t == 1)
        def _():
            outward.spread()
            pair.spread()

        @pl.when(t == 3)
        def _():
            query.spread()

        @pl.when(t == chunks)
        def _():
            outward.share()
            pair.share()

        whole = t - latest

        @pl.when(whole == 0)
        def _():
            kept.wait()
            for fetch in fetches:
                fetch.wait()
            project(chunks - 1)

            @pl.when(at + 1 < n)
            def _():
                border().start()

            @pl.when(at == 0)
            def _():
                inner[0:pad, :] = jnp.zeros((pad, width), jnp.float32)

        @pl.when(jnp.logical_and(whole > 0, whole < chunks))
        def _():
            project(whole - 1)

            @pl.when(jnp.logical_and(whole == 1, at > 0))
            def _():
                border().wait_recv()

            mix(whole - 1)

    loop(chunks + m - 1, tick)
    mix(chunks - 1)
    copies = []
    for step in range(1, n):
        copy = pltpu.make_async_remote_copy(
            src_ref=edge,
            dst_ref=got.at[step],
            send_sem=e_send.at[step],
            recv_sem=e_recv.at[step],
            device_id={"ctx": lax.rem(at + step, n)},
        )
        copy.start()
        copies.append(copy)
    half, rank = me // h, lax.rem(me, h)
    shares = [
        pltpu.make_async_copy(
            full.at[
                pl.ds(pl.multiple_of(half * few, few), few),
                pl.ds(pl.multiple_of((rank + side * h) * cols, cols), cols),
            ],
            share_ref.at[:, side * cols : (side + 1) * cols],
            local.at[1 + side],
        )
        for side in (0, 1)
    ]
    for copy in shares:
        copy.start()
    for copy in copies:
        copy.wait()
    carry = jnp.zeros((1, width), jnp.float32)
    for step in range(n - 1, 0, -1):
        fresh = got[step, 0:1, :] + got[step, 1:2, :] * carry
        carry = jnp.where(at >= step, fresh, 0.0)

    def finish(index, _):
        span = span_of(index, 16)
        whole = state[span, :] + product[span, :] * carry
        gated_ref[span, :] = (whole * branch[span, :]).astype(gated_ref.dtype)
        return 0

    lax.fori_loop(0, count // 16, finish, 0, unroll=4)
    query.share()
    gather.settle()
    for lend in (outward, pair, query):
        lend.end()

    @pl.when(at + 1 < n)
    def _():
        border().wait_send()

    for copy in shares:
        copy.wait()


def first(own, w_branch, w_input, taps, w_rate, w_admit, soft, w_out, w_query, w_kv, mark, chunks):
    n, m = lax.axis_size("ctx"), lax.axis_size("mp")
    count, cols = own.shape
    full_width, width = w_branch.shape
    rows = count // chunks
    vmem = pl.BlockSpec(memory_space=pltpu.VMEM)
    hbm = pl.BlockSpec(memory_space=pl.ANY)
    dma = pltpu.SemaphoreType.DMA
    wide = jnp.float32
    like = lambda x: jax.ShapeDtypeStruct(x.shape, x.dtype)
    return pl.pallas_call(
        functools.partial(first_kernel, n, m, chunks),
        out_shape=(
            jax.ShapeDtypeStruct((count, width), own.dtype),
            jax.ShapeDtypeStruct((count // 2, 2 * cols), own.dtype),
            like(w_out),
            like(w_query),
            like(w_kv),
        ),
        in_specs=[vmem, hbm, hbm, vmem, vmem, vmem, vmem, hbm, hbm, hbm],
        out_specs=(vmem,) + (hbm,) * 4,
        scratch_shapes=[
            pltpu.VMEM((full_width, width), w_branch.dtype),
            pltpu.VMEM((full_width, width), w_input.dtype),
            pltpu.VMEM((count, full_width), own.dtype),
            pltpu.VMEM((count + 8, width), wide),
            pltpu.VMEM((count, width), wide),
            pltpu.VMEM((rows, width), wide),
            pltpu.VMEM((rows, width), wide),
            pltpu.VMEM((count, width), wide),
            pltpu.VMEM((count, width), wide),
            pltpu.VMEM((2, width), wide),
            pltpu.VMEM((n, 2, width), wide),
            dma((2,)),
            dma((2, m, chunks)),
            dma((2, m, chunks)),
            dma((3,)),
            dma((3, n)),
            dma((3, n)),
            dma((n,)),
            dma((n,)),
            dma((1,)),
            dma((1,)),
        ],
        compiler_params=pltpu.CompilerParams(
            collective_id=mark, has_side_effects=True, vmem_limit_bytes=VMEM_LIMIT
        ),
    )(own, w_branch, w_input, taps, w_rate, w_admit, soft, w_out, w_query, w_kv)


def place_of(block, h):
    return block % h * 2 + block // h


def middle_kernel(
    n, m, chunks,
    gated_ref, base_ref, w_out_ref, w_out_far_ref, w_query_ref, w_query_far_ref,
    w_kv_ref, w_kv_far_ref, w_attn_ref, cos_ref, sin_ref,
    own_ref, query_ref, window_ref, w_attn_far_ref,
    w_out, w_query, w_kv, got, part, total, held, full, raw, kv, zeros,
    loads, h_send, h_recv, s_send, s_recv, g_send, g_recv, r_send, r_recv,
    k_send, k_recv, k_local, z_local, l_send, l_recv,
):
    at, me = lax.axis_index("ctx"), lax.axis_index("mp")
    h = m // 2
    half, local = me // h, lax.rem(me, h)
    far = lax.rem(me + h, m)
    count = gated_ref.shape[0]
    cols = base_ref.shape[1]
    block = cols // 2
    rows = base_ref.shape[0] // chunks
    queries = w_query_ref.shape[1]
    back = window_ref.shape[0] // count - 1

    def fetches(kind):
        for side in (0, 1):
            for index in range(m):
                rank = side * m + index
                here = slice(index * block, (index + 1) * block)
                put = place_of(index, h)
                there = slice(put * block, (put + 1) * block)
                if kind == 0:
                    src = (w_out_ref, w_out_far_ref)[side].at[:, here]
                    dst = w_out.at[side, :, there]
                elif kind == 1:
                    src = (w_query_ref, w_query_far_ref)[side].at[here, :]
                    dst = w_query.at[there, side * queries : (side + 1) * queries]
                else:
                    src = (w_kv_ref, w_kv_far_ref)[side].at[here, :]
                    dst = w_kv.at[side, there, :]
                yield pltpu.make_async_copy(src, dst, loads.at[kind, rank])

    for kind in range(3):
        for fetch in fetches(kind):
            fetch.start()
    meet(n, m)
    line = Line(local, h, half * h)
    scatter = Scatter(line, part, held, s_send, s_recv, cols, rows, chunks)
    gather = Gather(line, full, g_send, g_recv, cols, rows, chunks)

    def handed(chunk):
        return pltpu.make_async_remote_copy(
            src_ref=gated_ref.at[span_of((1 - half) * chunks + chunk, rows), :],
            dst_ref=got.at[span_of(chunk, rows), :],
            send_sem=h_send.at[chunk],
            recv_sem=h_recv.at[chunk],
            device_id={"mp": far},
        )

    def product(chunk):
        handed(chunk).wait_recv()
        near = gated_ref[span_of(half * chunks + chunk, rows), :]
        other = got[span_of(chunk, rows), :]
        for index in range(m):
            there = slice(index * block, (index + 1) * block)
            part[span_of(chunk, rows), there] = jnp.dot(
                near, w_out[0, :, there], preferred_element_type=jnp.float32
            ) + jnp.dot(other, w_out[1, :, there], preferred_element_type=jnp.float32)

    odd = lax.rem(at, 2)
    buddy = at + 1 - 2 * odd

    def slot(distance, chunk):
        return window_ref.at[span_of((back - distance) * 2 * chunks + chunk, rows), :]

    def ahead(distance, chunk):
        return pltpu.make_async_remote_copy(
            src_ref=kv.at[span_of(chunk, rows), :],
            dst_ref=slot(distance, chunk),
            send_sem=k_send.at[distance - 1, chunk],
            recv_sem=k_recv.at[distance - 1, chunk],
            device_id={"ctx": lax.rem(at + distance, n)},
        )

    def relayed(distance, chunk):
        other = distance + 1 - 2 * odd
        return pltpu.make_async_remote_copy(
            src_ref=slot(distance, chunk),
            dst_ref=slot(other, chunk),
            send_sem=k_send.at[other - 1, chunk],
            recv_sem=k_recv.at[other - 1, chunk],
            device_id={"ctx": buddy},
        )

    def relays(distance):
        wanted = jnp.logical_or(odd == 1, distance + 1 <= back)
        return jnp.logical_and(at >= distance, wanted)

    def kept(chunk):
        return pltpu.make_async_copy(
            kv.at[span_of(chunk, rows), :],
            window_ref.at[span_of(back * 2 * chunks + chunk, rows), :],
            k_local.at[chunk],
        )

    def blank(distance):
        return pltpu.make_async_copy(
            zeros, window_ref.at[span_of(back - distance, count), :], z_local.at[distance - 1]
        )

    def late(source):
        return jnp.maximum(source, h - 1 - source)

    def latest(mine):
        most = late(mine)
        for source in range(h):
            most = jnp.maximum(most, max(source, h - 1 - source) + jnp.abs(mine - source))
        return most

    def passed(turn, side, chunk, sender):
        owner = lax.rem(sender + side * h, m)
        place = raw.at[owner, span_of(sender // h * chunks + chunk, rows), :]
        return pltpu.make_async_remote_copy(
            src_ref=place,
            dst_ref=place,
            send_sem=r_send.at[turn - 1, side, chunk],
            recv_sem=r_recv.at[turn - 1, side, chunk],
            device_id={"mp": lax.rem(me + turn, m)},
        )

    def project(chunk):
        span = span_of(chunk, rows)
        whole_span = span_of(half * chunks + chunk, rows)
        wide = full[span, :].astype(jnp.float32)
        scale = lax.rsqrt(jnp.mean(wide * wide, axis=-1, keepdims=True) + EPSILON)
        normed = (wide * scale).astype(jnp.bfloat16)
        for side, owner in ((0, me), (1, far)):
            both = jnp.dot(normed, w_kv[side], preferred_element_type=jnp.float32)
            raw[owner, whole_span, :] = both.astype(raw.dtype)
        for turn in range(1, m):
            for side in (0, 1):
                passed(turn, side, chunk, me).start()
        cosine, sine = cos_ref[whole_span, :], sin_ref[whole_span, :]
        query = jnp.dot(normed, w_query[...], preferred_element_type=jnp.float32)
        for head in range(query.shape[1] // HD):
            there = slice(head * HD, (head + 1) * HD)
            turned = turn_pairs(query[:, there], cosine, sine) * HD ** (-0.5)
            query_ref[span, there] = turned.astype(query_ref.dtype)

    def spread(chunk):
        for turn in range(1, m):
            for side in (0, 1):
                passed(turn, side, chunk, lax.rem(me - turn + m, m)).wait_recv()
        part_width = raw.shape[2] // 2
        for portion in (0, 1):
            index = portion * chunks + chunk
            span = span_of(index, rows)
            pieces = [raw[owner, span, :].astype(jnp.float32) for owner in range(m)]
            key = jnp.concatenate([piece[:, :part_width] for piece in pieces], axis=-1)
            value = jnp.concatenate([piece[:, part_width:] for piece in pieces], axis=-1)
            kv[span, :HD] = turn_pairs(key, cos_ref[span, :], sin_ref[span, :]).astype(kv.dtype)
            kv[span, HD:] = value.astype(kv.dtype)
            kept(index).start()
            for distance in range(2, back + 1, 2):

                @pl.when(at + distance < n)
                def _(distance=distance, index=index):
                    ahead(distance, index).start()

            @pl.when(odd == 0)
            def _(index=index):
                ahead(1, index).start()

    each(chunks, lambda chunk: handed(chunk).start())
    lend = Lend(w_attn_ref, w_attn_far_ref, 1, n, m, l_send, l_recv)
    lend.start()
    zeros[...] = jnp.zeros_like(zeros)
    for distance in range(1, back + 1):

        @pl.when(at < distance)
        def _(distance=distance):
            blank(distance).start()

    for fetch in fetches(0):
        fetch.wait()
    product(0)
    everywhere = 2 * (h - 1) + 1

    def tick(t):
        scatter.pass_on(t)
        done = t - scatter.late()

        @pl.when(within(done, chunks))
        def _():
            span = span_of(done, rows)
            scatter.arrive(done, base_ref[span, :], total)
            mine = total[...].astype(own_ref.dtype)
            own_ref[span, :] = mine
            full[span, pl.ds(pl.multiple_of(local * cols, cols), cols)] = mine
            gather.begin(done)

        gather.relay(t, late)

        @pl.when(t + 1 < chunks)
        def _():
            product(t + 1)

        joined = t - everywhere

        @pl.when(within(joined, chunks))
        def _():
            spread(joined)

        whole = t - latest(local)

        @pl.when(whole == 0)
        def _():
            for kind in (1, 2):
                for fetch in fetches(kind):
                    fetch.wait()

        @pl.when(within(whole, chunks))
        def _():
            project(whole)

        @pl.when(t == 2)
        def _():
            lend.spread()

        @pl.when(t == chunks)
        def _():
            lend.share()

    loop(chunks + everywhere, tick)
    each(chunks, lambda chunk: handed(chunk).wait_send())
    lend.end()
    scatter.settle()
    gather.settle()
    for distance in range(1, back + 1):

        @pl.when(at < distance)
        def _(distance=distance):
            blank(distance).wait()

    def pass_over(chunk):
        for distance in range(2, back + 1, 2):

            @pl.when(at >= distance)
            def _(distance=distance):
                ahead(distance, chunk).wait_recv()

            @pl.when(relays(distance))
            def _(distance=distance):
                relayed(distance, chunk).start()

    each(2 * chunks, pass_over)

    def end(chunk):
        for distance in range(1, back + 1, 2):

            @pl.when(at >= distance)
            def _(distance=distance):
                ahead(distance, chunk).wait_recv()

        for distance in range(2, back + 1, 2):

            @pl.when(at + distance < n)
            def _(distance=distance):
                ahead(distance, chunk).wait_send()

            @pl.when(relays(distance))
            def _(distance=distance):
                relayed(distance, chunk).wait_send()

        @pl.when(odd == 0)
        def _():
            ahead(1, chunk).wait_send()

    each(2 * chunks, end)
    each(2 * chunks, lambda chunk: kept(chunk).wait())
    for turn in range(1, m):
        for side in (0, 1):
            each(
                chunks,
                lambda chunk, turn=turn, side=side: passed(turn, side, chunk, me).wait_send(),
            )


def middle(gated, base, w_out, w_query, w_kv, w_attn, cosine, sine, mark, chunks):
    n, m = lax.axis_size("ctx"), lax.axis_size("mp")
    h = m // 2
    count, channels = gated.shape
    few, cols = base.shape
    width = w_out[0].shape[1]
    queries = w_query[0].shape[1]
    part = w_kv[0].shape[1]
    wide = m * part
    rows = few // chunks
    back = WINDOW // count
    vmem = pl.BlockSpec(memory_space=pltpu.VMEM)
    hbm = pl.BlockSpec(memory_space=pl.ANY)
    low = jnp.bfloat16
    dma = pltpu.SemaphoreType.DMA
    return pl.pallas_call(
        functools.partial(middle_kernel, n, m, chunks),
        out_shape=(
            jax.ShapeDtypeStruct((few, cols), low),
            jax.ShapeDtypeStruct((few, 2 * queries), low),
            jax.ShapeDtypeStruct(((back + 1) * count, wide), low),
            jax.ShapeDtypeStruct(w_attn.shape, low),
        ),
        in_specs=[vmem, vmem] + [hbm] * 7 + [vmem, vmem],
        out_specs=(vmem, vmem, hbm, hbm),
        scratch_shapes=[
            pltpu.VMEM((2, channels, width), low),
            pltpu.VMEM((width, 2 * queries), low),
            pltpu.VMEM((2, width, part), low),
            pltpu.VMEM((few, channels), low),
            pltpu.VMEM((few, width), jnp.float32),
            pltpu.VMEM((rows, cols), jnp.float32),
            pltpu.VMEM((2, h - 1, few, cols), low),
            pltpu.VMEM((few, width), low),
            pltpu.VMEM((m, count, part), low),
            pltpu.VMEM((count, wide), low),
            pltpu.VMEM((count, wide), low),
            dma((3, 2 * m)),
            dma((chunks,)),
            dma((chunks,)),
            dma((2, h - 1, chunks)),
            dma((2, h - 1, chunks)),
            dma((2, h, chunks)),
            dma((2, h, chunks)),
            dma((m - 1, 2, chunks)),
            dma((m - 1, 2, chunks)),
            dma((back, 2 * chunks)),
            dma((back, 2 * chunks)),
            dma((2 * chunks,)),
            dma((back,)),
            dma((n,)),
            dma((n,)),
        ],
        compiler_params=pltpu.CompilerParams(
            collective_id=mark, has_side_effects=True, vmem_limit_bytes=VMEM_LIMIT
        ),
    )(gated, base, *w_out, *w_query, *w_kv, w_attn, cosine, sine)


def last_kernel(
    m, chunks,
    query_ref, window_ref, base_ref, w_out_ref, w_out_far_ref,
    result_ref,
    w_out, part, total, made, held, loads, s_send, s_recv, o_send, o_recv, o_local,
):
    at, me = lax.axis_index("ctx"), lax.axis_index("mp")
    h = m // 2
    half, local = me // h, lax.rem(me, h)
    far = lax.rem(me + h, m)
    few, cols = base_ref.shape
    count = 2 * few
    block = cols // 2
    channels = w_out_ref.shape[0]
    rows = few // chunks
    heads = query_ref.shape[1] // HD

    def fetches():
        for side in (0, 1):
            for index in range(m):
                put = place_of(index, h)
                yield pltpu.make_async_copy(
                    (w_out_ref, w_out_far_ref)[side].at[
                        :, index * block : (index + 1) * block
                    ],
                    w_out.at[
                        side * channels : (side + 1) * channels,
                        put * block : (put + 1) * block,
                    ],
                    loads.at[side * m + index],
                )

    for fetch in fetches():
        fetch.start()
    meet_line(m)
    line = Line(local, h, half * h)
    scatter = Scatter(line, part, held, s_send, s_recv, cols, rows, chunks)
    step = max(rows, 128)
    reach = WINDOW + step

    def sent(chunk):
        return pltpu.make_async_remote_copy(
            src_ref=made.at[
                span_of(chunk, rows), pl.ds(pl.multiple_of((1 - half) * block, block), block)
            ],
            dst_ref=result_ref.at[span_of(half * chunks + chunk, rows), :],
            send_sem=o_send.at[chunk],
            recv_sem=o_recv.at[chunk],
            device_id={"mp": far},
        )

    def came(chunk):
        place = result_ref.at[span_of((1 - half) * chunks + chunk, rows), :]
        return pltpu.make_async_remote_copy(
            src_ref=place,
            dst_ref=place,
            send_sem=o_send.at[chunk],
            recv_sem=o_recv.at[chunk],
            device_id={"mp": far},
        )

    def kept(chunk):
        return pltpu.make_async_copy(
            made.at[span_of(chunk, rows), pl.ds(pl.multiple_of(half * block, block), block)],
            result_ref.at[span_of(half * chunks + chunk, rows), :],
            o_local.at[chunk],
        )

    def attend(chunk):
        span = span_of(chunk, rows)
        place = half * few + chunk * rows
        first = pl.multiple_of(place // step * step, step)
        keys = window_ref[pl.ds(first, reach), :HD]
        values = window_ref[pl.ds(first, reach), HD:]
        row = place + lax.broadcasted_iota(jnp.int32, (rows, reach), 0)
        col = first + lax.broadcasted_iota(jnp.int32, (rows, reach), 1)
        distance = row + WINDOW - col
        valid = (distance >= 0) & (distance < WINDOW) & (col >= WINDOW - at * count)
        attended = []
        for head in range(heads):
            scores = lax.dot_general(
                query_ref[span, head * HD : (head + 1) * HD],
                keys,
                (((1,), (1,)), ((), ())),
                preferred_element_type=jnp.float32,
            )
            masked = jnp.where(valid, scores, -1e30)
            top = jnp.max(masked, axis=-1, keepdims=True)
            weights = jnp.exp(masked - top)
            share = 1.0 / jnp.sum(weights, axis=-1, keepdims=True)
            probs = (weights * share).astype(jnp.bfloat16)
            attended.append(
                jnp.dot(probs, values, preferred_element_type=jnp.float32).astype(jnp.bfloat16)
            )
        taken = jnp.concatenate(attended, axis=-1)
        for index in range(m):
            there = slice(index * block, (index + 1) * block)
            part[span, there] = jnp.dot(
                taken, w_out[:, there], preferred_element_type=jnp.float32
            )

    for fetch in fetches():
        fetch.wait()
    attend(0)

    def tick(t):
        scatter.pass_on(t)
        done = t - scatter.late()

        @pl.when(within(done, chunks))
        def _():
            span = span_of(done, rows)
            scatter.arrive(done, base_ref[span, :], total)
            made[span, :] = total[...].astype(made.dtype)
            sent(done).start()
            kept(done).start()

        @pl.when(t + 1 < chunks)
        def _():
            attend(t + 1)

    loop(chunks + h - 1, tick)
    scatter.settle()

    def end(chunk):
        sent(chunk).wait_send()
        came(chunk).wait_recv()
        kept(chunk).wait()

    each(chunks, end)


def last(query, window, base, w_out, mark, chunks):
    m = lax.axis_size("mp")
    h = m // 2
    few, cols = base.shape
    channels, width = w_out[0].shape
    rows = few // chunks
    vmem = pl.BlockSpec(memory_space=pltpu.VMEM)
    hbm = pl.BlockSpec(memory_space=pl.ANY)
    low = jnp.bfloat16
    dma = pltpu.SemaphoreType.DMA
    return pl.pallas_call(
        functools.partial(last_kernel, m, chunks),
        out_shape=jax.ShapeDtypeStruct((2 * few, cols // 2), low),
        in_specs=[vmem, vmem, vmem, hbm, hbm],
        out_specs=hbm,
        scratch_shapes=[
            pltpu.VMEM((2 * channels, width), low),
            pltpu.VMEM((few, width), jnp.float32),
            pltpu.VMEM((rows, cols), jnp.float32),
            pltpu.VMEM((few, cols), low),
            pltpu.VMEM((2, h - 1, few, cols), low),
            dma((2 * m,)),
            dma((2, h - 1, chunks)),
            dma((2, h - 1, chunks)),
            dma((chunks,)),
            dma((chunks,)),
            dma((chunks,)),
        ],
        compiler_params=pltpu.CompilerParams(
            collective_id=mark, has_side_effects=True, vmem_limit_bytes=VMEM_LIMIT
        ),
    )(query, window, base, *w_out)


def turns(positions):
    turned = HD // 2
    half = turned // 2
    freqs = 10000.0 ** (-jnp.arange(half, dtype=jnp.float32) * 2.0 / turned)
    angles = positions.astype(jnp.float32)[:, None] * freqs[None, :]
    cosine, sine = jnp.cos(angles), jnp.sin(angles)
    return (
        jnp.concatenate([cosine, cosine], axis=-1),
        jnp.concatenate([-sine, sine], axis=-1),
    )


def on_device(
    tokens,
    w_branch,
    w_input,
    conv_kernel,
    w_rate,
    w_admit,
    lam,
    w_out,
    w_query,
    w_key,
    w_value,
    w_attn_out,
):
    batch, rows_dev, cols_dev = tokens.shape
    count = batch * rows_dev
    tokens_flat = tokens.reshape(count, cols_dev)
    w_kv = jnp.concatenate([w_key, w_value], axis=1)
    soft = jax.nn.softplus(-lam)[None, :]
    gated, share, w_out_far, w_query_far, w_kv_far = first(
        tokens_flat, w_branch, w_input, conv_kernel, w_rate, w_admit, soft,
        w_out, w_query, w_kv, 1, CHUNKS,
    )
    base = lax.axis_index("ctx") * rows_dev
    positions = base + jnp.arange(rows_dev, dtype=jnp.int32)
    cosine, sine = turns(positions)
    resid, query, window, w_attn_out_far = middle(
        gated, share, (w_out, w_out_far), (w_query, w_query_far), (w_kv, w_kv_far),
        w_attn_out, cosine, sine, 2, CHUNKS_MIDDLE,
    )
    result = last(query, window, resid, (w_attn_out, w_attn_out_far), 3, CHUNKS_LAST)
    return result.reshape(batch, rows_dev, cols_dev)


def solution(mesh):
    in_specs = (
        P(None, "ctx", "mp"),
        P(None, "mp"),
        P(None, "mp"),
        P(None, "mp"),
        P("mp", None, None),
        P("mp", None, None),
        P("mp"),
        P("mp", None),
        P(None, "mp"),
        P(None, "mp"),
        P(None, "mp"),
        P("mp", None),
    )
    out_specs = P(None, "ctx", "mp")
    return jax.shard_map(
        on_device, mesh=mesh, in_specs=in_specs, out_specs=out_specs, check_vma=False
    )
```

```python
import functools

import jax
import jax.numpy as jnp
from jax import lax
from jax.experimental import pallas as pl
from jax.experimental.pallas import tpu as pltpu
from jax.sharding import PartitionSpec as P

HD = 256
WINDOW = 2048


EPSILON = 1e-06


CHUNKS = 8
CHUNKS_MIDDLE = 8
LENT = (-2, 3, 5)
LENT_LATE = (0, 3, 5)
CHUNKS_LAST = 8


def each(chunks, body):
    def turn(chunk, _):
        body(chunk)
        return 0

    lax.fori_loop(0, chunks, turn, 0)


def span_of(chunk, rows):
    return pl.ds(pl.multiple_of(chunk * rows, rows), rows)


class Line:
    def __init__(self, me, count, start=0):
        self.me, self.count, self.start = me, count, start

    def steps(self, way):
        return self.me + 1 if way == 0 else self.me - 1

    def has_next(self, way):
        return self.me < self.count - 1 if way == 0 else self.me > 0

    def has_last(self, way):
        return self.me > 0 if way == 0 else self.me < self.count - 1

    def copy(self, way, src, dst, send, recv):
        return pltpu.make_async_remote_copy(
            src_ref=src,
            dst_ref=dst,
            send_sem=send,
            recv_sem=recv,
            device_id={"mp": self.start + self.steps(way)},
        )


VMEM_LIMIT = 56 * 1024 * 1024


def meet(n, m):
    at, me = lax.axis_index("ctx"), lax.axis_index("mp")
    barrier = pltpu.get_barrier_semaphore()
    for step in range(1, n):
        pl.semaphore_signal(barrier, inc=1, device_id={"ctx": lax.rem(at + step, n)})
    for step in range(1, m):
        pl.semaphore_signal(barrier, inc=1, device_id={"mp": lax.rem(me + step, m)})
    pl.semaphore_wait(barrier, n + m - 2)


def meet_line(m):
    me = lax.axis_index("mp")
    barrier = pltpu.get_barrier_semaphore()
    for step in range(1, m):
        pl.semaphore_signal(barrier, inc=1, device_id={"mp": lax.rem(me + step, m)})
    pl.semaphore_wait(barrier, m - 1)


def within(chunk, chunks):
    return jnp.logical_and(chunk >= 0, chunk < chunks)


class Scatter:
    def __init__(self, line, part, held, send, recv, cols, rows, chunks):
        self.line, self.part, self.held = line, part, held
        self.send, self.recv = send, recv
        self.cols, self.rows, self.chunks = cols, rows, chunks

    def goal(self, way, step):
        return self.line.count - 1 - step if way == 0 else step

    def beyond(self, way, step):
        goal = self.goal(way, step)
        return goal > self.line.me if way == 0 else goal < self.line.me

    def hop(self, way):
        return self.line.me if way == 0 else self.line.count - 1 - self.line.me

    def late(self):
        return jnp.maximum(self.hop(0), self.hop(1))

    def moved(self, way, step, chunk, towards):
        place = self.held.at[way, step, span_of(chunk, self.rows), :]
        return self.line.copy(
            towards, place, place, self.send.at[way, step, chunk], self.recv.at[way, step, chunk]
        )

    def term(self, owner, chunk):
        at = pl.ds(pl.multiple_of(owner * self.cols, self.cols), self.cols)
        return self.part[span_of(chunk, self.rows), at]

    def pass_on(self, tick):
        line, held = self.line, self.held
        for way in (0, 1):
            chunk = tick - self.hop(way)
            at = span_of(chunk, self.rows)
            for step in range(line.count - 1):

                @pl.when(jnp.logical_and(within(chunk, self.chunks), self.beyond(way, step)))
                def _(way=way, step=step, chunk=chunk, at=at):
                    own = self.term(self.goal(way, step), chunk)

                    @pl.when(line.has_last(way))
                    def _():
                        self.moved(way, step, chunk, 1 - way).wait_recv()
                        total = held[way, step, at, :].astype(jnp.float32) + own
                        held[way, step, at, :] = total.astype(held.dtype)

                    @pl.when(jnp.logical_not(line.has_last(way)))
                    def _():
                        held[way, step, at, :] = own.astype(held.dtype)

                    self.moved(way, step, chunk, way).start()

    def arrive(self, chunk, base, total):
        line = self.line
        total[...] = base.astype(jnp.float32) + self.term(line.me, chunk)
        for way in (0, 1):
            step = line.count - 1 - line.me if way == 0 else line.me

            @pl.when(line.has_last(way))
            def _(way=way, step=step):
                self.moved(way, step, chunk, 1 - way).wait_recv()
                total[...] += self.held[way, step, span_of(chunk, self.rows), :].astype(
                    jnp.float32
                )

    def settle(self):
        for step in range(self.line.count - 1):

            def turn(chunk, step=step):
                for way in (0, 1):

                    @pl.when(self.beyond(way, step))
                    def _(way=way):
                        self.moved(way, step, chunk, way).wait_send()

            each(self.chunks, turn)


class Gather:
    def __init__(self, line, full, send, recv, cols, rows, chunks, own=None, shift=0):
        self.line, self.full, self.own, self.shift = line, full, own, shift
        self.send, self.recv = send, recv
        self.cols, self.rows, self.chunks = cols, rows, chunks

    def place(self, owner, chunk):
        at = pl.ds(pl.multiple_of(owner * self.cols, self.cols), self.cols)
        return self.full.at[self.span(chunk), at]

    def span(self, chunk):
        return span_of(lax.rem(chunk + self.shift, self.chunks), self.rows)

    def source(self, way, step):
        return self.line.me - step if way == 0 else self.line.me + step

    def there(self, way, step):
        source = self.source(way, step)
        return source >= 0 if way == 0 else source < self.line.count

    def moved(self, way, step, source, chunk, towards):
        place = self.place(source, chunk)
        return self.line.copy(
            towards, place, place, self.send.at[way, step, chunk], self.recv.at[way, step, chunk]
        )

    def begin(self, chunk):
        for way in (0, 1):

            @pl.when(self.line.has_next(way))
            def _(way=way):
                place = self.place(self.line.me, chunk)
                src = place if self.own is None else self.own.at[self.span(chunk), :]
                self.line.copy(
                    way, src, place, self.send.at[way, 0, chunk], self.recv.at[way, 0, chunk]
                ).start()

    def relay(self, tick, late):
        for step in range(1, self.line.count):
            for way in (0, 1):
                source = self.source(way, step)
                chunk = tick - late(source) - step

                @pl.when(jnp.logical_and(within(chunk, self.chunks), self.there(way, step)))
                def _(way=way, step=step, source=source, chunk=chunk):
                    self.moved(way, step - 1, source, chunk, 1 - way).wait_recv()

                    @pl.when(self.line.has_next(way))
                    def _():
                        self.moved(way, step, source, chunk, way).start()

    def settle(self):
        for step in range(self.line.count):

            def turn(chunk, step=step):
                for way in (0, 1):

                    @pl.when(jnp.logical_and(self.there(way, step), self.line.has_next(way)))
                    def _(way=way):
                        self.moved(way, step, self.source(way, step), chunk, way).wait_send()

            each(self.chunks, turn)


def loop(count, body):
    def turn(index, _):
        body(index)
        return 0

    lax.fori_loop(0, count, turn, 0)


def turn_pairs(values, cosine, sine):
    turned = cosine.shape[-1]
    head = values[:, :turned]
    head = head * cosine + pltpu.roll(head, turned // 2, 1) * sine
    return jnp.concatenate([head, values[:, turned:]], axis=-1)


class Lend:
    def __init__(self, own, far, axis, n, m, parts, send, recv):
        self.own, self.far, self.axis, self.n, self.parts = own, far, axis, n, parts
        self.at, me = lax.axis_index("ctx"), lax.axis_index("mp")
        self.buddy = self.at + 1 - 2 * lax.rem(self.at, 2)
        self.other = lax.rem(me + m // 2, m)
        self.send, self.recv = send, recv

    def piece(self, ref, owner, part):
        size = ref.shape[self.axis] // self.n
        if self.axis == 0:
            rows = size // self.parts
            return ref.at[span_of(owner * self.parts + part, rows), :]
        return ref.at[span_of(part, ref.shape[0] // self.parts), span_of(owner, size)]

    def copy(self, src, dst, index, part, device):
        return pltpu.make_async_remote_copy(
            src_ref=src,
            dst_ref=dst,
            send_sem=self.send.at[index, part],
            recv_sem=self.recv.at[index, part],
            device_id=device,
        )

    def cross(self, part):
        return self.copy(
            self.piece(self.own, self.at, part),
            self.piece(self.far, self.at, part),
            0,
            part,
            {"mp": self.other},
        )

    def plane(self, k, back, part):
        place = self.piece(self.far, lax.rem(self.at - 2 * k * back + self.n, self.n), part)
        return self.copy(place, place, k, part, {"ctx": lax.rem(self.at + 2 * k, self.n)})

    def core(self, k, back, part):
        mine = self.buddy if back else self.at
        place = self.piece(self.far, lax.rem(mine - 2 * k + self.n, self.n), part)
        return self.copy(place, place, self.n // 2 + k, part, {"ctx": self.buddy})

    def start(self, part):
        self.cross(part).start()

    def spread(self, part):
        self.cross(part).wait_recv()
        for k in range(1, self.n // 2):
            self.plane(k, 0, part).start()
        self.core(0, 0, part).start()

    def share(self, part):
        for k in range(1, self.n // 2):
            self.plane(k, 1, part).wait_recv()
            self.core(k, 0, part).start()

    def step(self, tick, lags):
        for lag, action in zip(lags, (self.start, self.spread, self.share)):
            part = tick - lag

            @pl.when(within(part, self.parts))
            def _(part=part, action=action):
                action(part)

    def end(self):
        def turn(part):
            for k in range(self.n // 2):
                self.core(k, 1, part).wait_recv()
            self.cross(part).wait_send()
            for k in range(1, self.n // 2):
                self.plane(k, 0, part).wait_send()
            for k in range(self.n // 2):
                self.core(k, 0, part).wait_send()

        each(self.parts, turn)


def shortfall(x):
    series = jnp.ones_like(x)
    for term in range(12, 1, -1):
        series = 1.0 + series * x * (1.0 / term)
    return jnp.where(x > -1.0, -x * series, 1.0 - jnp.exp(x))


def first_kernel(
    n, m, chunks,
    own_ref, w_branch_ref, w_input_ref, taps_ref, w_rate_ref, w_admit_ref, soft_ref,
    w_out_ref, w_query_ref, w_kv_ref,
    gated_ref, share_ref, w_out_far_ref, w_query_far_ref, w_kv_far_ref,
    w_branch, w_input, full, inner, branch, decay, scaled, state, product, edge, got,
    loads, send, recv, local, l_send, l_recv, e_send, e_recv, b_send, b_recv,
):
    at, me = lax.axis_index("ctx"), lax.axis_index("mp")
    h = m // 2
    count, cols = own_ref.shape
    rows = count // chunks
    few = count // 2
    width = branch.shape[1]
    pad = 8
    fetches = [
        pltpu.make_async_copy(w_input_ref, w_input, loads.at[0]),
        pltpu.make_async_copy(w_branch_ref, w_branch, loads.at[1]),
    ]
    for fetch in fetches:
        fetch.start()
    meet(n, m)
    line = Line(me, m)
    gather = Gather(line, full, send, recv, cols, rows, chunks, own_ref, chunks - 1)
    outward, query, pair = [
        Lend(own, far, axis, n, m, chunks, l_send.at[index], l_recv.at[index])
        for index, (own, far, axis) in enumerate(
            [
                (w_out_ref, w_out_far_ref, 1),
                (w_query_ref, w_query_far_ref, 0),
                (w_kv_ref, w_kv_far_ref, 0),
            ]
        )
    ]
    for tick_zero in (0, 1):
        gather.begin(tick_zero)
        for lend in (outward, query, pair):
            lend.start(tick_zero)
    mine = full.at[:, pl.ds(pl.multiple_of(me * cols, cols), cols)]
    kept = pltpu.make_async_copy(own_ref, mine, local.at[0])
    kept.start()

    def border():
        return pltpu.make_async_remote_copy(
            src_ref=inner.at[pl.ds(count, pad), :],
            dst_ref=inner.at[pl.ds(0, pad), :],
            send_sem=b_send.at[0],
            recv_sem=b_recv.at[0],
            device_id={"ctx": lax.rem(at + 1, n)},
        )

    def project(chunk):
        span = span_of(chunk, rows)
        wide = full[span, :].astype(jnp.float32)
        scale = lax.rsqrt(jnp.mean(wide * wide, axis=-1, keepdims=True) + EPSILON)
        normed = (wide * scale).astype(jnp.bfloat16)
        inner[pl.ds(pl.multiple_of(chunk * rows + pad, pad), rows), :] = jnp.dot(
            normed, w_input[...], preferred_element_type=jnp.float32
        )
        branch[span, :] = jax.nn.gelu(
            jnp.dot(normed, w_branch[...], preferred_element_type=jnp.float32)
        )

    tile = 8
    place = lax.broadcasted_iota(jnp.int32, (tile, width), 0)

    def mix(chunk):
        span = span_of(chunk, rows)
        seen = inner[pl.ds(pl.multiple_of(chunk * rows, rows), rows + pad), :]
        convolved = jnp.zeros((rows, width), jnp.float32)
        for tap in range(taps_ref.shape[0]):
            convolved = convolved + taps_ref[tap : tap + 1, :] * seen[pad - tap : pad - tap + rows]
        low = convolved.astype(jnp.bfloat16)
        each_block = w_rate_ref.shape[1]

        def gate(weights):
            return jax.nn.sigmoid(
                jnp.concatenate(
                    [
                        jnp.dot(
                            low[:, index * each_block : (index + 1) * each_block],
                            weights[index],
                            preferred_element_type=jnp.float32,
                        )
                        for index in range(weights.shape[0])
                    ],
                    axis=-1,
                )
            )

        log_decay = -8.0 * gate(w_rate_ref) * soft_ref[...]
        decay[...] = jnp.exp(log_decay)
        scaled[...] = gate(w_admit_ref) * convolved * jnp.sqrt(shortfall(2.0 * log_decay))

        def advance(index, carried):
            last_state, last_product = carried
            here = pl.ds(pl.multiple_of(index * tile, tile), tile)
            there = pl.ds(pl.multiple_of(chunk * rows + index * tile, tile), tile)
            a = decay[here, :]
            b = scaled[here, :]
            for shift in (1, 2, 4):
                inside = place >= shift
                a_back = jnp.where(inside, pltpu.roll(a, shift, 0), 1.0)
                b_back = jnp.where(inside, pltpu.roll(b, shift, 0), 0.0)
                b = a * b_back + b
                a = a * a_back
            b = b + a * last_state
            a = a * last_product
            state[there, :] = b
            product[there, :] = a
            return b[tile - 1 :, :], a[tile - 1 :, :]

        ends = lax.fori_loop(
            0, rows // tile, advance, (edge[0:1, :], edge[1:2, :]), unroll=True
        )
        edge[0:1, :] = ends[0]
        edge[1:2, :] = ends[1]

    edge[0:1, :] = jnp.zeros((1, width), jnp.float32)
    edge[1:2, :] = jnp.ones((1, width), jnp.float32)
    latest = jnp.maximum(me, m - 1 - me)

    def tick(t):
        gather.relay(t, lambda source: 0)

        @pl.when(t + 2 < chunks)
        def _():
            gather.begin(t + 2)

        for lend in (outward, query, pair):
            lend.step(t, LENT)

        whole = t - latest

        @pl.when(whole == 0)
        def _():
            kept.wait()
            for fetch in fetches:
                fetch.wait()
            project(chunks - 1)

            @pl.when(at + 1 < n)
            def _():
                border().start()

            @pl.when(at == 0)
            def _():
                inner[0:pad, :] = jnp.zeros((pad, width), jnp.float32)

        @pl.when(jnp.logical_and(whole > 0, whole < chunks))
        def _():
            project(whole - 1)

            @pl.when(jnp.logical_and(whole == 1, at > 0))
            def _():
                border().wait_recv()

            mix(whole - 1)

    loop(chunks + m - 1, tick)
    mix(chunks - 1)
    copies = []
    for step in range(1, n):
        copy = pltpu.make_async_remote_copy(
            src_ref=edge,
            dst_ref=got.at[step],
            send_sem=e_send.at[step],
            recv_sem=e_recv.at[step],
            device_id={"ctx": lax.rem(at + step, n)},
        )
        copy.start()
        copies.append(copy)
    half, rank = me // h, lax.rem(me, h)
    shares = [
        pltpu.make_async_copy(
            full.at[
                pl.ds(pl.multiple_of(half * few, few), few),
                pl.ds(pl.multiple_of((rank + side * h) * cols, cols), cols),
            ],
            share_ref.at[:, side * cols : (side + 1) * cols],
            local.at[1 + side],
        )
        for side in (0, 1)
    ]
    for copy in shares:
        copy.start()
    for copy in copies:
        copy.wait()
    carry = jnp.zeros((1, width), jnp.float32)
    for step in range(n - 1, 0, -1):
        fresh = got[step, 0:1, :] + got[step, 1:2, :] * carry
        carry = jnp.where(at >= step, fresh, 0.0)

    def finish(index, _):
        span = span_of(index, 16)
        whole = state[span, :] + product[span, :] * carry
        gated_ref[span, :] = (whole * branch[span, :]).astype(gated_ref.dtype)
        return 0

    lax.fori_loop(0, count // 16, finish, 0, unroll=4)
    for tick_more in range(chunks + m - 1, chunks + LENT[2]):
        for lend in (outward, query, pair):
            lend.step(tick_more, LENT)
    gather.settle()
    for lend in (outward, pair, query):
        lend.end()

    @pl.when(at + 1 < n)
    def _():
        border().wait_send()

    for copy in shares:
        copy.wait()


def first(own, w_branch, w_input, taps, w_rate, w_admit, soft, w_out, w_query, w_kv, mark, chunks):
    n, m = lax.axis_size("ctx"), lax.axis_size("mp")
    count, cols = own.shape
    full_width, width = w_branch.shape
    rows = count // chunks
    vmem = pl.BlockSpec(memory_space=pltpu.VMEM)
    hbm = pl.BlockSpec(memory_space=pl.ANY)
    dma = pltpu.SemaphoreType.DMA
    wide = jnp.float32
    like = lambda x: jax.ShapeDtypeStruct(x.shape, x.dtype)
    return pl.pallas_call(
        functools.partial(first_kernel, n, m, chunks),
        out_shape=(
            jax.ShapeDtypeStruct((count, width), own.dtype),
            jax.ShapeDtypeStruct((count // 2, 2 * cols), own.dtype),
            like(w_out),
            like(w_query),
            like(w_kv),
        ),
        in_specs=[vmem, hbm, hbm, vmem, vmem, vmem, vmem, hbm, hbm, hbm],
        out_specs=(vmem,) + (hbm,) * 4,
        scratch_shapes=[
            pltpu.VMEM((full_width, width), w_branch.dtype),
            pltpu.VMEM((full_width, width), w_input.dtype),
            pltpu.VMEM((count, full_width), own.dtype),
            pltpu.VMEM((count + 8, width), wide),
            pltpu.VMEM((count, width), wide),
            pltpu.VMEM((rows, width), wide),
            pltpu.VMEM((rows, width), wide),
            pltpu.VMEM((count, width), wide),
            pltpu.VMEM((count, width), wide),
            pltpu.VMEM((2, width), wide),
            pltpu.VMEM((n, 2, width), wide),
            dma((2,)),
            dma((2, m, chunks)),
            dma((2, m, chunks)),
            dma((3,)),
            dma((3, n, chunks)),
            dma((3, n, chunks)),
            dma((n,)),
            dma((n,)),
            dma((1,)),
            dma((1,)),
        ],
        compiler_params=pltpu.CompilerParams(
            collective_id=mark, has_side_effects=True, vmem_limit_bytes=VMEM_LIMIT
        ),
    )(own, w_branch, w_input, taps, w_rate, w_admit, soft, w_out, w_query, w_kv)


def place_of(block, h):
    return block % h * 2 + block // h


def middle_kernel(
    n, m, chunks,
    gated_ref, base_ref, w_out_ref, w_out_far_ref, w_query_ref, w_query_far_ref,
    w_kv_ref, w_kv_far_ref, w_attn_ref, cos_ref, sin_ref,
    own_ref, query_ref, window_ref, w_attn_far_ref,
    w_out, w_query, w_kv, got, part, total, held, full, raw, kv, zeros,
    loads, h_send, h_recv, s_send, s_recv, g_send, g_recv, r_send, r_recv,
    k_send, k_recv, k_local, z_local, l_send, l_recv,
):
    at, me = lax.axis_index("ctx"), lax.axis_index("mp")
    h = m // 2
    half, local = me // h, lax.rem(me, h)
    far = lax.rem(me + h, m)
    count = gated_ref.shape[0]
    cols = base_ref.shape[1]
    block = cols // 2
    rows = base_ref.shape[0] // chunks
    queries = w_query_ref.shape[1]
    back = window_ref.shape[0] // count - 1

    def fetches(kind):
        for side in (0, 1):
            for index in range(m):
                rank = side * m + index
                here = slice(index * block, (index + 1) * block)
                put = place_of(index, h)
                there = slice(put * block, (put + 1) * block)
                if kind == 0:
                    src = (w_out_ref, w_out_far_ref)[side].at[:, here]
                    dst = w_out.at[side, :, there]
                elif kind == 1:
                    src = (w_query_ref, w_query_far_ref)[side].at[here, :]
                    dst = w_query.at[there, side * queries : (side + 1) * queries]
                else:
                    src = (w_kv_ref, w_kv_far_ref)[side].at[here, :]
                    dst = w_kv.at[side, there, :]
                yield pltpu.make_async_copy(src, dst, loads.at[kind, rank])

    for kind in range(3):
        for fetch in fetches(kind):
            fetch.start()
    meet(n, m)
    line = Line(local, h, half * h)
    scatter = Scatter(line, part, held, s_send, s_recv, cols, rows, chunks)
    gather = Gather(line, full, g_send, g_recv, cols, rows, chunks)

    def handed(chunk):
        return pltpu.make_async_remote_copy(
            src_ref=gated_ref.at[span_of((1 - half) * chunks + chunk, rows), :],
            dst_ref=got.at[span_of(chunk, rows), :],
            send_sem=h_send.at[chunk],
            recv_sem=h_recv.at[chunk],
            device_id={"mp": far},
        )

    def product(chunk):
        handed(chunk).wait_recv()
        near = gated_ref[span_of(half * chunks + chunk, rows), :]
        other = got[span_of(chunk, rows), :]
        for index in range(m):
            there = slice(index * block, (index + 1) * block)
            part[span_of(chunk, rows), there] = jnp.dot(
                near, w_out[0, :, there], preferred_element_type=jnp.float32
            ) + jnp.dot(other, w_out[1, :, there], preferred_element_type=jnp.float32)

    odd = lax.rem(at, 2)
    buddy = at + 1 - 2 * odd

    def slot(distance, chunk):
        return window_ref.at[span_of((back - distance) * 2 * chunks + chunk, rows), :]

    def ahead(distance, chunk):
        return pltpu.make_async_remote_copy(
            src_ref=kv.at[span_of(chunk, rows), :],
            dst_ref=slot(distance, chunk),
            send_sem=k_send.at[distance - 1, chunk],
            recv_sem=k_recv.at[distance - 1, chunk],
            device_id={"ctx": lax.rem(at + distance, n)},
        )

    def relayed(distance, chunk):
        other = distance + 1 - 2 * odd
        return pltpu.make_async_remote_copy(
            src_ref=slot(distance, chunk),
            dst_ref=slot(other, chunk),
            send_sem=k_send.at[other - 1, chunk],
            recv_sem=k_recv.at[other - 1, chunk],
            device_id={"ctx": buddy},
        )

    def relays(distance):
        wanted = jnp.logical_or(odd == 1, distance + 1 <= back)
        return jnp.logical_and(at >= distance, wanted)

    def kept(chunk):
        return pltpu.make_async_copy(
            kv.at[span_of(chunk, rows), :],
            window_ref.at[span_of(back * 2 * chunks + chunk, rows), :],
            k_local.at[chunk],
        )

    def blank(distance):
        return pltpu.make_async_copy(
            zeros, window_ref.at[span_of(back - distance, count), :], z_local.at[distance - 1]
        )

    def late(source):
        return jnp.maximum(source, h - 1 - source)

    def latest(mine):
        most = late(mine)
        for source in range(h):
            most = jnp.maximum(most, max(source, h - 1 - source) + jnp.abs(mine - source))
        return most

    def passed(turn, side, chunk, sender):
        owner = lax.rem(sender + side * h, m)
        place = raw.at[owner, span_of(sender // h * chunks + chunk, rows), :]
        return pltpu.make_async_remote_copy(
            src_ref=place,
            dst_ref=place,
            send_sem=r_send.at[turn - 1, side, chunk],
            recv_sem=r_recv.at[turn - 1, side, chunk],
            device_id={"mp": lax.rem(me + turn, m)},
        )

    def project(chunk):
        span = span_of(chunk, rows)
        whole_span = span_of(half * chunks + chunk, rows)
        wide = full[span, :].astype(jnp.float32)
        scale = lax.rsqrt(jnp.mean(wide * wide, axis=-1, keepdims=True) + EPSILON)
        normed = (wide * scale).astype(jnp.bfloat16)
        for side, owner in ((0, me), (1, far)):
            both = jnp.dot(normed, w_kv[side], preferred_element_type=jnp.float32)
            raw[owner, whole_span, :] = both.astype(raw.dtype)
        for turn in range(1, m):
            for side in (0, 1):
                passed(turn, side, chunk, me).start()
        cosine, sine = cos_ref[whole_span, :], sin_ref[whole_span, :]
        query = jnp.dot(normed, w_query[...], preferred_element_type=jnp.float32)
        for head in range(query.shape[1] // HD):
            there = slice(head * HD, (head + 1) * HD)
            turned = turn_pairs(query[:, there], cosine, sine) * HD ** (-0.5)
            query_ref[span, there] = turned.astype(query_ref.dtype)

    def spread(chunk):
        for turn in range(1, m):
            for side in (0, 1):
                passed(turn, side, chunk, lax.rem(me - turn + m, m)).wait_recv()
        part_width = raw.shape[2] // 2
        for portion in (0, 1):
            index = portion * chunks + chunk
            span = span_of(index, rows)
            pieces = [raw[owner, span, :].astype(jnp.float32) for owner in range(m)]
            key = jnp.concatenate([piece[:, :part_width] for piece in pieces], axis=-1)
            value = jnp.concatenate([piece[:, part_width:] for piece in pieces], axis=-1)
            kv[span, :HD] = turn_pairs(key, cos_ref[span, :], sin_ref[span, :]).astype(kv.dtype)
            kv[span, HD:] = value.astype(kv.dtype)
            kept(index).start()
            for distance in range(2, back + 1, 2):

                @pl.when(at + distance < n)
                def _(distance=distance, index=index):
                    ahead(distance, index).start()

            @pl.when(odd == 0)
            def _(index=index):
                ahead(1, index).start()

    each(chunks, lambda chunk: handed(chunk).start())
    lend = Lend(w_attn_ref, w_attn_far_ref, 1, n, m, chunks, l_send, l_recv)
    zeros[...] = jnp.zeros_like(zeros)
    for distance in range(1, back + 1):

        @pl.when(at < distance)
        def _(distance=distance):
            blank(distance).start()

    for fetch in fetches(0):
        fetch.wait()
    product(0)
    everywhere = 2 * (h - 1) + 1

    def tick(t):
        scatter.pass_on(t)
        done = t - scatter.late()

        @pl.when(within(done, chunks))
        def _():
            span = span_of(done, rows)
            scatter.arrive(done, base_ref[span, :], total)
            mine = total[...].astype(own_ref.dtype)
            own_ref[span, :] = mine
            full[span, pl.ds(pl.multiple_of(local * cols, cols), cols)] = mine
            gather.begin(done)

        gather.relay(t, late)

        @pl.when(t + 1 < chunks)
        def _():
            product(t + 1)

        joined = t - everywhere

        @pl.when(within(joined, chunks))
        def _():
            spread(joined)

        whole = t - latest(local)

        @pl.when(whole == 0)
        def _():
            for kind in (1, 2):
                for fetch in fetches(kind):
                    fetch.wait()

        @pl.when(within(whole, chunks))
        def _():
            project(whole)

        lend.step(t, LENT_LATE)

    loop(chunks + everywhere, tick)
    each(chunks, lambda chunk: handed(chunk).wait_send())
    for tick_more in range(chunks + everywhere, chunks + LENT_LATE[2]):
        lend.step(tick_more, LENT_LATE)
    lend.end()
    scatter.settle()
    gather.settle()
    for distance in range(1, back + 1):

        @pl.when(at < distance)
        def _(distance=distance):
            blank(distance).wait()

    def pass_over(chunk):
        for distance in range(2, back + 1, 2):

            @pl.when(at >= distance)
            def _(distance=distance):
                ahead(distance, chunk).wait_recv()

            @pl.when(relays(distance))
            def _(distance=distance):
                relayed(distance, chunk).start()

    each(2 * chunks, pass_over)

    def end(chunk):
        for distance in range(1, back + 1, 2):

            @pl.when(at >= distance)
            def _(distance=distance):
                ahead(distance, chunk).wait_recv()

        for distance in range(2, back + 1, 2):

            @pl.when(at + distance < n)
            def _(distance=distance):
                ahead(distance, chunk).wait_send()

            @pl.when(relays(distance))
            def _(distance=distance):
                relayed(distance, chunk).wait_send()

        @pl.when(odd == 0)
        def _():
            ahead(1, chunk).wait_send()

    each(2 * chunks, end)
    each(2 * chunks, lambda chunk: kept(chunk).wait())
    for turn in range(1, m):
        for side in (0, 1):
            each(
                chunks,
                lambda chunk, turn=turn, side=side: passed(turn, side, chunk, me).wait_send(),
            )


def middle(gated, base, w_out, w_query, w_kv, w_attn, cosine, sine, mark, chunks):
    n, m = lax.axis_size("ctx"), lax.axis_size("mp")
    h = m // 2
    count, channels = gated.shape
    few, cols = base.shape
    width = w_out[0].shape[1]
    queries = w_query[0].shape[1]
    part = w_kv[0].shape[1]
    wide = m * part
    rows = few // chunks
    back = WINDOW // count
    vmem = pl.BlockSpec(memory_space=pltpu.VMEM)
    hbm = pl.BlockSpec(memory_space=pl.ANY)
    low = jnp.bfloat16
    dma = pltpu.SemaphoreType.DMA
    return pl.pallas_call(
        functools.partial(middle_kernel, n, m, chunks),
        out_shape=(
            jax.ShapeDtypeStruct((few, cols), low),
            jax.ShapeDtypeStruct((few, 2 * queries), low),
            jax.ShapeDtypeStruct(((back + 1) * count, wide), low),
            jax.ShapeDtypeStruct(w_attn.shape, low),
        ),
        in_specs=[vmem, vmem] + [hbm] * 7 + [vmem, vmem],
        out_specs=(vmem, vmem, hbm, hbm),
        scratch_shapes=[
            pltpu.VMEM((2, channels, width), low),
            pltpu.VMEM((width, 2 * queries), low),
            pltpu.VMEM((2, width, part), low),
            pltpu.VMEM((few, channels), low),
            pltpu.VMEM((few, width), jnp.float32),
            pltpu.VMEM((rows, cols), jnp.float32),
            pltpu.VMEM((2, h - 1, few, cols), low),
            pltpu.VMEM((few, width), low),
            pltpu.VMEM((m, count, part), low),
            pltpu.VMEM((count, wide), low),
            pltpu.VMEM((count, wide), low),
            dma((3, 2 * m)),
            dma((chunks,)),
            dma((chunks,)),
            dma((2, h - 1, chunks)),
            dma((2, h - 1, chunks)),
            dma((2, h, chunks)),
            dma((2, h, chunks)),
            dma((m - 1, 2, chunks)),
            dma((m - 1, 2, chunks)),
            dma((back, 2 * chunks)),
            dma((back, 2 * chunks)),
            dma((2 * chunks,)),
            dma((back,)),
            dma((n, chunks)),
            dma((n, chunks)),
        ],
        compiler_params=pltpu.CompilerParams(
            collective_id=mark, has_side_effects=True, vmem_limit_bytes=VMEM_LIMIT
        ),
    )(gated, base, *w_out, *w_query, *w_kv, w_attn, cosine, sine)


def last_kernel(
    m, chunks,
    query_ref, window_ref, base_ref, w_out_ref, w_out_far_ref,
    result_ref,
    w_out, part, total, made, held, loads, s_send, s_recv, o_send, o_recv, o_local,
):
    at, me = lax.axis_index("ctx"), lax.axis_index("mp")
    h = m // 2
    half, local = me // h, lax.rem(me, h)
    far = lax.rem(me + h, m)
    few, cols = base_ref.shape
    count = 2 * few
    block = cols // 2
    channels = w_out_ref.shape[0]
    rows = few // chunks
    heads = query_ref.shape[1] // HD

    def fetches():
        for side in (0, 1):
            for index in range(m):
                put = place_of(index, h)
                yield pltpu.make_async_copy(
                    (w_out_ref, w_out_far_ref)[side].at[
                        :, index * block : (index + 1) * block
                    ],
                    w_out.at[
                        side * channels : (side + 1) * channels,
                        put * block : (put + 1) * block,
                    ],
                    loads.at[side * m + index],
                )

    for fetch in fetches():
        fetch.start()
    meet_line(m)
    line = Line(local, h, half * h)
    scatter = Scatter(line, part, held, s_send, s_recv, cols, rows, chunks)
    step = max(rows, 128)
    reach = WINDOW + step

    def sent(chunk):
        return pltpu.make_async_remote_copy(
            src_ref=made.at[
                span_of(chunk, rows), pl.ds(pl.multiple_of((1 - half) * block, block), block)
            ],
            dst_ref=result_ref.at[span_of(half * chunks + chunk, rows), :],
            send_sem=o_send.at[chunk],
            recv_sem=o_recv.at[chunk],
            device_id={"mp": far},
        )

    def came(chunk):
        place = result_ref.at[span_of((1 - half) * chunks + chunk, rows), :]
        return pltpu.make_async_remote_copy(
            src_ref=place,
            dst_ref=place,
            send_sem=o_send.at[chunk],
            recv_sem=o_recv.at[chunk],
            device_id={"mp": far},
        )

    def kept(chunk):
        return pltpu.make_async_copy(
            made.at[span_of(chunk, rows), pl.ds(pl.multiple_of(half * block, block), block)],
            result_ref.at[span_of(half * chunks + chunk, rows), :],
            o_local.at[chunk],
        )

    def attend(chunk):
        span = span_of(chunk, rows)
        place = half * few + chunk * rows
        first = pl.multiple_of(place // step * step, step)
        keys = window_ref[pl.ds(first, reach), :HD]
        values = window_ref[pl.ds(first, reach), HD:]
        tall = (heads * rows, reach)
        row = place + lax.rem(lax.broadcasted_iota(jnp.int32, tall, 0), rows)
        col = first + lax.broadcasted_iota(jnp.int32, tall, 1)
        distance = row + WINDOW - col
        valid = (distance >= 0) & (distance < WINDOW) & (col >= WINDOW - at * count)
        stacked = jnp.concatenate(
            [query_ref[span, head * HD : (head + 1) * HD] for head in range(heads)], axis=0
        )
        scores = lax.dot_general(
            stacked, keys, (((1,), (1,)), ((), ())), preferred_element_type=jnp.float32
        )
        masked = jnp.where(valid, scores, -1e30)
        top = jnp.max(masked, axis=-1, keepdims=True)
        weights = jnp.exp(masked - top)
        share = 1.0 / jnp.sum(weights, axis=-1, keepdims=True)
        probs = (weights * share).astype(jnp.bfloat16)
        mixed = jnp.dot(probs, values, preferred_element_type=jnp.float32).astype(jnp.bfloat16)
        attended = [mixed[head * rows : (head + 1) * rows, :] for head in range(heads)]
        taken = jnp.concatenate(attended, axis=-1)
        for index in range(m):
            there = slice(index * block, (index + 1) * block)
            part[span, there] = jnp.dot(
                taken, w_out[:, there], preferred_element_type=jnp.float32
            )

    for fetch in fetches():
        fetch.wait()
    attend(0)

    def tick(t):
        scatter.pass_on(t)
        done = t - scatter.late()

        @pl.when(within(done, chunks))
        def _():
            span = span_of(done, rows)
            scatter.arrive(done, base_ref[span, :], total)
            made[span, :] = total[...].astype(made.dtype)
            sent(done).start()
            kept(done).start()

        @pl.when(t + 1 < chunks)
        def _():
            attend(t + 1)

    loop(chunks + h - 1, tick)
    scatter.settle()

    def end(chunk):
        sent(chunk).wait_send()
        came(chunk).wait_recv()
        kept(chunk).wait()

    each(chunks, end)


def last(query, window, base, w_out, mark, chunks):
    m = lax.axis_size("mp")
    h = m // 2
    few, cols = base.shape
    channels, width = w_out[0].shape
    rows = few // chunks
    vmem = pl.BlockSpec(memory_space=pltpu.VMEM)
    hbm = pl.BlockSpec(memory_space=pl.ANY)
    low = jnp.bfloat16
    dma = pltpu.SemaphoreType.DMA
    return pl.pallas_call(
        functools.partial(last_kernel, m, chunks),
        out_shape=jax.ShapeDtypeStruct((2 * few, cols // 2), low),
        in_specs=[vmem, vmem, vmem, hbm, hbm],
        out_specs=hbm,
        scratch_shapes=[
            pltpu.VMEM((2 * channels, width), low),
            pltpu.VMEM((few, width), jnp.float32),
            pltpu.VMEM((rows, cols), jnp.float32),
            pltpu.VMEM((few, cols), low),
            pltpu.VMEM((2, h - 1, few, cols), low),
            dma((2 * m,)),
            dma((2, h - 1, chunks)),
            dma((2, h - 1, chunks)),
            dma((chunks,)),
            dma((chunks,)),
            dma((chunks,)),
        ],
        compiler_params=pltpu.CompilerParams(
            collective_id=mark, has_side_effects=True, vmem_limit_bytes=VMEM_LIMIT
        ),
    )(query, window, base, *w_out)


def turns(positions):
    turned = HD // 2
    half = turned // 2
    freqs = 10000.0 ** (-jnp.arange(half, dtype=jnp.float32) * 2.0 / turned)
    angles = positions.astype(jnp.float32)[:, None] * freqs[None, :]
    cosine, sine = jnp.cos(angles), jnp.sin(angles)
    return (
        jnp.concatenate([cosine, cosine], axis=-1),
        jnp.concatenate([-sine, sine], axis=-1),
    )


def on_device(
    tokens,
    w_branch,
    w_input,
    conv_kernel,
    w_rate,
    w_admit,
    lam,
    w_out,
    w_query,
    w_key,
    w_value,
    w_attn_out,
):
    batch, rows_dev, cols_dev = tokens.shape
    count = batch * rows_dev
    tokens_flat = tokens.reshape(count, cols_dev)
    w_kv = jnp.concatenate([w_key, w_value], axis=1)
    soft = jax.nn.softplus(-lam)[None, :]
    gated, share, w_out_far, w_query_far, w_kv_far = first(
        tokens_flat, w_branch, w_input, conv_kernel, w_rate, w_admit, soft,
        w_out, w_query, w_kv, 1, CHUNKS,
    )
    base = lax.axis_index("ctx") * rows_dev
    positions = base + jnp.arange(rows_dev, dtype=jnp.int32)
    cosine, sine = turns(positions)
    resid, query, window, w_attn_out_far = middle(
        gated, share, (w_out, w_out_far), (w_query, w_query_far), (w_kv, w_kv_far),
        w_attn_out, cosine, sine, 2, CHUNKS_MIDDLE,
    )
    result = last(query, window, resid, (w_attn_out, w_attn_out_far), 3, CHUNKS_LAST)
    return result.reshape(batch, rows_dev, cols_dev)


def solution(mesh):
    in_specs = (
        P(None, "ctx", "mp"),
        P(None, "mp"),
        P(None, "mp"),
        P(None, "mp"),
        P("mp", None, None),
        P("mp", None, None),
        P("mp"),
        P("mp", None),
        P(None, "mp"),
        P(None, "mp"),
        P(None, "mp"),
        P("mp", None),
    )
    out_specs = P(None, "ctx", "mp")
    return jax.shard_map(
        on_device, mesh=mesh, in_specs=in_specs, out_specs=out_specs, check_vma=False
    )
```

```python
import functools

import jax
import jax.numpy as jnp
from jax import lax
from jax.experimental import pallas as pl
from jax.experimental.pallas import tpu as pltpu
from jax.sharding import PartitionSpec as P

HD = 256
WINDOW = 2048


EPSILON = 1e-06


CHUNKS = 8
CHUNKS_MIDDLE = 8
LENT = (-2, 1, 3)
LENT_LATE = (0, 1, 3)
CHUNKS_LAST = 8


def each(chunks, body):
    def turn(chunk, _):
        body(chunk)
        return 0

    lax.fori_loop(0, chunks, turn, 0)


def span_of(chunk, rows):
    return pl.ds(pl.multiple_of(chunk * rows, rows), rows)


class Line:
    def __init__(self, me, count, start=0):
        self.me, self.count, self.start = me, count, start

    def steps(self, way):
        return self.me + 1 if way == 0 else self.me - 1

    def has_next(self, way):
        return self.me < self.count - 1 if way == 0 else self.me > 0

    def has_last(self, way):
        return self.me > 0 if way == 0 else self.me < self.count - 1

    def copy(self, way, src, dst, send, recv):
        return pltpu.make_async_remote_copy(
            src_ref=src,
            dst_ref=dst,
            send_sem=send,
            recv_sem=recv,
            device_id={"mp": self.start + self.steps(way)},
        )


VMEM_LIMIT = 56 * 1024 * 1024


def meet(n, m):
    at, me = lax.axis_index("ctx"), lax.axis_index("mp")
    barrier = pltpu.get_barrier_semaphore()
    for step in range(1, n):
        pl.semaphore_signal(barrier, inc=1, device_id={"ctx": lax.rem(at + step, n)})
    for step in range(1, m):
        pl.semaphore_signal(barrier, inc=1, device_id={"mp": lax.rem(me + step, m)})
    pl.semaphore_wait(barrier, n + m - 2)


def meet_line(m):
    me = lax.axis_index("mp")
    barrier = pltpu.get_barrier_semaphore()
    for step in range(1, m):
        pl.semaphore_signal(barrier, inc=1, device_id={"mp": lax.rem(me + step, m)})
    pl.semaphore_wait(barrier, m - 1)


def within(chunk, chunks):
    return jnp.logical_and(chunk >= 0, chunk < chunks)


class Scatter:
    def __init__(self, line, part, held, send, recv, cols, rows, chunks):
        self.line, self.part, self.held = line, part, held
        self.send, self.recv = send, recv
        self.cols, self.rows, self.chunks = cols, rows, chunks

    def goal(self, way, step):
        return self.line.count - 1 - step if way == 0 else step

    def beyond(self, way, step):
        goal = self.goal(way, step)
        return goal > self.line.me if way == 0 else goal < self.line.me

    def hop(self, way):
        return self.line.me if way == 0 else self.line.count - 1 - self.line.me

    def late(self):
        return jnp.maximum(self.hop(0), self.hop(1))

    def moved(self, way, step, chunk, towards):
        place = self.held.at[way, step, span_of(chunk, self.rows), :]
        return self.line.copy(
            towards, place, place, self.send.at[way, step, chunk], self.recv.at[way, step, chunk]
        )

    def term(self, owner, chunk):
        at = pl.ds(pl.multiple_of(owner * self.cols, self.cols), self.cols)
        return self.part[span_of(chunk, self.rows), at]

    def pass_on(self, tick):
        line, held = self.line, self.held
        for way in (0, 1):
            chunk = tick - self.hop(way)
            at = span_of(chunk, self.rows)
            for step in range(line.count - 1):

                @pl.when(jnp.logical_and(within(chunk, self.chunks), self.beyond(way, step)))
                def _(way=way, step=step, chunk=chunk, at=at):
                    own = self.term(self.goal(way, step), chunk)

                    @pl.when(line.has_last(way))
                    def _():
                        self.moved(way, step, chunk, 1 - way).wait_recv()
                        total = held[way, step, at, :].astype(jnp.float32) + own
                        held[way, step, at, :] = total.astype(held.dtype)

                    @pl.when(jnp.logical_not(line.has_last(way)))
                    def _():
                        held[way, step, at, :] = own.astype(held.dtype)

                    self.moved(way, step, chunk, way).start()

    def arrive(self, chunk, base, total):
        line = self.line
        total[...] = base.astype(jnp.float32) + self.term(line.me, chunk)
        for way in (0, 1):
            step = line.count - 1 - line.me if way == 0 else line.me

            @pl.when(line.has_last(way))
            def _(way=way, step=step):
                self.moved(way, step, chunk, 1 - way).wait_recv()
                total[...] += self.held[way, step, span_of(chunk, self.rows), :].astype(
                    jnp.float32
                )

    def settle(self):
        for step in range(self.line.count - 1):

            def turn(chunk, step=step):
                for way in (0, 1):

                    @pl.when(self.beyond(way, step))
                    def _(way=way):
                        self.moved(way, step, chunk, way).wait_send()

            each(self.chunks, turn)


class Gather:
    def __init__(self, line, full, send, recv, cols, rows, chunks, own=None, shift=0):
        self.line, self.full, self.own, self.shift = line, full, own, shift
        self.send, self.recv = send, recv
        self.cols, self.rows, self.chunks = cols, rows, chunks

    def place(self, owner, chunk):
        at = pl.ds(pl.multiple_of(owner * self.cols, self.cols), self.cols)
        return self.full.at[self.span(chunk), at]

    def span(self, chunk):
        return span_of(lax.rem(chunk + self.shift, self.chunks), self.rows)

    def source(self, way, step):
        return self.line.me - step if way == 0 else self.line.me + step

    def there(self, way, step):
        source = self.source(way, step)
        return source >= 0 if way == 0 else source < self.line.count

    def moved(self, way, step, source, chunk, towards):
        place = self.place(source, chunk)
        return self.line.copy(
            towards, place, place, self.send.at[way, step, chunk], self.recv.at[way, step, chunk]
        )

    def begin(self, chunk):
        for way in (0, 1):

            @pl.when(self.line.has_next(way))
            def _(way=way):
                place = self.place(self.line.me, chunk)
                src = place if self.own is None else self.own.at[self.span(chunk), :]
                self.line.copy(
                    way, src, place, self.send.at[way, 0, chunk], self.recv.at[way, 0, chunk]
                ).start()

    def relay(self, tick, late):
        for step in range(1, self.line.count):
            for way in (0, 1):
                source = self.source(way, step)
                chunk = tick - late(source) - step

                @pl.when(jnp.logical_and(within(chunk, self.chunks), self.there(way, step)))
                def _(way=way, step=step, source=source, chunk=chunk):
                    self.moved(way, step - 1, source, chunk, 1 - way).wait_recv()

                    @pl.when(self.line.has_next(way))
                    def _():
                        self.moved(way, step, source, chunk, way).start()

    def settle(self):
        for step in range(self.line.count):

            def turn(chunk, step=step):
                for way in (0, 1):

                    @pl.when(jnp.logical_and(self.there(way, step), self.line.has_next(way)))
                    def _(way=way):
                        self.moved(way, step, self.source(way, step), chunk, way).wait_send()

            each(self.chunks, turn)


def loop(count, body):
    def turn(index, _):
        body(index)
        return 0

    lax.fori_loop(0, count, turn, 0)


def turn_pairs(values, cosine, sine):
    turned = cosine.shape[-1]
    head = values[:, :turned]
    head = head * cosine + pltpu.roll(head, turned // 2, 1) * sine
    return jnp.concatenate([head, values[:, turned:]], axis=-1)


class Lend:
    def __init__(self, own, far, axis, n, m, parts, send, recv):
        self.own, self.far, self.axis, self.n, self.parts = own, far, axis, n, parts
        self.at, me = lax.axis_index("ctx"), lax.axis_index("mp")
        self.buddy = self.at + 1 - 2 * lax.rem(self.at, 2)
        self.other = lax.rem(me + m // 2, m)
        self.send, self.recv = send, recv

    def piece(self, ref, owner, part):
        size = ref.shape[self.axis] // self.n
        if self.axis == 0:
            rows = size // self.parts
            return ref.at[span_of(owner * self.parts + part, rows), :]
        return ref.at[span_of(part, ref.shape[0] // self.parts), span_of(owner, size)]

    def copy(self, src, dst, index, part, device):
        return pltpu.make_async_remote_copy(
            src_ref=src,
            dst_ref=dst,
            send_sem=self.send.at[index, part],
            recv_sem=self.recv.at[index, part],
            device_id=device,
        )

    def cross(self, part):
        return self.copy(
            self.piece(self.own, self.at, part),
            self.piece(self.far, self.at, part),
            0,
            part,
            {"mp": self.other},
        )

    def plane(self, k, back, part):
        place = self.piece(self.far, lax.rem(self.at - 2 * k * back + self.n, self.n), part)
        return self.copy(place, place, k, part, {"ctx": lax.rem(self.at + 2 * k, self.n)})

    def core(self, k, back, part):
        mine = self.buddy if back else self.at
        place = self.piece(self.far, lax.rem(mine - 2 * k + self.n, self.n), part)
        return self.copy(place, place, self.n // 2 + k, part, {"ctx": self.buddy})

    def start(self, part):
        self.cross(part).start()

    def spread(self, part):
        self.cross(part).wait_recv()
        for k in range(1, self.n // 2):
            self.plane(k, 0, part).start()
        self.core(0, 0, part).start()

    def share(self, part):
        for k in range(1, self.n // 2):
            self.plane(k, 1, part).wait_recv()
            self.core(k, 0, part).start()

    def step(self, tick, lags):
        for lag, action in zip(lags, (self.start, self.spread, self.share)):
            part = tick - lag

            @pl.when(within(part, self.parts))
            def _(part=part, action=action):
                action(part)

    def end(self):
        def turn(part):
            for k in range(self.n // 2):
                self.core(k, 1, part).wait_recv()
            self.cross(part).wait_send()
            for k in range(1, self.n // 2):
                self.plane(k, 0, part).wait_send()
            for k in range(self.n // 2):
                self.core(k, 0, part).wait_send()

        each(self.parts, turn)


def shortfall(x):
    series = jnp.ones_like(x)
    for term in range(12, 1, -1):
        series = 1.0 + series * x * (1.0 / term)
    return jnp.where(x > -1.0, -x * series, 1.0 - jnp.exp(x))


def first_kernel(
    n, m, chunks,
    own_ref, w_branch_ref, w_input_ref, taps_ref, w_rate_ref, w_admit_ref, soft_ref,
    w_out_ref, w_query_ref, w_kv_ref,
    gated_ref, share_ref, w_out_far_ref, w_query_far_ref, w_kv_far_ref,
    w_branch, w_input, full, inner, branch, decay, scaled, state, product, edge, got,
    loads, send, recv, local, l_send, l_recv, e_send, e_recv, b_send, b_recv,
):
    at, me = lax.axis_index("ctx"), lax.axis_index("mp")
    h = m // 2
    count, cols = own_ref.shape
    rows = count // chunks
    few = count // 2
    width = branch.shape[1]
    pad = 8
    fetches = [
        pltpu.make_async_copy(w_input_ref, w_input, loads.at[0]),
        pltpu.make_async_copy(w_branch_ref, w_branch, loads.at[1]),
    ]
    for fetch in fetches:
        fetch.start()
    meet(n, m)
    line = Line(me, m)
    gather = Gather(line, full, send, recv, cols, rows, chunks, own_ref, chunks - 1)
    outward, query, pair = [
        Lend(own, far, axis, n, m, chunks, l_send.at[index], l_recv.at[index])
        for index, (own, far, axis) in enumerate(
            [
                (w_out_ref, w_out_far_ref, 1),
                (w_query_ref, w_query_far_ref, 0),
                (w_kv_ref, w_kv_far_ref, 0),
            ]
        )
    ]
    for tick_zero in (0, 1):
        gather.begin(tick_zero)
        for lend in (outward, query, pair):
            lend.start(tick_zero)
    mine = full.at[:, pl.ds(pl.multiple_of(me * cols, cols), cols)]
    kept = pltpu.make_async_copy(own_ref, mine, local.at[0])
    kept.start()

    def border():
        return pltpu.make_async_remote_copy(
            src_ref=inner.at[pl.ds(count, pad), :],
            dst_ref=inner.at[pl.ds(0, pad), :],
            send_sem=b_send.at[0],
            recv_sem=b_recv.at[0],
            device_id={"ctx": lax.rem(at + 1, n)},
        )

    def project(chunk):
        span = span_of(chunk, rows)
        wide = full[span, :].astype(jnp.float32)
        scale = lax.rsqrt(jnp.mean(wide * wide, axis=-1, keepdims=True) + EPSILON)
        normed = (wide * scale).astype(jnp.bfloat16)
        inner[pl.ds(pl.multiple_of(chunk * rows + pad, pad), rows), :] = jnp.dot(
            normed, w_input[...], preferred_element_type=jnp.float32
        )
        branch[span, :] = jax.nn.gelu(
            jnp.dot(normed, w_branch[...], preferred_element_type=jnp.float32)
        )

    tile = 8
    place = lax.broadcasted_iota(jnp.int32, (tile, width), 0)

    def mix(chunk):
        span = span_of(chunk, rows)
        seen = inner[pl.ds(pl.multiple_of(chunk * rows, rows), rows + pad), :]
        convolved = jnp.zeros((rows, width), jnp.float32)
        for tap in range(taps_ref.shape[0]):
            convolved = convolved + taps_ref[tap : tap + 1, :] * seen[pad - tap : pad - tap + rows]
        low = convolved.astype(jnp.bfloat16)
        each_block = w_rate_ref.shape[1]

        def gate(weights):
            return jax.nn.sigmoid(
                jnp.concatenate(
                    [
                        jnp.dot(
                            low[:, index * each_block : (index + 1) * each_block],
                            weights[index],
                            preferred_element_type=jnp.float32,
                        )
                        for index in range(weights.shape[0])
                    ],
                    axis=-1,
                )
            )

        log_decay = -8.0 * gate(w_rate_ref) * soft_ref[...]
        decay[...] = jnp.exp(log_decay)
        scaled[...] = gate(w_admit_ref) * convolved * jnp.sqrt(shortfall(2.0 * log_decay))

        def advance(index, carried):
            last_state, last_product = carried
            here = pl.ds(pl.multiple_of(index * tile, tile), tile)
            there = pl.ds(pl.multiple_of(chunk * rows + index * tile, tile), tile)
            a = decay[here, :]
            b = scaled[here, :]
            for shift in (1, 2, 4):
                inside = place >= shift
                a_back = jnp.where(inside, pltpu.roll(a, shift, 0), 1.0)
                b_back = jnp.where(inside, pltpu.roll(b, shift, 0), 0.0)
                b = a * b_back + b
                a = a * a_back
            b = b + a * last_state
            a = a * last_product
            state[there, :] = b
            product[there, :] = a
            return b[tile - 1 :, :], a[tile - 1 :, :]

        ends = lax.fori_loop(
            0, rows // tile, advance, (edge[0:1, :], edge[1:2, :]), unroll=True
        )
        edge[0:1, :] = ends[0]
        edge[1:2, :] = ends[1]

    edge[0:1, :] = jnp.zeros((1, width), jnp.float32)
    edge[1:2, :] = jnp.ones((1, width), jnp.float32)
    latest = jnp.maximum(me, m - 1 - me)

    def tick(t):
        gather.relay(t, lambda source: 0)

        @pl.when(t + 2 < chunks)
        def _():
            gather.begin(t + 2)

        for lend in (outward, query, pair):
            lend.step(t, LENT)

        whole = t - latest

        @pl.when(whole == 0)
        def _():
            kept.wait()
            for fetch in fetches:
                fetch.wait()
            project(chunks - 1)

            @pl.when(at + 1 < n)
            def _():
                border().start()

            @pl.when(at == 0)
            def _():
                inner[0:pad, :] = jnp.zeros((pad, width), jnp.float32)

        @pl.when(jnp.logical_and(whole > 0, whole < chunks))
        def _():
            project(whole - 1)

            @pl.when(jnp.logical_and(whole == 1, at > 0))
            def _():
                border().wait_recv()

            mix(whole - 1)

    loop(chunks + m - 1, tick)
    mix(chunks - 1)
    copies = []
    for step in range(1, n):
        copy = pltpu.make_async_remote_copy(
            src_ref=edge,
            dst_ref=got.at[step],
            send_sem=e_send.at[step],
            recv_sem=e_recv.at[step],
            device_id={"ctx": lax.rem(at + step, n)},
        )
        copy.start()
        copies.append(copy)
    half, rank = me // h, lax.rem(me, h)
    shares = [
        pltpu.make_async_copy(
            full.at[
                pl.ds(pl.multiple_of(half * few, few), few),
                pl.ds(pl.multiple_of((rank + side * h) * cols, cols), cols),
            ],
            share_ref.at[:, side * cols : (side + 1) * cols],
            local.at[1 + side],
        )
        for side in (0, 1)
    ]
    for copy in shares:
        copy.start()
    for copy in copies:
        copy.wait()
    carry = jnp.zeros((1, width), jnp.float32)
    for step in range(n - 1, 0, -1):
        fresh = got[step, 0:1, :] + got[step, 1:2, :] * carry
        carry = jnp.where(at >= step, fresh, 0.0)

    def finish(index, _):
        span = span_of(index, 16)
        whole = state[span, :] + product[span, :] * carry
        gated_ref[span, :] = (whole * branch[span, :]).astype(gated_ref.dtype)
        return 0

    lax.fori_loop(0, count // 16, finish, 0, unroll=4)
    for tick_more in range(chunks + m - 1, chunks + LENT[2]):
        for lend in (outward, query, pair):
            lend.step(tick_more, LENT)
    gather.settle()
    for lend in (outward, pair, query):
        lend.end()

    @pl.when(at + 1 < n)
    def _():
        border().wait_send()

    for copy in shares:
        copy.wait()


def first(own, w_branch, w_input, taps, w_rate, w_admit, soft, w_out, w_query, w_kv, mark, chunks):
    n, m = lax.axis_size("ctx"), lax.axis_size("mp")
    count, cols = own.shape
    full_width, width = w_branch.shape
    rows = count // chunks
    vmem = pl.BlockSpec(memory_space=pltpu.VMEM)
    hbm = pl.BlockSpec(memory_space=pl.ANY)
    dma = pltpu.SemaphoreType.DMA
    wide = jnp.float32
    like = lambda x: jax.ShapeDtypeStruct(x.shape, x.dtype)
    return pl.pallas_call(
        functools.partial(first_kernel, n, m, chunks),
        out_shape=(
            jax.ShapeDtypeStruct((count, width), own.dtype),
            jax.ShapeDtypeStruct((count // 2, 2 * cols), own.dtype),
            like(w_out),
            like(w_query),
            like(w_kv),
        ),
        in_specs=[vmem, hbm, hbm, vmem, vmem, vmem, vmem, hbm, hbm, hbm],
        out_specs=(vmem,) + (hbm,) * 4,
        scratch_shapes=[
            pltpu.VMEM((full_width, width), w_branch.dtype),
            pltpu.VMEM((full_width, width), w_input.dtype),
            pltpu.VMEM((count, full_width), own.dtype),
            pltpu.VMEM((count + 8, width), wide),
            pltpu.VMEM((count, width), wide),
            pltpu.VMEM((rows, width), wide),
            pltpu.VMEM((rows, width), wide),
            pltpu.VMEM((count, width), wide),
            pltpu.VMEM((count, width), wide),
            pltpu.VMEM((2, width), wide),
            pltpu.VMEM((n, 2, width), wide),
            dma((2,)),
            dma((2, m, chunks)),
            dma((2, m, chunks)),
            dma((3,)),
            dma((3, n, chunks)),
            dma((3, n, chunks)),
            dma((n,)),
            dma((n,)),
            dma((1,)),
            dma((1,)),
        ],
        compiler_params=pltpu.CompilerParams(
            collective_id=mark, has_side_effects=True, vmem_limit_bytes=VMEM_LIMIT
        ),
    )(own, w_branch, w_input, taps, w_rate, w_admit, soft, w_out, w_query, w_kv)


def place_of(block, h):
    return block % h * 2 + block // h


def middle_kernel(
    n, m, chunks,
    gated_ref, base_ref, w_out_ref, w_out_far_ref, w_query_ref, w_query_far_ref,
    w_kv_ref, w_kv_far_ref, w_attn_ref, cos_ref, sin_ref,
    own_ref, query_ref, window_ref, w_attn_far_ref,
    w_out, w_query, w_kv, got, part, total, held, full, raw, kv, zeros,
    loads, h_send, h_recv, s_send, s_recv, g_send, g_recv, r_send, r_recv,
    k_send, k_recv, k_local, z_local, l_send, l_recv,
):
    at, me = lax.axis_index("ctx"), lax.axis_index("mp")
    h = m // 2
    half, local = me // h, lax.rem(me, h)
    far = lax.rem(me + h, m)
    count = gated_ref.shape[0]
    cols = base_ref.shape[1]
    block = cols // 2
    rows = base_ref.shape[0] // chunks
    queries = w_query_ref.shape[1]
    back = window_ref.shape[0] // count - 1

    def fetches(kind):
        for side in (0, 1):
            for index in range(m):
                rank = side * m + index
                here = slice(index * block, (index + 1) * block)
                put = place_of(index, h)
                there = slice(put * block, (put + 1) * block)
                if kind == 0:
                    src = (w_out_ref, w_out_far_ref)[side].at[:, here]
                    dst = w_out.at[side, :, there]
                elif kind == 1:
                    src = (w_query_ref, w_query_far_ref)[side].at[here, :]
                    dst = w_query.at[there, side * queries : (side + 1) * queries]
                else:
                    src = (w_kv_ref, w_kv_far_ref)[side].at[here, :]
                    dst = w_kv.at[side, there, :]
                yield pltpu.make_async_copy(src, dst, loads.at[kind, rank])

    for kind in range(3):
        for fetch in fetches(kind):
            fetch.start()
    meet(n, m)
    line = Line(local, h, half * h)
    scatter = Scatter(line, part, held, s_send, s_recv, cols, rows, chunks)
    gather = Gather(line, full, g_send, g_recv, cols, rows, chunks)

    def handed(chunk):
        return pltpu.make_async_remote_copy(
            src_ref=gated_ref.at[span_of((1 - half) * chunks + chunk, rows), :],
            dst_ref=got.at[span_of(chunk, rows), :],
            send_sem=h_send.at[chunk],
            recv_sem=h_recv.at[chunk],
            device_id={"mp": far},
        )

    def product(chunk):
        handed(chunk).wait_recv()
        near = gated_ref[span_of(half * chunks + chunk, rows), :]
        other = got[span_of(chunk, rows), :]
        for index in range(m):
            there = slice(index * block, (index + 1) * block)
            part[span_of(chunk, rows), there] = jnp.dot(
                near, w_out[0, :, there], preferred_element_type=jnp.float32
            ) + jnp.dot(other, w_out[1, :, there], preferred_element_type=jnp.float32)

    odd = lax.rem(at, 2)
    buddy = at + 1 - 2 * odd

    def slot(distance, chunk):
        return window_ref.at[span_of((back - distance) * 2 * chunks + chunk, rows), :]

    def ahead(distance, chunk):
        return pltpu.make_async_remote_copy(
            src_ref=kv.at[span_of(chunk, rows), :],
            dst_ref=slot(distance, chunk),
            send_sem=k_send.at[distance - 1, chunk],
            recv_sem=k_recv.at[distance - 1, chunk],
            device_id={"ctx": lax.rem(at + distance, n)},
        )

    def relayed(distance, chunk):
        other = distance + 1 - 2 * odd
        return pltpu.make_async_remote_copy(
            src_ref=slot(distance, chunk),
            dst_ref=slot(other, chunk),
            send_sem=k_send.at[other - 1, chunk],
            recv_sem=k_recv.at[other - 1, chunk],
            device_id={"ctx": buddy},
        )

    def relays(distance):
        wanted = jnp.logical_or(odd == 1, distance + 1 <= back)
        return jnp.logical_and(at >= distance, wanted)

    def kept(chunk):
        return pltpu.make_async_copy(
            kv.at[span_of(chunk, rows), :],
            window_ref.at[span_of(back * 2 * chunks + chunk, rows), :],
            k_local.at[chunk],
        )

    def blank(distance):
        return pltpu.make_async_copy(
            zeros, window_ref.at[span_of(back - distance, count), :], z_local.at[distance - 1]
        )

    def late(source):
        return jnp.maximum(source, h - 1 - source)

    def latest(mine):
        most = late(mine)
        for source in range(h):
            most = jnp.maximum(most, max(source, h - 1 - source) + jnp.abs(mine - source))
        return most

    def passed(turn, side, chunk, sender):
        owner = lax.rem(sender + side * h, m)
        place = raw.at[owner, span_of(sender // h * chunks + chunk, rows), :]
        return pltpu.make_async_remote_copy(
            src_ref=place,
            dst_ref=place,
            send_sem=r_send.at[turn - 1, side, chunk],
            recv_sem=r_recv.at[turn - 1, side, chunk],
            device_id={"mp": lax.rem(me + turn, m)},
        )

    def project(chunk):
        span = span_of(chunk, rows)
        whole_span = span_of(half * chunks + chunk, rows)
        wide = full[span, :].astype(jnp.float32)
        scale = lax.rsqrt(jnp.mean(wide * wide, axis=-1, keepdims=True) + EPSILON)
        normed = (wide * scale).astype(jnp.bfloat16)
        for side, owner in ((0, me), (1, far)):
            both = jnp.dot(normed, w_kv[side], preferred_element_type=jnp.float32)
            raw[owner, whole_span, :] = both.astype(raw.dtype)
        for turn in range(1, m):
            for side in (0, 1):
                passed(turn, side, chunk, me).start()
        cosine, sine = cos_ref[whole_span, :], sin_ref[whole_span, :]
        query = jnp.dot(normed, w_query[...], preferred_element_type=jnp.float32)
        for head in range(query.shape[1] // HD):
            there = slice(head * HD, (head + 1) * HD)
            turned = turn_pairs(query[:, there], cosine, sine) * HD ** (-0.5)
            query_ref[span, there] = turned.astype(query_ref.dtype)

    def spread(chunk):
        for turn in range(1, m):
            for side in (0, 1):
                passed(turn, side, chunk, lax.rem(me - turn + m, m)).wait_recv()
        part_width = raw.shape[2] // 2
        for portion in (0, 1):
            index = portion * chunks + chunk
            span = span_of(index, rows)
            pieces = [raw[owner, span, :].astype(jnp.float32) for owner in range(m)]
            key = jnp.concatenate([piece[:, :part_width] for piece in pieces], axis=-1)
            value = jnp.concatenate([piece[:, part_width:] for piece in pieces], axis=-1)
            kv[span, :HD] = turn_pairs(key, cos_ref[span, :], sin_ref[span, :]).astype(kv.dtype)
            kv[span, HD:] = value.astype(kv.dtype)
            kept(index).start()
            for distance in range(2, back + 1, 2):

                @pl.when(at + distance < n)
                def _(distance=distance, index=index):
                    ahead(distance, index).start()

            @pl.when(odd == 0)
            def _(index=index):
                ahead(1, index).start()

    each(chunks, lambda chunk: handed(chunk).start())
    lend = Lend(w_attn_ref, w_attn_far_ref, 1, n, m, chunks, l_send, l_recv)
    zeros[...] = jnp.zeros_like(zeros)
    for distance in range(1, back + 1):

        @pl.when(at < distance)
        def _(distance=distance):
            blank(distance).start()

    for fetch in fetches(0):
        fetch.wait()
    product(0)
    everywhere = 2 * (h - 1) + 1

    def tick(t):
        scatter.pass_on(t)
        done = t - scatter.late()

        @pl.when(within(done, chunks))
        def _():
            span = span_of(done, rows)
            scatter.arrive(done, base_ref[span, :], total)
            mine = total[...].astype(own_ref.dtype)
            own_ref[span, :] = mine
            full[span, pl.ds(pl.multiple_of(local * cols, cols), cols)] = mine
            gather.begin(done)

        gather.relay(t, late)

        @pl.when(t + 1 < chunks)
        def _():
            product(t + 1)

        joined = t - everywhere

        @pl.when(within(joined, chunks))
        def _():
            spread(joined)

        whole = t - latest(local)

        @pl.when(whole == 0)
        def _():
            for kind in (1, 2):
                for fetch in fetches(kind):
                    fetch.wait()

        @pl.when(within(whole, chunks))
        def _():
            project(whole)

        lend.step(t, LENT_LATE)

    loop(chunks + everywhere, tick)
    each(chunks, lambda chunk: handed(chunk).wait_send())
    for tick_more in range(chunks + everywhere, chunks + LENT_LATE[2]):
        lend.step(tick_more, LENT_LATE)
    lend.end()
    scatter.settle()
    gather.settle()
    for distance in range(1, back + 1):

        @pl.when(at < distance)
        def _(distance=distance):
            blank(distance).wait()

    def pass_over(chunk):
        for distance in range(2, back + 1, 2):

            @pl.when(at >= distance)
            def _(distance=distance):
                ahead(distance, chunk).wait_recv()

            @pl.when(relays(distance))
            def _(distance=distance):
                relayed(distance, chunk).start()

    each(2 * chunks, pass_over)

    def end(chunk):
        for distance in range(1, back + 1, 2):

            @pl.when(at >= distance)
            def _(distance=distance):
                ahead(distance, chunk).wait_recv()

        for distance in range(2, back + 1, 2):

            @pl.when(at + distance < n)
            def _(distance=distance):
                ahead(distance, chunk).wait_send()

            @pl.when(relays(distance))
            def _(distance=distance):
                relayed(distance, chunk).wait_send()

        @pl.when(odd == 0)
        def _():
            ahead(1, chunk).wait_send()

    each(2 * chunks, end)
    each(2 * chunks, lambda chunk: kept(chunk).wait())
    for turn in range(1, m):
        for side in (0, 1):
            each(
                chunks,
                lambda chunk, turn=turn, side=side: passed(turn, side, chunk, me).wait_send(),
            )


def middle(gated, base, w_out, w_query, w_kv, w_attn, cosine, sine, mark, chunks):
    n, m = lax.axis_size("ctx"), lax.axis_size("mp")
    h = m // 2
    count, channels = gated.shape
    few, cols = base.shape
    width = w_out[0].shape[1]
    queries = w_query[0].shape[1]
    part = w_kv[0].shape[1]
    wide = m * part
    rows = few // chunks
    back = WINDOW // count
    vmem = pl.BlockSpec(memory_space=pltpu.VMEM)
    hbm = pl.BlockSpec(memory_space=pl.ANY)
    low = jnp.bfloat16
    dma = pltpu.SemaphoreType.DMA
    return pl.pallas_call(
        functools.partial(middle_kernel, n, m, chunks),
        out_shape=(
            jax.ShapeDtypeStruct((few, cols), low),
            jax.ShapeDtypeStruct((few, 2 * queries), low),
            jax.ShapeDtypeStruct(((back + 1) * count, wide), low),
            jax.ShapeDtypeStruct(w_attn.shape, low),
        ),
        in_specs=[vmem, vmem] + [hbm] * 7 + [vmem, vmem],
        out_specs=(vmem, vmem, hbm, hbm),
        scratch_shapes=[
            pltpu.VMEM((2, channels, width), low),
            pltpu.VMEM((width, 2 * queries), low),
            pltpu.VMEM((2, width, part), low),
            pltpu.VMEM((few, channels), low),
            pltpu.VMEM((few, width), jnp.float32),
            pltpu.VMEM((rows, cols), jnp.float32),
            pltpu.VMEM((2, h - 1, few, cols), low),
            pltpu.VMEM((few, width), low),
            pltpu.VMEM((m, count, part), low),
            pltpu.VMEM((count, wide), low),
            pltpu.VMEM((count, wide), low),
            dma((3, 2 * m)),
            dma((chunks,)),
            dma((chunks,)),
            dma((2, h - 1, chunks)),
            dma((2, h - 1, chunks)),
            dma((2, h, chunks)),
            dma((2, h, chunks)),
            dma((m - 1, 2, chunks)),
            dma((m - 1, 2, chunks)),
            dma((back, 2 * chunks)),
            dma((back, 2 * chunks)),
            dma((2 * chunks,)),
            dma((back,)),
            dma((n, chunks)),
            dma((n, chunks)),
        ],
        compiler_params=pltpu.CompilerParams(
            collective_id=mark, has_side_effects=True, vmem_limit_bytes=VMEM_LIMIT
        ),
    )(gated, base, *w_out, *w_query, *w_kv, w_attn, cosine, sine)


def last_kernel(
    m, chunks,
    query_ref, window_ref, base_ref, w_out_ref, w_out_far_ref,
    result_ref,
    w_out, part, total, made, held, loads, s_send, s_recv, o_send, o_recv, o_local,
):
    at, me = lax.axis_index("ctx"), lax.axis_index("mp")
    h = m // 2
    half, local = me // h, lax.rem(me, h)
    far = lax.rem(me + h, m)
    few, cols = base_ref.shape
    count = 2 * few
    block = cols // 2
    channels = w_out_ref.shape[0]
    rows = few // chunks
    heads = query_ref.shape[1] // HD

    def fetches():
        for side in (0, 1):
            for index in range(m):
                put = place_of(index, h)
                yield pltpu.make_async_copy(
                    (w_out_ref, w_out_far_ref)[side].at[
                        :, index * block : (index + 1) * block
                    ],
                    w_out.at[
                        side * channels : (side + 1) * channels,
                        put * block : (put + 1) * block,
                    ],
                    loads.at[side * m + index],
                )

    for fetch in fetches():
        fetch.start()
    meet_line(m)
    line = Line(local, h, half * h)
    scatter = Scatter(line, part, held, s_send, s_recv, cols, rows, chunks)
    step = max(rows, 128)
    reach = WINDOW + step

    def sent(chunk):
        return pltpu.make_async_remote_copy(
            src_ref=made.at[
                span_of(chunk, rows), pl.ds(pl.multiple_of((1 - half) * block, block), block)
            ],
            dst_ref=result_ref.at[span_of(half * chunks + chunk, rows), :],
            send_sem=o_send.at[chunk],
            recv_sem=o_recv.at[chunk],
            device_id={"mp": far},
        )

    def came(chunk):
        place = result_ref.at[span_of((1 - half) * chunks + chunk, rows), :]
        return pltpu.make_async_remote_copy(
            src_ref=place,
            dst_ref=place,
            send_sem=o_send.at[chunk],
            recv_sem=o_recv.at[chunk],
            device_id={"mp": far},
        )

    def kept(chunk):
        return pltpu.make_async_copy(
            made.at[span_of(chunk, rows), pl.ds(pl.multiple_of(half * block, block), block)],
            result_ref.at[span_of(half * chunks + chunk, rows), :],
            o_local.at[chunk],
        )

    def attend(chunk):
        span = span_of(chunk, rows)
        place = half * few + chunk * rows
        first = pl.multiple_of(place // step * step, step)
        keys = window_ref[pl.ds(first, reach), :HD]
        values = window_ref[pl.ds(first, reach), HD:]
        tall = (heads * rows, reach)
        row = place + lax.rem(lax.broadcasted_iota(jnp.int32, tall, 0), rows)
        col = first + lax.broadcasted_iota(jnp.int32, tall, 1)
        distance = row + WINDOW - col
        valid = (distance >= 0) & (distance < WINDOW) & (col >= WINDOW - at * count)
        stacked = jnp.concatenate(
            [query_ref[span, head * HD : (head + 1) * HD] for head in range(heads)], axis=0
        )
        scores = lax.dot_general(
            stacked, keys, (((1,), (1,)), ((), ())), preferred_element_type=jnp.float32
        )
        masked = jnp.where(valid, scores, -1e30)
        top = jnp.max(masked, axis=-1, keepdims=True)
        weights = jnp.exp(masked - top)
        share = 1.0 / jnp.sum(weights, axis=-1, keepdims=True)
        probs = (weights * share).astype(jnp.bfloat16)
        mixed = jnp.dot(probs, values, preferred_element_type=jnp.float32).astype(jnp.bfloat16)
        attended = [mixed[head * rows : (head + 1) * rows, :] for head in range(heads)]
        taken = jnp.concatenate(attended, axis=-1)
        for index in range(m):
            there = slice(index * block, (index + 1) * block)
            part[span, there] = jnp.dot(
                taken, w_out[:, there], preferred_element_type=jnp.float32
            )

    for fetch in fetches():
        fetch.wait()
    attend(0)

    def tick(t):
        scatter.pass_on(t)
        done = t - scatter.late()

        @pl.when(within(done, chunks))
        def _():
            span = span_of(done, rows)
            scatter.arrive(done, base_ref[span, :], total)
            made[span, :] = total[...].astype(made.dtype)
            sent(done).start()
            kept(done).start()

        @pl.when(t + 1 < chunks)
        def _():
            attend(t + 1)

    loop(chunks + h - 1, tick)
    scatter.settle()

    def end(chunk):
        sent(chunk).wait_send()
        came(chunk).wait_recv()
        kept(chunk).wait()

    each(chunks, end)


def last(query, window, base, w_out, mark, chunks):
    m = lax.axis_size("mp")
    h = m // 2
    few, cols = base.shape
    channels, width = w_out[0].shape
    rows = few // chunks
    vmem = pl.BlockSpec(memory_space=pltpu.VMEM)
    hbm = pl.BlockSpec(memory_space=pl.ANY)
    low = jnp.bfloat16
    dma = pltpu.SemaphoreType.DMA
    return pl.pallas_call(
        functools.partial(last_kernel, m, chunks),
        out_shape=jax.ShapeDtypeStruct((2 * few, cols // 2), low),
        in_specs=[vmem, vmem, vmem, hbm, hbm],
        out_specs=hbm,
        scratch_shapes=[
            pltpu.VMEM((2 * channels, width), low),
            pltpu.VMEM((few, width), jnp.float32),
            pltpu.VMEM((rows, cols), jnp.float32),
            pltpu.VMEM((few, cols), low),
            pltpu.VMEM((2, h - 1, few, cols), low),
            dma((2 * m,)),
            dma((2, h - 1, chunks)),
            dma((2, h - 1, chunks)),
            dma((chunks,)),
            dma((chunks,)),
            dma((chunks,)),
        ],
        compiler_params=pltpu.CompilerParams(
            collective_id=mark, has_side_effects=True, vmem_limit_bytes=VMEM_LIMIT
        ),
    )(query, window, base, *w_out)


def turns(positions):
    turned = HD // 2
    half = turned // 2
    freqs = 10000.0 ** (-jnp.arange(half, dtype=jnp.float32) * 2.0 / turned)
    angles = positions.astype(jnp.float32)[:, None] * freqs[None, :]
    cosine, sine = jnp.cos(angles), jnp.sin(angles)
    return (
        jnp.concatenate([cosine, cosine], axis=-1),
        jnp.concatenate([-sine, sine], axis=-1),
    )


def on_device(
    tokens,
    w_branch,
    w_input,
    conv_kernel,
    w_rate,
    w_admit,
    lam,
    w_out,
    w_query,
    w_key,
    w_value,
    w_attn_out,
):
    batch, rows_dev, cols_dev = tokens.shape
    count = batch * rows_dev
    tokens_flat = tokens.reshape(count, cols_dev)
    w_kv = jnp.concatenate([w_key, w_value], axis=1)
    soft = jax.nn.softplus(-lam)[None, :]
    gated, share, w_out_far, w_query_far, w_kv_far = first(
        tokens_flat, w_branch, w_input, conv_kernel, w_rate, w_admit, soft,
        w_out, w_query, w_kv, 1, CHUNKS,
    )
    base = lax.axis_index("ctx") * rows_dev
    positions = base + jnp.arange(rows_dev, dtype=jnp.int32)
    cosine, sine = turns(positions)
    resid, query, window, w_attn_out_far = middle(
        gated, share, (w_out, w_out_far), (w_query, w_query_far), (w_kv, w_kv_far),
        w_attn_out, cosine, sine, 2, CHUNKS_MIDDLE,
    )
    result = last(query, window, resid, (w_attn_out, w_attn_out_far), 3, CHUNKS_LAST)
    return result.reshape(batch, rows_dev, cols_dev)


def solution(mesh):
    in_specs = (
        P(None, "ctx", "mp"),
        P(None, "mp"),
        P(None, "mp"),
        P(None, "mp"),
        P("mp", None, None),
        P("mp", None, None),
        P("mp"),
        P("mp", None),
        P(None, "mp"),
        P(None, "mp"),
        P(None, "mp"),
        P("mp", None),
    )
    out_specs = P(None, "ctx", "mp")
    return jax.shard_map(
        on_device, mesh=mesh, in_specs=in_specs, out_specs=out_specs, check_vma=False
    )
```

```python
import functools

import jax
import jax.numpy as jnp
from jax import lax
from jax.experimental import pallas as pl
from jax.experimental.pallas import tpu as pltpu
from jax.sharding import PartitionSpec as P

HD = 256
WINDOW = 2048


EPSILON = 1e-06


CHUNKS = 8
CHUNKS_MIDDLE = 8
LENT = (-2, 1, 4)
LENT_LATE = (0, 1, 4)
CHUNKS_LAST = 8


def each(chunks, body):
    def turn(chunk, _):
        body(chunk)
        return 0

    lax.fori_loop(0, chunks, turn, 0)


def span_of(chunk, rows):
    return pl.ds(pl.multiple_of(chunk * rows, rows), rows)


class Line:
    def __init__(self, me, count, start=0):
        self.me, self.count, self.start = me, count, start

    def steps(self, way):
        return self.me + 1 if way == 0 else self.me - 1

    def has_next(self, way):
        return self.me < self.count - 1 if way == 0 else self.me > 0

    def has_last(self, way):
        return self.me > 0 if way == 0 else self.me < self.count - 1

    def copy(self, way, src, dst, send, recv):
        return pltpu.make_async_remote_copy(
            src_ref=src,
            dst_ref=dst,
            send_sem=send,
            recv_sem=recv,
            device_id={"mp": self.start + self.steps(way)},
        )


VMEM_LIMIT = 56 * 1024 * 1024


def meet(n, m):
    at, me = lax.axis_index("ctx"), lax.axis_index("mp")
    barrier = pltpu.get_barrier_semaphore()
    for step in range(1, n):
        pl.semaphore_signal(barrier, inc=1, device_id={"ctx": lax.rem(at + step, n)})
    for step in range(1, m):
        pl.semaphore_signal(barrier, inc=1, device_id={"mp": lax.rem(me + step, m)})
    pl.semaphore_wait(barrier, n + m - 2)


def meet_line(m):
    me = lax.axis_index("mp")
    barrier = pltpu.get_barrier_semaphore()
    for step in range(1, m):
        pl.semaphore_signal(barrier, inc=1, device_id={"mp": lax.rem(me + step, m)})
    pl.semaphore_wait(barrier, m - 1)


def within(chunk, chunks):
    return jnp.logical_and(chunk >= 0, chunk < chunks)


class Scatter:
    def __init__(self, line, part, held, send, recv, cols, rows, chunks):
        self.line, self.part, self.held = line, part, held
        self.send, self.recv = send, recv
        self.cols, self.rows, self.chunks = cols, rows, chunks

    def goal(self, way, step):
        return self.line.count - 1 - step if way == 0 else step

    def beyond(self, way, step):
        goal = self.goal(way, step)
        return goal > self.line.me if way == 0 else goal < self.line.me

    def hop(self, way):
        return self.line.me if way == 0 else self.line.count - 1 - self.line.me

    def late(self):
        return jnp.maximum(self.hop(0), self.hop(1))

    def moved(self, way, step, chunk, towards):
        place = self.held.at[way, step, span_of(chunk, self.rows), :]
        return self.line.copy(
            towards, place, place, self.send.at[way, step, chunk], self.recv.at[way, step, chunk]
        )

    def term(self, owner, chunk):
        at = pl.ds(pl.multiple_of(owner * self.cols, self.cols), self.cols)
        return self.part[span_of(chunk, self.rows), at]

    def pass_on(self, tick):
        line, held = self.line, self.held
        for way in (0, 1):
            chunk = tick - self.hop(way)
            at = span_of(chunk, self.rows)
            for step in range(line.count - 1):

                @pl.when(jnp.logical_and(within(chunk, self.chunks), self.beyond(way, step)))
                def _(way=way, step=step, chunk=chunk, at=at):
                    own = self.term(self.goal(way, step), chunk)

                    @pl.when(line.has_last(way))
                    def _():
                        self.moved(way, step, chunk, 1 - way).wait_recv()
                        total = held[way, step, at, :].astype(jnp.float32) + own
                        held[way, step, at, :] = total.astype(held.dtype)

                    @pl.when(jnp.logical_not(line.has_last(way)))
                    def _():
                        held[way, step, at, :] = own.astype(held.dtype)

                    self.moved(way, step, chunk, way).start()

    def arrive(self, chunk, base, total):
        line = self.line
        total[...] = base.astype(jnp.float32) + self.term(line.me, chunk)
        for way in (0, 1):
            step = line.count - 1 - line.me if way == 0 else line.me

            @pl.when(line.has_last(way))
            def _(way=way, step=step):
                self.moved(way, step, chunk, 1 - way).wait_recv()
                total[...] += self.held[way, step, span_of(chunk, self.rows), :].astype(
                    jnp.float32
                )

    def settle(self):
        for step in range(self.line.count - 1):

            def turn(chunk, step=step):
                for way in (0, 1):

                    @pl.when(self.beyond(way, step))
                    def _(way=way):
                        self.moved(way, step, chunk, way).wait_send()

            each(self.chunks, turn)


class Gather:
    def __init__(self, line, full, send, recv, cols, rows, chunks, own=None, shift=0):
        self.line, self.full, self.own, self.shift = line, full, own, shift
        self.send, self.recv = send, recv
        self.cols, self.rows, self.chunks = cols, rows, chunks

    def place(self, owner, chunk):
        at = pl.ds(pl.multiple_of(owner * self.cols, self.cols), self.cols)
        return self.full.at[self.span(chunk), at]

    def span(self, chunk):
        return span_of(lax.rem(chunk + self.shift, self.chunks), self.rows)

    def source(self, way, step):
        return self.line.me - step if way == 0 else self.line.me + step

    def there(self, way, step):
        source = self.source(way, step)
        return source >= 0 if way == 0 else source < self.line.count

    def moved(self, way, step, source, chunk, towards):
        place = self.place(source, chunk)
        return self.line.copy(
            towards, place, place, self.send.at[way, step, chunk], self.recv.at[way, step, chunk]
        )

    def begin(self, chunk):
        for way in (0, 1):

            @pl.when(self.line.has_next(way))
            def _(way=way):
                place = self.place(self.line.me, chunk)
                src = place if self.own is None else self.own.at[self.span(chunk), :]
                self.line.copy(
                    way, src, place, self.send.at[way, 0, chunk], self.recv.at[way, 0, chunk]
                ).start()

    def relay(self, tick, late):
        for step in range(1, self.line.count):
            for way in (0, 1):
                source = self.source(way, step)
                chunk = tick - late(source) - step

                @pl.when(jnp.logical_and(within(chunk, self.chunks), self.there(way, step)))
                def _(way=way, step=step, source=source, chunk=chunk):
                    self.moved(way, step - 1, source, chunk, 1 - way).wait_recv()

                    @pl.when(self.line.has_next(way))
                    def _():
                        self.moved(way, step, source, chunk, way).start()

    def settle(self):
        for step in range(self.line.count):

            def turn(chunk, step=step):
                for way in (0, 1):

                    @pl.when(jnp.logical_and(self.there(way, step), self.line.has_next(way)))
                    def _(way=way):
                        self.moved(way, step, self.source(way, step), chunk, way).wait_send()

            each(self.chunks, turn)


def loop(count, body):
    def turn(index, _):
        body(index)
        return 0

    lax.fori_loop(0, count, turn, 0)


def turn_pairs(values, cosine, sine):
    turned = cosine.shape[-1]
    head = values[:, :turned]
    head = head * cosine + pltpu.roll(head, turned // 2, 1) * sine
    return jnp.concatenate([head, values[:, turned:]], axis=-1)


class Lend:
    def __init__(self, own, far, axis, n, m, parts, send, recv):
        self.own, self.far, self.axis, self.n, self.parts = own, far, axis, n, parts
        self.at, me = lax.axis_index("ctx"), lax.axis_index("mp")
        self.buddy = self.at + 1 - 2 * lax.rem(self.at, 2)
        self.other = lax.rem(me + m // 2, m)
        self.send, self.recv = send, recv

    def piece(self, ref, owner, part):
        size = ref.shape[self.axis] // self.n
        if self.axis == 0:
            rows = size // self.parts
            return ref.at[span_of(owner * self.parts + part, rows), :]
        return ref.at[span_of(part, ref.shape[0] // self.parts), span_of(owner, size)]

    def copy(self, src, dst, index, part, device):
        return pltpu.make_async_remote_copy(
            src_ref=src,
            dst_ref=dst,
            send_sem=self.send.at[index, part],
            recv_sem=self.recv.at[index, part],
            device_id=device,
        )

    def cross(self, part):
        return self.copy(
            self.piece(self.own, self.at, part),
            self.piece(self.far, self.at, part),
            0,
            part,
            {"mp": self.other},
        )

    def plane(self, k, back, part):
        place = self.piece(self.far, lax.rem(self.at - 2 * k * back + self.n, self.n), part)
        return self.copy(place, place, k, part, {"ctx": lax.rem(self.at + 2 * k, self.n)})

    def core(self, k, back, part):
        mine = self.buddy if back else self.at
        place = self.piece(self.far, lax.rem(mine - 2 * k + self.n, self.n), part)
        return self.copy(place, place, self.n // 2 + k, part, {"ctx": self.buddy})

    def start(self, part):
        self.cross(part).start()

    def spread(self, part):
        self.cross(part).wait_recv()
        for k in range(1, self.n // 2):
            self.plane(k, 0, part).start()
        self.core(0, 0, part).start()

    def share(self, part):
        for k in range(1, self.n // 2):
            self.plane(k, 1, part).wait_recv()
            self.core(k, 0, part).start()

    def step(self, tick, lags):
        for lag, action in zip(lags, (self.start, self.spread, self.share)):
            part = tick - lag

            @pl.when(within(part, self.parts))
            def _(part=part, action=action):
                action(part)

    def end(self):
        def turn(part):
            for k in range(self.n // 2):
                self.core(k, 1, part).wait_recv()
            self.cross(part).wait_send()
            for k in range(1, self.n // 2):
                self.plane(k, 0, part).wait_send()
            for k in range(self.n // 2):
                self.core(k, 0, part).wait_send()

        each(self.parts, turn)


def shortfall(x):
    series = jnp.ones_like(x)
    for term in range(12, 1, -1):
        series = 1.0 + series * x * (1.0 / term)
    return jnp.where(x > -1.0, -x * series, 1.0 - jnp.exp(x))


def first_kernel(
    n, m, chunks,
    own_ref, w_branch_ref, w_input_ref, taps_ref, w_rate_ref, w_admit_ref, soft_ref,
    w_out_ref, w_query_ref, w_kv_ref,
    gated_ref, share_ref, w_out_far_ref, w_query_far_ref, w_kv_far_ref,
    w_branch, w_input, full, inner, branch, decay, scaled, state, product, edge, got,
    loads, send, recv, local, l_send, l_recv, e_send, e_recv, b_send, b_recv,
):
    at, me = lax.axis_index("ctx"), lax.axis_index("mp")
    h = m // 2
    count, cols = own_ref.shape
    rows = count // chunks
    few = count // 2
    width = branch.shape[1]
    pad = 8
    fetches = [
        pltpu.make_async_copy(w_input_ref, w_input, loads.at[0]),
        pltpu.make_async_copy(w_branch_ref, w_branch, loads.at[1]),
    ]
    for fetch in fetches:
        fetch.start()
    meet(n, m)
    line = Line(me, m)
    gather = Gather(line, full, send, recv, cols, rows, chunks, own_ref, chunks - 1)
    outward, query, pair = [
        Lend(own, far, axis, n, m, chunks, l_send.at[index], l_recv.at[index])
        for index, (own, far, axis) in enumerate(
            [
                (w_out_ref, w_out_far_ref, 1),
                (w_query_ref, w_query_far_ref, 0),
                (w_kv_ref, w_kv_far_ref, 0),
            ]
        )
    ]
    for tick_zero in (0, 1):
        gather.begin(tick_zero)
        for lend in (outward, query, pair):
            lend.start(tick_zero)
    mine = full.at[:, pl.ds(pl.multiple_of(me * cols, cols), cols)]
    kept = pltpu.make_async_copy(own_ref, mine, local.at[0])
    kept.start()

    def border():
        return pltpu.make_async_remote_copy(
            src_ref=inner.at[pl.ds(count, pad), :],
            dst_ref=inner.at[pl.ds(0, pad), :],
            send_sem=b_send.at[0],
            recv_sem=b_recv.at[0],
            device_id={"ctx": lax.rem(at + 1, n)},
        )

    def project(chunk):
        span = span_of(chunk, rows)
        wide = full[span, :].astype(jnp.float32)
        scale = lax.rsqrt(jnp.mean(wide * wide, axis=-1, keepdims=True) + EPSILON)
        normed = (wide * scale).astype(jnp.bfloat16)
        inner[pl.ds(pl.multiple_of(chunk * rows + pad, pad), rows), :] = jnp.dot(
            normed, w_input[...], preferred_element_type=jnp.float32
        )
        branch[span, :] = jax.nn.gelu(
            jnp.dot(normed, w_branch[...], preferred_element_type=jnp.float32)
        )

    tile = 8
    place = lax.broadcasted_iota(jnp.int32, (tile, width), 0)

    def mix(chunk):
        span = span_of(chunk, rows)
        seen = inner[pl.ds(pl.multiple_of(chunk * rows, rows), rows + pad), :]
        convolved = jnp.zeros((rows, width), jnp.float32)
        for tap in range(taps_ref.shape[0]):
            convolved = convolved + taps_ref[tap : tap + 1, :] * seen[pad - tap : pad - tap + rows]
        low = convolved.astype(jnp.bfloat16)
        each_block = w_rate_ref.shape[1]

        def gate(weights):
            return jax.nn.sigmoid(
                jnp.concatenate(
                    [
                        jnp.dot(
                            low[:, index * each_block : (index + 1) * each_block],
                            weights[index],
                            preferred_element_type=jnp.float32,
                        )
                        for index in range(weights.shape[0])
                    ],
                    axis=-1,
                )
            )

        log_decay = -8.0 * gate(w_rate_ref) * soft_ref[...]
        decay[...] = jnp.exp(log_decay)
        scaled[...] = gate(w_admit_ref) * convolved * jnp.sqrt(shortfall(2.0 * log_decay))

        def advance(index, carried):
            last_state, last_product = carried
            here = pl.ds(pl.multiple_of(index * tile, tile), tile)
            there = pl.ds(pl.multiple_of(chunk * rows + index * tile, tile), tile)
            a = decay[here, :]
            b = scaled[here, :]
            for shift in (1, 2, 4):
                inside = place >= shift
                a_back = jnp.where(inside, pltpu.roll(a, shift, 0), 1.0)
                b_back = jnp.where(inside, pltpu.roll(b, shift, 0), 0.0)
                b = a * b_back + b
                a = a * a_back
            b = b + a * last_state
            a = a * last_product
            state[there, :] = b
            product[there, :] = a
            return b[tile - 1 :, :], a[tile - 1 :, :]

        ends = lax.fori_loop(
            0, rows // tile, advance, (edge[0:1, :], edge[1:2, :]), unroll=True
        )
        edge[0:1, :] = ends[0]
        edge[1:2, :] = ends[1]

    edge[0:1, :] = jnp.zeros((1, width), jnp.float32)
    edge[1:2, :] = jnp.ones((1, width), jnp.float32)
    latest = jnp.maximum(me, m - 1 - me)

    def tick(t):
        gather.relay(t, lambda source: 0)

        @pl.when(t + 2 < chunks)
        def _():
            gather.begin(t + 2)

        for lend in (outward, query, pair):
            lend.step(t, LENT)

        whole = t - latest

        @pl.when(whole == 0)
        def _():
            kept.wait()
            for fetch in fetches:
                fetch.wait()
            project(chunks - 1)

            @pl.when(at + 1 < n)
            def _():
                border().start()

            @pl.when(at == 0)
            def _():
                inner[0:pad, :] = jnp.zeros((pad, width), jnp.float32)

        @pl.when(jnp.logical_and(whole > 0, whole < chunks))
        def _():
            project(whole - 1)

            @pl.when(jnp.logical_and(whole == 1, at > 0))
            def _():
                border().wait_recv()

            mix(whole - 1)

    loop(chunks + m - 1, tick)
    mix(chunks - 1)
    copies = []
    for step in range(1, n):
        copy = pltpu.make_async_remote_copy(
            src_ref=edge,
            dst_ref=got.at[step],
            send_sem=e_send.at[step],
            recv_sem=e_recv.at[step],
            device_id={"ctx": lax.rem(at + step, n)},
        )
        copy.start()
        copies.append(copy)
    half, rank = me // h, lax.rem(me, h)
    shares = [
        pltpu.make_async_copy(
            full.at[
                pl.ds(pl.multiple_of(half * few, few), few),
                pl.ds(pl.multiple_of((rank + side * h) * cols, cols), cols),
            ],
            share_ref.at[:, side * cols : (side + 1) * cols],
            local.at[1 + side],
        )
        for side in (0, 1)
    ]
    for copy in shares:
        copy.start()
    for copy in copies:
        copy.wait()
    carry = jnp.zeros((1, width), jnp.float32)
    for step in range(n - 1, 0, -1):
        fresh = got[step, 0:1, :] + got[step, 1:2, :] * carry
        carry = jnp.where(at >= step, fresh, 0.0)

    def finish(index, _):
        span = span_of(index, 16)
        whole = state[span, :] + product[span, :] * carry
        gated_ref[span, :] = (whole * branch[span, :]).astype(gated_ref.dtype)
        return 0

    lax.fori_loop(0, count // 16, finish, 0, unroll=4)
    for tick_more in range(chunks + m - 1, chunks + LENT[2]):
        for lend in (outward, query, pair):
            lend.step(tick_more, LENT)
    gather.settle()
    for lend in (outward, pair, query):
        lend.end()

    @pl.when(at + 1 < n)
    def _():
        border().wait_send()

    for copy in shares:
        copy.wait()


def first(own, w_branch, w_input, taps, w_rate, w_admit, soft, w_out, w_query, w_kv, mark, chunks):
    n, m = lax.axis_size("ctx"), lax.axis_size("mp")
    count, cols = own.shape
    full_width, width = w_branch.shape
    rows = count // chunks
    vmem = pl.BlockSpec(memory_space=pltpu.VMEM)
    hbm = pl.BlockSpec(memory_space=pl.ANY)
    dma = pltpu.SemaphoreType.DMA
    wide = jnp.float32
    like = lambda x: jax.ShapeDtypeStruct(x.shape, x.dtype)
    return pl.pallas_call(
        functools.partial(first_kernel, n, m, chunks),
        out_shape=(
            jax.ShapeDtypeStruct((count, width), own.dtype),
            jax.ShapeDtypeStruct((count // 2, 2 * cols), own.dtype),
            like(w_out),
            like(w_query),
            like(w_kv),
        ),
        in_specs=[vmem, hbm, hbm, vmem, vmem, vmem, vmem, hbm, hbm, hbm],
        out_specs=(vmem,) + (hbm,) * 4,
        scratch_shapes=[
            pltpu.VMEM((full_width, width), w_branch.dtype),
            pltpu.VMEM((full_width, width), w_input.dtype),
            pltpu.VMEM((count, full_width), own.dtype),
            pltpu.VMEM((count + 8, width), wide),
            pltpu.VMEM((count, width), wide),
            pltpu.VMEM((rows, width), wide),
            pltpu.VMEM((rows, width), wide),
            pltpu.VMEM((count, width), wide),
            pltpu.VMEM((count, width), wide),
            pltpu.VMEM((2, width), wide),
            pltpu.VMEM((n, 2, width), wide),
            dma((2,)),
            dma((2, m, chunks)),
            dma((2, m, chunks)),
            dma((3,)),
            dma((3, n, chunks)),
            dma((3, n, chunks)),
            dma((n,)),
            dma((n,)),
            dma((1,)),
            dma((1,)),
        ],
        compiler_params=pltpu.CompilerParams(
            collective_id=mark, has_side_effects=True, vmem_limit_bytes=VMEM_LIMIT
        ),
    )(own, w_branch, w_input, taps, w_rate, w_admit, soft, w_out, w_query, w_kv)


def place_of(block, h):
    return block % h * 2 + block // h


def middle_kernel(
    n, m, chunks,
    gated_ref, base_ref, w_out_ref, w_out_far_ref, w_query_ref, w_query_far_ref,
    w_kv_ref, w_kv_far_ref, w_attn_ref, cos_ref, sin_ref,
    own_ref, query_ref, window_ref, w_attn_far_ref,
    w_out, w_query, w_kv, got, part, total, held, full, raw, kv, zeros,
    loads, h_send, h_recv, s_send, s_recv, g_send, g_recv, r_send, r_recv,
    k_send, k_recv, k_local, z_local, l_send, l_recv,
):
    at, me = lax.axis_index("ctx"), lax.axis_index("mp")
    h = m // 2
    half, local = me // h, lax.rem(me, h)
    far = lax.rem(me + h, m)
    count = gated_ref.shape[0]
    cols = base_ref.shape[1]
    block = cols // 2
    rows = base_ref.shape[0] // chunks
    queries = w_query_ref.shape[1]
    back = window_ref.shape[0] // count - 1

    def fetches(kind):
        for side in (0, 1):
            for index in range(m):
                rank = side * m + index
                here = slice(index * block, (index + 1) * block)
                put = place_of(index, h)
                there = slice(put * block, (put + 1) * block)
                if kind == 0:
                    src = (w_out_ref, w_out_far_ref)[side].at[:, here]
                    dst = w_out.at[side, :, there]
                elif kind == 1:
                    src = (w_query_ref, w_query_far_ref)[side].at[here, :]
                    dst = w_query.at[there, side * queries : (side + 1) * queries]
                else:
                    src = (w_kv_ref, w_kv_far_ref)[side].at[here, :]
                    dst = w_kv.at[side, there, :]
                yield pltpu.make_async_copy(src, dst, loads.at[kind, rank])

    for kind in range(3):
        for fetch in fetches(kind):
            fetch.start()
    meet(n, m)
    line = Line(local, h, half * h)
    scatter = Scatter(line, part, held, s_send, s_recv, cols, rows, chunks)
    gather = Gather(line, full, g_send, g_recv, cols, rows, chunks)

    def handed(chunk):
        return pltpu.make_async_remote_copy(
            src_ref=gated_ref.at[span_of((1 - half) * chunks + chunk, rows), :],
            dst_ref=got.at[span_of(chunk, rows), :],
            send_sem=h_send.at[chunk],
            recv_sem=h_recv.at[chunk],
            device_id={"mp": far},
        )

    def product(chunk):
        handed(chunk).wait_recv()
        near = gated_ref[span_of(half * chunks + chunk, rows), :]
        other = got[span_of(chunk, rows), :]
        for index in range(m):
            there = slice(index * block, (index + 1) * block)
            part[span_of(chunk, rows), there] = jnp.dot(
                near, w_out[0, :, there], preferred_element_type=jnp.float32
            ) + jnp.dot(other, w_out[1, :, there], preferred_element_type=jnp.float32)

    odd = lax.rem(at, 2)
    buddy = at + 1 - 2 * odd

    def slot(distance, chunk):
        return window_ref.at[span_of((back - distance) * 2 * chunks + chunk, rows), :]

    def ahead(distance, chunk):
        return pltpu.make_async_remote_copy(
            src_ref=kv.at[span_of(chunk, rows), :],
            dst_ref=slot(distance, chunk),
            send_sem=k_send.at[distance - 1, chunk],
            recv_sem=k_recv.at[distance - 1, chunk],
            device_id={"ctx": lax.rem(at + distance, n)},
        )

    def relayed(distance, chunk):
        other = distance + 1 - 2 * odd
        return pltpu.make_async_remote_copy(
            src_ref=slot(distance, chunk),
            dst_ref=slot(other, chunk),
            send_sem=k_send.at[other - 1, chunk],
            recv_sem=k_recv.at[other - 1, chunk],
            device_id={"ctx": buddy},
        )

    def relays(distance):
        wanted = jnp.logical_or(odd == 1, distance + 1 <= back)
        return jnp.logical_and(at >= distance, wanted)

    def kept(chunk):
        return pltpu.make_async_copy(
            kv.at[span_of(chunk, rows), :],
            window_ref.at[span_of(back * 2 * chunks + chunk, rows), :],
            k_local.at[chunk],
        )

    def blank(distance):
        return pltpu.make_async_copy(
            zeros, window_ref.at[span_of(back - distance, count), :], z_local.at[distance - 1]
        )

    def late(source):
        return jnp.maximum(source, h - 1 - source)

    def latest(mine):
        most = late(mine)
        for source in range(h):
            most = jnp.maximum(most, max(source, h - 1 - source) + jnp.abs(mine - source))
        return most

    def passed(turn, side, chunk, sender):
        owner = lax.rem(sender + side * h, m)
        place = raw.at[owner, span_of(sender // h * chunks + chunk, rows), :]
        return pltpu.make_async_remote_copy(
            src_ref=place,
            dst_ref=place,
            send_sem=r_send.at[turn - 1, side, chunk],
            recv_sem=r_recv.at[turn - 1, side, chunk],
            device_id={"mp": lax.rem(me + turn, m)},
        )

    def project(chunk):
        span = span_of(chunk, rows)
        whole_span = span_of(half * chunks + chunk, rows)
        wide = full[span, :].astype(jnp.float32)
        scale = lax.rsqrt(jnp.mean(wide * wide, axis=-1, keepdims=True) + EPSILON)
        normed = (wide * scale).astype(jnp.bfloat16)
        for side, owner in ((0, me), (1, far)):
            both = jnp.dot(normed, w_kv[side], preferred_element_type=jnp.float32)
            raw[owner, whole_span, :] = both.astype(raw.dtype)
        for turn in range(1, m):
            for side in (0, 1):
                passed(turn, side, chunk, me).start()
        cosine, sine = cos_ref[whole_span, :], sin_ref[whole_span, :]
        query = jnp.dot(normed, w_query[...], preferred_element_type=jnp.float32)
        for head in range(query.shape[1] // HD):
            there = slice(head * HD, (head + 1) * HD)
            turned = turn_pairs(query[:, there], cosine, sine) * HD ** (-0.5)
            query_ref[span, there] = turned.astype(query_ref.dtype)

    def spread(chunk):
        for turn in range(1, m):
            for side in (0, 1):
                passed(turn, side, chunk, lax.rem(me - turn + m, m)).wait_recv()
        part_width = raw.shape[2] // 2
        for portion in (0, 1):
            index = portion * chunks + chunk
            span = span_of(index, rows)
            pieces = [raw[owner, span, :].astype(jnp.float32) for owner in range(m)]
            key = jnp.concatenate([piece[:, :part_width] for piece in pieces], axis=-1)
            value = jnp.concatenate([piece[:, part_width:] for piece in pieces], axis=-1)
            kv[span, :HD] = turn_pairs(key, cos_ref[span, :], sin_ref[span, :]).astype(kv.dtype)
            kv[span, HD:] = value.astype(kv.dtype)
            kept(index).start()
            for distance in range(2, back + 1, 2):

                @pl.when(at + distance < n)
                def _(distance=distance, index=index):
                    ahead(distance, index).start()

            @pl.when(odd == 0)
            def _(index=index):
                ahead(1, index).start()

    each(chunks, lambda chunk: handed(chunk).start())
    lend = Lend(w_attn_ref, w_attn_far_ref, 1, n, m, chunks, l_send, l_recv)
    zeros[...] = jnp.zeros_like(zeros)
    for distance in range(1, back + 1):

        @pl.when(at < distance)
        def _(distance=distance):
            blank(distance).start()

    for fetch in fetches(0):
        fetch.wait()
    product(0)
    everywhere = 2 * (h - 1) + 1

    def tick(t):
        scatter.pass_on(t)
        done = t - scatter.late()

        @pl.when(within(done, chunks))
        def _():
            span = span_of(done, rows)
            scatter.arrive(done, base_ref[span, :], total)
            mine = total[...].astype(own_ref.dtype)
            own_ref[span, :] = mine
            full[span, pl.ds(pl.multiple_of(local * cols, cols), cols)] = mine
            gather.begin(done)

        gather.relay(t, late)

        @pl.when(t + 1 < chunks)
        def _():
            product(t + 1)

        joined = t - everywhere

        @pl.when(within(joined, chunks))
        def _():
            spread(joined)

        whole = t - latest(local)

        @pl.when(whole == 0)
        def _():
            for kind in (1, 2):
                for fetch in fetches(kind):
                    fetch.wait()

        @pl.when(within(whole, chunks))
        def _():
            project(whole)

        lend.step(t, LENT_LATE)

    loop(chunks + everywhere, tick)
    each(chunks, lambda chunk: handed(chunk).wait_send())
    for tick_more in range(chunks + everywhere, chunks + LENT_LATE[2]):
        lend.step(tick_more, LENT_LATE)
    lend.end()
    scatter.settle()
    gather.settle()
    for distance in range(1, back + 1):

        @pl.when(at < distance)
        def _(distance=distance):
            blank(distance).wait()

    def pass_over(chunk):
        for distance in range(2, back + 1, 2):

            @pl.when(at >= distance)
            def _(distance=distance):
                ahead(distance, chunk).wait_recv()

            @pl.when(relays(distance))
            def _(distance=distance):
                relayed(distance, chunk).start()

    each(2 * chunks, pass_over)

    def end(chunk):
        for distance in range(1, back + 1, 2):

            @pl.when(at >= distance)
            def _(distance=distance):
                ahead(distance, chunk).wait_recv()

        for distance in range(2, back + 1, 2):

            @pl.when(at + distance < n)
            def _(distance=distance):
                ahead(distance, chunk).wait_send()

            @pl.when(relays(distance))
            def _(distance=distance):
                relayed(distance, chunk).wait_send()

        @pl.when(odd == 0)
        def _():
            ahead(1, chunk).wait_send()

    each(2 * chunks, end)
    each(2 * chunks, lambda chunk: kept(chunk).wait())
    for turn in range(1, m):
        for side in (0, 1):
            each(
                chunks,
                lambda chunk, turn=turn, side=side: passed(turn, side, chunk, me).wait_send(),
            )


def middle(gated, base, w_out, w_query, w_kv, w_attn, cosine, sine, mark, chunks):
    n, m = lax.axis_size("ctx"), lax.axis_size("mp")
    h = m // 2
    count, channels = gated.shape
    few, cols = base.shape
    width = w_out[0].shape[1]
    queries = w_query[0].shape[1]
    part = w_kv[0].shape[1]
    wide = m * part
    rows = few // chunks
    back = WINDOW // count
    vmem = pl.BlockSpec(memory_space=pltpu.VMEM)
    hbm = pl.BlockSpec(memory_space=pl.ANY)
    low = jnp.bfloat16
    dma = pltpu.SemaphoreType.DMA
    return pl.pallas_call(
        functools.partial(middle_kernel, n, m, chunks),
        out_shape=(
            jax.ShapeDtypeStruct((few, cols), low),
            jax.ShapeDtypeStruct((few, 2 * queries), low),
            jax.ShapeDtypeStruct(((back + 1) * count, wide), low),
            jax.ShapeDtypeStruct(w_attn.shape, low),
        ),
        in_specs=[vmem, vmem] + [hbm] * 7 + [vmem, vmem],
        out_specs=(vmem, vmem, hbm, hbm),
        scratch_shapes=[
            pltpu.VMEM((2, channels, width), low),
            pltpu.VMEM((width, 2 * queries), low),
            pltpu.VMEM((2, width, part), low),
            pltpu.VMEM((few, channels), low),
            pltpu.VMEM((few, width), jnp.float32),
            pltpu.VMEM((rows, cols), jnp.float32),
            pltpu.VMEM((2, h - 1, few, cols), low),
            pltpu.VMEM((few, width), low),
            pltpu.VMEM((m, count, part), low),
            pltpu.VMEM((count, wide), low),
            pltpu.VMEM((count, wide), low),
            dma((3, 2 * m)),
            dma((chunks,)),
            dma((chunks,)),
            dma((2, h - 1, chunks)),
            dma((2, h - 1, chunks)),
            dma((2, h, chunks)),
            dma((2, h, chunks)),
            dma((m - 1, 2, chunks)),
            dma((m - 1, 2, chunks)),
            dma((back, 2 * chunks)),
            dma((back, 2 * chunks)),
            dma((2 * chunks,)),
            dma((back,)),
            dma((n, chunks)),
            dma((n, chunks)),
        ],
        compiler_params=pltpu.CompilerParams(
            collective_id=mark, has_side_effects=True, vmem_limit_bytes=VMEM_LIMIT
        ),
    )(gated, base, *w_out, *w_query, *w_kv, w_attn, cosine, sine)


def last_kernel(
    m, chunks,
    query_ref, window_ref, base_ref, w_out_ref, w_out_far_ref,
    result_ref,
    w_out, part, total, made, held, loads, s_send, s_recv, o_send, o_recv, o_local,
):
    at, me = lax.axis_index("ctx"), lax.axis_index("mp")
    h = m // 2
    half, local = me // h, lax.rem(me, h)
    far = lax.rem(me + h, m)
    few, cols = base_ref.shape
    count = 2 * few
    block = cols // 2
    channels = w_out_ref.shape[0]
    rows = few // chunks
    heads = query_ref.shape[1] // HD

    def fetches():
        for side in (0, 1):
            for index in range(m):
                put = place_of(index, h)
                yield pltpu.make_async_copy(
                    (w_out_ref, w_out_far_ref)[side].at[
                        :, index * block : (index + 1) * block
                    ],
                    w_out.at[
                        side * channels : (side + 1) * channels,
                        put * block : (put + 1) * block,
                    ],
                    loads.at[side * m + index],
                )

    for fetch in fetches():
        fetch.start()
    meet_line(m)
    line = Line(local, h, half * h)
    scatter = Scatter(line, part, held, s_send, s_recv, cols, rows, chunks)
    step = max(rows, 128)
    reach = WINDOW + step

    def sent(chunk):
        return pltpu.make_async_remote_copy(
            src_ref=made.at[
                span_of(chunk, rows), pl.ds(pl.multiple_of((1 - half) * block, block), block)
            ],
            dst_ref=result_ref.at[span_of(half * chunks + chunk, rows), :],
            send_sem=o_send.at[chunk],
            recv_sem=o_recv.at[chunk],
            device_id={"mp": far},
        )

    def came(chunk):
        place = result_ref.at[span_of((1 - half) * chunks + chunk, rows), :]
        return pltpu.make_async_remote_copy(
            src_ref=place,
            dst_ref=place,
            send_sem=o_send.at[chunk],
            recv_sem=o_recv.at[chunk],
            device_id={"mp": far},
        )

    def kept(chunk):
        return pltpu.make_async_copy(
            made.at[span_of(chunk, rows), pl.ds(pl.multiple_of(half * block, block), block)],
            result_ref.at[span_of(half * chunks + chunk, rows), :],
            o_local.at[chunk],
        )

    def attend(chunk):
        span = span_of(chunk, rows)
        place = half * few + chunk * rows
        first = pl.multiple_of(place // step * step, step)
        keys = window_ref[pl.ds(first, reach), :HD]
        values = window_ref[pl.ds(first, reach), HD:]
        tall = (heads * rows, reach)
        row = place + lax.rem(lax.broadcasted_iota(jnp.int32, tall, 0), rows)
        col = first + lax.broadcasted_iota(jnp.int32, tall, 1)
        distance = row + WINDOW - col
        valid = (distance >= 0) & (distance < WINDOW) & (col >= WINDOW - at * count)
        stacked = jnp.concatenate(
            [query_ref[span, head * HD : (head + 1) * HD] for head in range(heads)], axis=0
        )
        scores = lax.dot_general(
            stacked, keys, (((1,), (1,)), ((), ())), preferred_element_type=jnp.float32
        )
        masked = jnp.where(valid, scores, -1e30)
        top = jnp.max(masked, axis=-1, keepdims=True)
        weights = jnp.exp(masked - top)
        share = 1.0 / jnp.sum(weights, axis=-1, keepdims=True)
        probs = (weights * share).astype(jnp.bfloat16)
        mixed = jnp.dot(probs, values, preferred_element_type=jnp.float32).astype(jnp.bfloat16)
        attended = [mixed[head * rows : (head + 1) * rows, :] for head in range(heads)]
        taken = jnp.concatenate(attended, axis=-1)
        for index in range(m):
            there = slice(index * block, (index + 1) * block)
            part[span, there] = jnp.dot(
                taken, w_out[:, there], preferred_element_type=jnp.float32
            )

    for fetch in fetches():
        fetch.wait()
    attend(0)

    def tick(t):
        scatter.pass_on(t)
        done = t - scatter.late()

        @pl.when(within(done, chunks))
        def _():
            span = span_of(done, rows)
            scatter.arrive(done, base_ref[span, :], total)
            made[span, :] = total[...].astype(made.dtype)
            sent(done).start()
            kept(done).start()

        @pl.when(t + 1 < chunks)
        def _():
            attend(t + 1)

    loop(chunks + h - 1, tick)
    scatter.settle()

    def end(chunk):
        sent(chunk).wait_send()
        came(chunk).wait_recv()
        kept(chunk).wait()

    each(chunks, end)


def last(query, window, base, w_out, mark, chunks):
    m = lax.axis_size("mp")
    h = m // 2
    few, cols = base.shape
    channels, width = w_out[0].shape
    rows = few // chunks
    vmem = pl.BlockSpec(memory_space=pltpu.VMEM)
    hbm = pl.BlockSpec(memory_space=pl.ANY)
    low = jnp.bfloat16
    dma = pltpu.SemaphoreType.DMA
    return pl.pallas_call(
        functools.partial(last_kernel, m, chunks),
        out_shape=jax.ShapeDtypeStruct((2 * few, cols // 2), low),
        in_specs=[vmem, vmem, vmem, hbm, hbm],
        out_specs=hbm,
        scratch_shapes=[
            pltpu.VMEM((2 * channels, width), low),
            pltpu.VMEM((few, width), jnp.float32),
            pltpu.VMEM((rows, cols), jnp.float32),
            pltpu.VMEM((few, cols), low),
            pltpu.VMEM((2, h - 1, few, cols), low),
            dma((2 * m,)),
            dma((2, h - 1, chunks)),
            dma((2, h - 1, chunks)),
            dma((chunks,)),
            dma((chunks,)),
            dma((chunks,)),
        ],
        compiler_params=pltpu.CompilerParams(
            collective_id=mark, has_side_effects=True, vmem_limit_bytes=VMEM_LIMIT
        ),
    )(query, window, base, *w_out)


def turns(positions):
    turned = HD // 2
    half = turned // 2
    freqs = 10000.0 ** (-jnp.arange(half, dtype=jnp.float32) * 2.0 / turned)
    angles = positions.astype(jnp.float32)[:, None] * freqs[None, :]
    cosine, sine = jnp.cos(angles), jnp.sin(angles)
    return (
        jnp.concatenate([cosine, cosine], axis=-1),
        jnp.concatenate([-sine, sine], axis=-1),
    )


def on_device(
    tokens,
    w_branch,
    w_input,
    conv_kernel,
    w_rate,
    w_admit,
    lam,
    w_out,
    w_query,
    w_key,
    w_value,
    w_attn_out,
):
    batch, rows_dev, cols_dev = tokens.shape
    count = batch * rows_dev
    tokens_flat = tokens.reshape(count, cols_dev)
    w_kv = jnp.concatenate([w_key, w_value], axis=1)
    soft = jax.nn.softplus(-lam)[None, :]
    gated, share, w_out_far, w_query_far, w_kv_far = first(
        tokens_flat, w_branch, w_input, conv_kernel, w_rate, w_admit, soft,
        w_out, w_query, w_kv, 1, CHUNKS,
    )
    base = lax.axis_index("ctx") * rows_dev
    positions = base + jnp.arange(rows_dev, dtype=jnp.int32)
    cosine, sine = turns(positions)
    resid, query, window, w_attn_out_far = middle(
        gated, share, (w_out, w_out_far), (w_query, w_query_far), (w_kv, w_kv_far),
        w_attn_out, cosine, sine, 2, CHUNKS_MIDDLE,
    )
    result = last(query, window, resid, (w_attn_out, w_attn_out_far), 3, CHUNKS_LAST)
    return result.reshape(batch, rows_dev, cols_dev)


def solution(mesh):
    in_specs = (
        P(None, "ctx", "mp"),
        P(None, "mp"),
        P(None, "mp"),
        P(None, "mp"),
        P("mp", None, None),
        P("mp", None, None),
        P("mp"),
        P("mp", None),
        P(None, "mp"),
        P(None, "mp"),
        P(None, "mp"),
        P("mp", None),
    )
    out_specs = P(None, "ctx", "mp")
    return jax.shard_map(
        on_device, mesh=mesh, in_specs=in_specs, out_specs=out_specs, check_vma=False
    )
```
